32 devices in a mesh: group: 2 (over x), tp: 16 (over z, y, core).
Axes of the slice: x: 2, y: 2, z: 4, core: 2. Of those that a mesh axis runs over, the one named last changes fastest.
Arguments:
- hidden_states: bfloat16 [16, 2, 8192], P('group'), parts along dimension 0, may hold values from -6 to 6
- qkv_weight: bfloat16 [10240, 8192], P('tp'), may hold values from -0.0625 to 0.0625
- out_weight: bfloat16 [8192, 8192], P('tp'), may hold values from -0.0625 to 0.0625
- cache_pages: bfloat16 [2048, 128, 256], P(('group', 'tp')), parts along dimension 0, may hold values from -6 to 6
- context_lengths: int32 [16], P('group'), parts along dimension 0, may hold values from 1 to 2046, 8184 in all
- new_units: int32 [128], P('group'), parts along dimension 0, may hold values from 0 to 63, as said below
- old_pages: int32 [2048], P('group'), parts along dimension 0, may hold values from 0 to 1023, as said below
Outputs:
- mixed_out: bfloat16 [16, 2, 8192], P('group', None, 'tp'), parts along dimension 0
- cache_out: bfloat16 [2048, 128, 256], P(('group', 'tp')), parts along dimension 0
The draws below stay inside these ranges and needn't reach their ends.
There are 2 independent parts, one for each index of `group`. The reference program is written for one: setup_inputs(seed, part) draws one part's arguments, and reference() takes and returns one part's arrays. A program takes and returns all parts, laid end to end along the dimension named above; an argument that names none is the same for every part. Nothing has to cross between parts.
Inputs may be any that keep to these rules, and one draw needn't show every extreme that they name: `new_units`: A permutation of all request head groups; slot q of the new layout is on device q // 4. `old_pages`: A permutation of all logical pages (page u * 16 + i is page i of unit u); position p is on device p // 64. The pages that one device holds go to exactly 16 devices of the new layout, exactly 4 to each.
All inputs are finite; a program needn't handle non-finite values.
Results may differ from the reference program's by a relative error of at most 0.013.
Values may be sent and summed in bfloat16 or wider, within the bound.
A program may use at most 128 MiB of HBM per device.

```python
import math
import jax
import jax.numpy as jnp
import numpy as np
from jax import lax

D = 8192
HEADS = 64
KVH = 8
HD = 128
GROUP = 8
U_DEV = 4
MAXCTX = 2048
PAGE = 128
PAGES_DEV = 64
CAP = 4
REQ = 8
PAGES = 1024
N_TP = 16


def layout_tables(key):
    unit_total = U_DEV * N_TP
    page_total = PAGES_DEV * N_TP
    per_unit = MAXCTX // PAGE
    capacity = CAP
    new_units = jax.random.permutation(jax.random.fold_in(key, 101), unit_total).astype(jnp.int32)
    offsets = jax.random.permutation(jax.random.fold_in(key, 102), N_TP).astype(jnp.int32)[:PAGES_DEV // capacity]
    first_perm = jax.random.permutation(jax.random.fold_in(key, 103), N_TP).astype(jnp.int32)
    second_perm = jax.random.permutation(jax.random.fold_in(key, 104), N_TP).astype(jnp.int32)
    within = jax.vmap(lambda sub: jax.random.permutation(sub, PAGES_DEV))(jax.random.split(jax.random.fold_in(key, 105), N_TP)).astype(jnp.int32)
    shuffle = jax.vmap(lambda sub: jax.random.permutation(sub, PAGES_DEV))(jax.random.split(jax.random.fold_in(key, 106), N_TP)).astype(jnp.int32)
    new_position = jnp.arange(page_total, dtype=jnp.int32)
    new_device = new_position // PAGES_DEV
    new_slot = new_position % PAGES_DEV
    page_id = new_units[new_position // per_unit] * per_unit + new_position % per_unit
    drawn_rank = within[new_device, new_slot]
    group_index = drawn_rank // capacity
    member = drawn_rank % capacity
    old_device = second_perm[(first_perm[new_device] + offsets[group_index]) % N_TP]
    old_slot = shuffle[old_device, group_index * capacity + member]
    old_position = old_device * PAGES_DEV + old_slot
    old_pages = jnp.zeros((page_total,), jnp.int32).at[old_position].set(page_id)
    return (new_units, old_pages)


def draw_new_units(key, part):
    return layout_tables(key)[0]


def draw_old_pages(key, part):
    return layout_tables(key)[1]


def block_levels(rng, extent, pieces, smallest, high):
    gain = 1.0
    for axis_at, blocks in pieces:
        heights = jax.random.uniform(jax.random.fold_in(jax.random.fold_in(rng, 6), axis_at), (blocks,), jnp.float32, smallest / len(pieces), high / len(pieces))
        gain = gain * jnp.repeat(jnp.exp(heights), extent[axis_at] // blocks).reshape((-1,) + (1,) * (len(extent) - 1 - axis_at))
    return gain


def split_up(number_of, total, most, lean):
    weights = [(1 << 20) // math.isqrt(rank ** lean) + 1 for rank in range(2, number_of + 1)]
    spare, given = total - most - (number_of - 1), [1] * (number_of - 1)
    while spare > 0:
        candidates = [i for i in range(number_of - 1) if given[i] < most]
        pool, left = sum([weights[i] for i in candidates]), spare
        for i in candidates:
            more = min(most - given[i], max(1, left * weights[i] // pool), spare)
            given[i] = given[i] + more
            spare = spare - more
    return np.array([most] + given)


def ragged(stream_key, count, total, most, lean):
    if count == 2:
        one = jax.random.randint(stream_key, (), max(1, total - most), min(most, total - 1) + 1)
        return jnp.stack([one, total - one])
    sizes = jnp.asarray(split_up(count, total, most, lean), jnp.int32)
    couples = (count - 1) // 2
    giver, sink = sizes[1:1 + 2 * couples:2], sizes[2:2 + 2 * couples:2]
    slack = jnp.minimum(giver - 1, most - sink)
    shifted = jax.random.randint(jax.random.fold_in(stream_key, 1), (couples,), 0, 1 << 20) % (slack + 1)
    sizes = sizes.at[1:1 + 2 * couples:2].set(giver - shifted).at[2:2 + 2 * couples:2].set(sink + shifted)
    return sizes[jax.random.permutation(jax.random.fold_in(stream_key, 2), count)]


def normal_values(own_key, extent, width, limit, cuts=(), kind=jnp.bfloat16):
    array = width * jax.random.normal(own_key, extent, jnp.float32)
    if cuts:
        array = array * block_levels(own_key, extent, cuts, -0.22, 0.18)
    return jnp.clip(array, -limit, limit).astype(kind)


def setup_inputs(seed: int = 0, part: int = 0) -> dict:
    splits = jax.random.split(jax.random.key(seed), 8)
    part_splits = jax.random.split(jax.random.fold_in(splits[7], part), 8)
    hidden_states = normal_values(part_splits[0], (REQ, 2, D), 1.0, 6.0)
    qkv_weight = normal_values(splits[1], (KVH * (GROUP + 2) * HD, D), D ** -0.5, 0.0625, ((0, 16),))
    out_weight = normal_values(splits[2], (D, HEADS * HD), (HEADS * HD) ** -0.5, 0.0625, ((0, 16),))
    cache_pages = normal_values(part_splits[3], (PAGES, PAGE, 2 * HD), 1.0, 6.0, ((0, 16),))
    context_lengths = ragged(part_splits[4], REQ, REQ * (MAXCTX - 2) // 2, MAXCTX - 2, 2).astype(jnp.int32)
    new_units = draw_new_units(jax.random.fold_in(jax.random.fold_in(splits[7], part), 71), part)
    old_pages = draw_old_pages(jax.random.fold_in(jax.random.fold_in(splits[7], part), 71), part)
    return {"hidden_states": hidden_states, "qkv_weight": qkv_weight, "out_weight": out_weight, "cache_pages": cache_pages, "context_lengths": context_lengths, "new_units": new_units, "old_pages": old_pages}


rope_base = 10000.0

def rotate_positions(values, positions):
    half_dim = values.shape[-1] // 2
    frequency = rope_base ** (-(jnp.arange(half_dim, dtype=jnp.float32) * 2.0 / values.shape[-1]))
    angles = positions.astype(jnp.float32)[..., None] * frequency
    cosine = jnp.concatenate([jnp.cos(angles), jnp.cos(angles)], axis=-1)
    sine_table = jnp.concatenate([jnp.sin(angles), jnp.sin(angles)], axis=-1)
    turned = jnp.concatenate([-values[..., half_dim:], values[..., :half_dim]], axis=-1)
    return values * cosine + turned * sine_table

def prepare(unit_qkv, base_lengths):
    group_count = HEADS // KVH
    count_units = unit_qkv.shape[0]
    positions = base_lengths[:, None] + jnp.arange(2, dtype=jnp.int32)[None, :]
    widened = unit_qkv.astype(jnp.float32)
    queries = widened[..., :group_count * HD].reshape(count_units, 2, group_count, HD)
    queries = rotate_positions(queries, positions[:, :, None]).astype(jnp.bfloat16)
    new_keys = rotate_positions(widened[..., group_count * HD:(group_count + 1) * HD], positions).astype(jnp.bfloat16)
    new_values = unit_qkv[..., (group_count + 1) * HD:]
    return (queries, new_keys, new_values)

def reference(hidden_states, qkv_weight, out_weight, cache_pages, context_lengths, new_units, old_pages):
    group_count = HEADS // KVH
    unit_rows = (group_count + 2) * HD
    requests = hidden_states.shape[0]
    total_units = requests * KVH
    per_unit = MAXCTX // PAGE
    page_width = cache_pages.shape[2]
    total_pages = old_pages.shape[0]
    score_scale = 1.0 / math.sqrt(HD)
    flat_rows = hidden_states.reshape(requests * 2, D)
    projected = jnp.dot(flat_rows, qkv_weight.T, preferred_element_type=jnp.float32).astype(jnp.bfloat16)
    unit_qkv = projected.reshape(requests, 2, KVH, unit_rows).transpose(0, 2, 1, 3).reshape(total_units, 2, unit_rows)
    unit_lengths = jnp.repeat(context_lengths, KVH)
    queries, new_keys, new_values = prepare(unit_qkv, unit_lengths)
    stored_position = jnp.zeros((total_pages,), jnp.int32).at[old_pages].set(jnp.arange(total_pages, dtype=jnp.int32))
    contexts = cache_pages[stored_position].reshape(total_units, MAXCTX, page_width)

    def one_unit(packed):
        context, unit_query, keys_new, values_new, valid_count = packed
        cached_keys = jnp.concatenate([context[:, :HD], keys_new], axis=0).astype(jnp.float32)
        cached_values = jnp.concatenate([context[:, HD:], values_new], axis=0).astype(jnp.float32)
        scores = jnp.einsum('sgd,td->sgt', unit_query.astype(jnp.float32), cached_keys) * score_scale
        cached = jnp.arange(MAXCTX, dtype=jnp.int32) < valid_count
        recent = jnp.arange(2, dtype=jnp.int32)[None, :] <= jnp.arange(2, dtype=jnp.int32)[:, None]
        visible = jnp.concatenate([jnp.broadcast_to(cached[None, :], (2, MAXCTX)), recent], axis=1)
        weights = jnp.where(visible[:, None, :], jnp.exp(scores), 0.0)
        totals = lax.optimization_barrier(jnp.sum(weights, axis=-1))
        rounded = lax.optimization_barrier(weights.astype(jnp.bfloat16)).astype(jnp.float32)
        weighted = jnp.einsum('sgt,td->sgd', rounded, cached_values)
        return (weighted / totals[..., None]).astype(jnp.bfloat16)
    attended = lax.map(one_unit, (contexts, queries, new_keys, new_values, unit_lengths))
    heads_out = attended.reshape(requests, KVH, 2, group_count * HD).transpose(0, 2, 1, 3).reshape(requests * 2, HEADS * HD)
    mixed_rows = jnp.dot(heads_out, out_weight.T, preferred_element_type=jnp.float32).astype(jnp.bfloat16).reshape(requests, 2, D)
    slot_contexts = contexts[new_units]
    slot_lengths = unit_lengths[new_units]
    fresh_rows = jnp.concatenate([new_keys, new_values], axis=-1)[new_units]
    positions = jnp.arange(MAXCTX, dtype=jnp.int32)[None, :]
    slot_contexts = jnp.where((positions == slot_lengths[:, None])[..., None], fresh_rows[:, 0:1], slot_contexts)
    slot_contexts = jnp.where((positions == slot_lengths[:, None] + 1)[..., None], fresh_rows[:, 1:2], slot_contexts)
    new_cache = slot_contexts.reshape(total_units * per_unit, PAGE, page_width)
    return (mixed_rows, new_cache)
```

```python
import math

import jax
import jax.numpy as jnp
from jax import lax
from jax.experimental import pallas as pl
from jax.experimental.pallas import tpu as pltpu
from jax.sharding import PartitionSpec as P

D = 8192
HEADS = 64
KVH = 8
HD = 128
U_DEV = 4
MAXCTX = 2048
PAGE = 128


rope_base = 10000.0


def rotate_positions(values, positions):
    half_dim = values.shape[-1] // 2
    frequency = rope_base ** (-(jnp.arange(half_dim, dtype=jnp.float32) * 2.0 / values.shape[-1]))
    angles = positions.astype(jnp.float32)[..., None] * frequency
    cosine = jnp.concatenate([jnp.cos(angles), jnp.cos(angles)], axis=-1)
    sine_table = jnp.concatenate([jnp.sin(angles), jnp.sin(angles)], axis=-1)
    turned = jnp.concatenate([-values[..., half_dim:], values[..., :half_dim]], axis=-1)
    return values * cosine + turned * sine_table


def prepare(unit_qkv, base_lengths):
    group_count = HEADS // KVH
    count_units = unit_qkv.shape[0]
    positions = base_lengths[:, None] + jnp.arange(2, dtype=jnp.int32)[None, :]
    widened = unit_qkv.astype(jnp.float32)
    queries = widened[..., : group_count * HD].reshape(count_units, 2, group_count, HD)
    queries = rotate_positions(queries, positions[:, :, None]).astype(jnp.bfloat16)
    new_keys = rotate_positions(
        widened[..., group_count * HD : (group_count + 1) * HD], positions
    ).astype(jnp.bfloat16)
    new_values = unit_qkv[..., (group_count + 1) * HD :]
    return (queries, new_keys, new_values)


def context_terms(context, queries, valid_count):
    score_scale = 1.0 / math.sqrt(HD)
    cached_keys = context[..., :HD]
    cached_values = context[..., HD:]
    scores = (
        jnp.einsum("psgd,ptd->psgt", queries, cached_keys, preferred_element_type=jnp.float32)
        * score_scale
    )
    visible = jnp.arange(context.shape[1], dtype=jnp.int32)[None, :] < valid_count[:, None]
    weights = jnp.where(visible[:, None, None, :], jnp.exp(scores), 0.0)
    totals = jnp.sum(weights, axis=-1)
    weighted = jnp.einsum(
        "psgt,ptd->psgd",
        weights.astype(jnp.bfloat16),
        cached_values,
        preferred_element_type=jnp.float32,
    )
    return (weighted, totals)


def own_terms(queries, new_keys, new_values):
    score_scale = 1.0 / math.sqrt(HD)
    scores = (
        jnp.einsum("usgd,ujd->usgj", queries, new_keys, preferred_element_type=jnp.float32)
        * score_scale
    )
    recent = jnp.arange(2, dtype=jnp.int32)[None, :] <= jnp.arange(2, dtype=jnp.int32)[:, None]
    weights = jnp.where(recent[None, :, None, :], jnp.exp(scores), 0.0)
    totals = jnp.sum(weights, axis=-1)
    weighted = jnp.einsum(
        "usgj,ujd->usgd",
        weights.astype(jnp.bfloat16),
        new_values,
        preferred_element_type=jnp.float32,
    )
    return (weighted, totals)


def plain_body(hidden_states, qkv_weight, out_weight, cache_pages, context_lengths, new_units, old_pages):
    devices = lax.axis_size("tp")
    device = lax.axis_index("tp")
    requests = hidden_states.shape[0]
    rows_dev = qkv_weight.shape[0]
    pages_dev, page_rows, page_width = cache_pages.shape
    group_count = HEADS // KVH
    unit_rows = (group_count + 2) * HD
    per_unit = MAXCTX // PAGE
    unit_slots = U_DEV
    capacity = max(1, pages_dev // devices)
    total_units = new_units.shape[0]
    total_pages = old_pages.shape[0]
    flat_rows = hidden_states.reshape(requests * 2, D)
    partial_qkv = lax.dot_general(
        flat_rows, qkv_weight, (((1,), (1,)), ((), ())), preferred_element_type=jnp.float32
    )
    partial_qkv = partial_qkv.astype(jnp.bfloat16).reshape(requests, 2, rows_dev)
    slot_index = (
        jnp.zeros((total_units,), jnp.int32)
        .at[new_units]
        .set(jnp.arange(total_units, dtype=jnp.int32))
    )
    own_units = lax.dynamic_slice_in_dim(new_units, device * unit_slots, unit_slots)
    own_requests = own_units // KVH
    own_heads = own_units % KVH
    own_lengths = context_lengths[own_requests]
    local_ids = lax.dynamic_slice_in_dim(old_pages, device * pages_dev, pages_dev)
    local_units = local_ids // per_unit
    local_index = local_ids % per_unit
    target_dev = (slot_index[local_units] * per_unit + local_index) // pages_dev
    local_order = jnp.arange(pages_dev, dtype=jnp.int32)
    send_rank = jnp.sum(
        (
            (target_dev[:, None] == target_dev[None, :])
            & (local_order[None, :] < local_order[:, None])
        ).astype(jnp.int32),
        axis=1,
    )
    outgoing = (
        jnp.zeros((devices, capacity, page_rows, page_width), jnp.bfloat16)
        .at[target_dev, send_rank]
        .set(cache_pages)
    )
    arrived = lax.all_to_all(outgoing, "tp", split_axis=0, concat_axis=0, tiled=True)
    stored_position = (
        jnp.zeros((total_pages,), jnp.int32)
        .at[old_pages]
        .set(jnp.arange(total_pages, dtype=jnp.int32))
    )
    wanted = (
        own_units[:, None] * per_unit + jnp.arange(per_unit, dtype=jnp.int32)[None, :]
    ).reshape(pages_dev)
    source_pos = stored_position[wanted]
    source_dev = source_pos // pages_dev
    source_slot = source_pos % pages_dev
    arrival_rank = jnp.sum(
        (
            (source_dev[:, None] == source_dev[None, :])
            & (source_slot[None, :] < source_slot[:, None])
        ).astype(jnp.int32),
        axis=1,
    )
    relaid = arrived[source_dev, arrival_rank]
    contexts = relaid.reshape(unit_slots, MAXCTX, page_width)
    sources_per_head = unit_rows // rows_dev
    request_table = (new_units // KVH).reshape(devices, unit_slots)
    outgoing_rows = partial_qkv[request_table]
    incoming = lax.all_to_all(outgoing_rows, "tp", split_axis=0, concat_axis=0, tiled=True)
    grouped = jnp.moveaxis(incoming.reshape(KVH, sources_per_head, unit_slots, 2, rows_dev), 2, 0)
    chosen = jnp.take_along_axis(grouped, own_heads[:, None, None, None, None], axis=1)[:, 0]
    own_rows = chosen.transpose(0, 2, 1, 3).reshape(unit_slots, 2, unit_rows)
    queries, new_keys, new_values = prepare(own_rows, own_lengths)
    cache_sums, cache_totals = context_terms(contexts, queries, own_lengths)
    own_sums, own_totals = own_terms(queries, new_keys, new_values)
    attended = ((cache_sums + own_sums) / (cache_totals + own_totals)[..., None]).astype(
        jnp.bfloat16
    )
    attended = attended.reshape(unit_slots, 2, group_count * HD)
    all_heads = lax.all_gather(attended, "tp", axis=0, tiled=True)
    logical = (
        all_heads[slot_index]
        .reshape(requests, KVH, 2, group_count * HD)
        .transpose(0, 2, 1, 3)
        .reshape(requests * 2, HEADS * HD)
    )
    mixed_rows = lax.dot_general(
        logical, out_weight, (((1,), (1,)), ((), ())), preferred_element_type=jnp.float32
    )
    mixed_rows = mixed_rows.astype(jnp.bfloat16).reshape(requests, 2, out_weight.shape[0])
    fresh_rows = jnp.concatenate([new_keys, new_values], axis=-1)
    positions = jnp.arange(MAXCTX, dtype=jnp.int32)[None, :]
    contexts = jnp.where(
        (positions == own_lengths[:, None])[..., None], fresh_rows[:, 0:1], contexts
    )
    contexts = jnp.where(
        (positions == own_lengths[:, None] + 1)[..., None], fresh_rows[:, 1:2], contexts
    )
    return (mixed_rows, contexts.reshape(pages_dev, page_rows, page_width))


def place_kernel(
    table_ref, arrived_ref, fresh_ref, mixed_ref, out_ref, rows_ref, patched, rows, sem, rows_sem
):
    count = out_ref.shape[0]
    per_unit = MAXCTX // PAGE
    steps = fresh_ref.shape[1]

    def outward(i, src):
        return pltpu.make_async_copy(src, out_ref.at[i], sem.at[i])

    def written(slot, step):
        return (table_ref[1, slot] + step) // PAGE

    @pl.loop(0, count)
    def _(i):
        slot, page = i // per_unit, i % per_unit

        @pl.when((written(slot, 0) != page) & (written(slot, 1) != page))
        def _():
            outward(i, arrived_ref.at[table_ref[0, i]]).start()

    for slot in range(U_DEV):
        for step in range(steps):
            page = written(slot, step)
            at = slot * per_unit + page
            block = patched.at[slot, step]
            block[...] = arrived_ref[table_ref[0, at]]
            for other in range(steps):
                row = table_ref[1, slot] + other - page * PAGE

                @pl.when((row >= 0) & (row < PAGE))
                def _():
                    base = pl.multiple_of((row // 16) * 16, 16)
                    tile = block[pl.ds(base, 16), :]
                    line = lax.broadcasted_iota(jnp.int32, tile.shape, 0)
                    new = jnp.broadcast_to(fresh_ref[slot, other : other + 1, :], tile.shape)
                    mixed = jnp.where(line == row - base, new, tile.astype(jnp.float32))
                    block[pl.ds(base, 16), :] = mixed.astype(jnp.bfloat16)

            if step == 0:
                outward(at, block).start()
            else:

                @pl.when(page != written(slot, 0))
                def _():
                    outward(at, block).start()

    mixed = mixed_ref[...].astype(jnp.float32)
    for r in range(rows.shape[0]):
        rows[r] = mixed[2 * r : 2 * r + 2].astype(jnp.bfloat16)
    rows_out = pltpu.make_async_copy(rows, rows_ref, rows_sem)
    rows_out.start()

    @pl.loop(0, count)
    def _(i):
        outward(i, arrived_ref.at[0]).wait()

    rows_out.wait()


NT = (((1,), (1,)), ((), ()))


def layer_kernel(
    devices, capacity,
    lengths_hbm, units_hbm, ids_hbm, hidden_hbm, qkv_hbm, out_hbm, pages_hbm,
    arrived_hbm, mixed_ref, fresh_ref, place_ref,
    lengths, units_s, units_v, ids, tables_v, table, hidden_in, hidden_wide, hidden_ref, cos_ref, sin_ref,
    qkv_w, out_w, unsorted, pages, rows_all, spread, queries, new_keys, new_values, part_out, part_in, swap_out, swap_in, att_all, flat,
    load_sem, page_send, page_recv, row_send, row_recv, part_send, part_recv, att_send, att_recv,
    self_sem, small_sem, table_sem,
):
    me = lax.axis_index("tp")
    pages_dev = pages.shape[0]
    rows = hidden_ref.shape[0]
    requests = rows // 2
    units = requests * KVH
    per_unit = MAXCTX // PAGE
    heads = qkv_w.shape[0]
    tiles = out_w.shape[0]
    group_count = HEADS // KVH
    head_rows = group_count + 2
    score_scale = 1.0 / math.sqrt(HD)
    span = requests * 2 * group_count
    in_order, of_query, of_left, of_target, of_slot = range(5)

    half = devices // 2
    here, side = lax.rem(me, half), me // half
    partner = lax.rem(me + half, devices)

    def near(offset):
        return side * half + lax.rem(here + offset, half)

    def near_sender(offset):
        return side * half + lax.rem(here + half - offset, half)

    def far(offset):
        return (1 - side) * half + lax.rem(here + offset, half)

    def far_sender(offset):
        return (1 - side) * half + lax.rem(here + half - offset, half)

    def remote(src, dst, send, recv, device):
        return pltpu.make_async_remote_copy(
            src_ref=src, dst_ref=dst, send_sem=send, recv_sem=recv,
            device_id={"tp": device}, device_id_type=pl.DeviceIdType.MESH,
        )

    def page_copy(rank, place, device):
        return remote(
            pages.at[device * capacity + rank], arrived_hbm.at[me * capacity + rank],
            page_send.at[rank, place], page_recv.at[rank, place], device,
        )

    def page_arrival(rank, place, device):
        at = device * capacity + rank
        return remote(
            pages.at[at], arrived_hbm.at[at],
            page_send.at[rank, place], page_recv.at[rank, place], device,
        )

    def row_copy(stage, place, owner, device):
        block = rows_all.at[owner]
        return remote(block, block, row_send.at[stage, place], row_recv.at[stage, place], device)

    def att_copy(stage, place, owner, device):
        block = att_all.at[pl.ds(owner * U_DEV, U_DEV)]
        return remote(block, block, att_send.at[stage, place], att_recv.at[stage, place], device)

    def part_copy(place, src, dst, device):
        return remote(
            part_out.at[src], part_in.at[dst], part_send.at[place], part_recv.at[place], device
        )

    def swap_copy():
        return remote(swap_out, swap_in, part_send.at[0], part_recv.at[0], partner)

    batches = 2 * capacity

    def send_pages(batch):
        if batch >= batches:
            return
        rank, low, high = batch // 2, (batch % 2) * (half // 2), (batch % 2 + 1) * (half // 2)
        if batch % 2:
            high = half

        if low == 0:
            page_copy(rank, 0, partner).start()

        @pl.loop(max(low, 1), high)
        def _(offset):
            page_copy(rank, offset, far(offset)).start()
            page_copy(rank, half + offset, near(offset)).start()

    def pack_totals(values):
        packed = jnp.zeros((2 * group_count, PAGE), jnp.float32)
        for j, total in enumerate(values):
            top = total.astype(jnp.bfloat16).astype(jnp.float32)
            packed = jnp.where(lane == j * strip, top, packed)
            packed = jnp.where(lane == j * strip + strip // 2, total - top, packed)
        return packed.astype(jnp.bfloat16)

    def unpack_total(packed, j):
        return jnp.sum(jnp.where(lane // strip == j, packed, 0.0), axis=-1, keepdims=True)

    lane = lax.broadcasted_iota(jnp.int32, (2 * group_count, PAGE), 1)
    strip = PAGE // U_DEV

    barrier = pltpu.get_barrier_semaphore()

    @pl.loop(1, devices)
    def _(offset):
        pl.semaphore_signal(
            barrier, inc=1, device_id={"tp": lax.rem(me + offset, devices)}, device_id_type=pl.DeviceIdType.MESH
        )

    small = [
        pltpu.make_async_copy(ids_hbm, ids, small_sem.at[0]),
        pltpu.make_async_copy(units_hbm, units_v, small_sem.at[1]),
        pltpu.make_async_copy(units_hbm, units_s, small_sem.at[2]),
        pltpu.make_async_copy(lengths_hbm, lengths, small_sem.at[3]),
    ]
    load_pages = pltpu.make_async_copy(pages_hbm, unsorted, small_sem.at[4])
    load_hidden = pltpu.make_async_copy(hidden_hbm, hidden_in, small_sem.at[5])
    loads = [
        pltpu.make_async_copy(qkv_hbm.at[pl.ds(c * HD, HD)], qkv_w.at[c], load_sem.at[c])
        for c in range(heads)
    ]
    loads += [
        pltpu.make_async_copy(
            out_hbm.at[pl.ds(c * HD, HD)], out_w.at[c], load_sem.at[heads + c]
        )
        for c in range(tiles)
    ]
    for load in small + [load_pages, load_hidden] + loads[:heads]:
        load.start()

    def numbers(shape, axis):
        return lax.broadcasted_iota(jnp.int32, shape, axis)

    def whole(values, size):
        return lax.shift_right_logical(values, jnp.full_like(values, size.bit_length() - 1))

    def index_row(values, size):
        return jnp.clip(values, 0, size - 1)

    def down(hit, values):
        return jnp.sum(jnp.where(hit, values, 0), axis=0, keepdims=True)

    def across(hit, values):
        return jnp.sum(jnp.where(hit, values, 0), axis=1, keepdims=True)

    square = (pages_dev, pages_dev)
    k_sub, k_lane = numbers(square, 0), numbers(square, 1)
    small[0].wait()
    first = me * pages_dev
    wide = (pages_dev, ids.shape[1])
    own_ids = ids[pl.ds(first // ids.shape[1], 1), :]
    mine = numbers(wide, 1) == numbers(wide, 0) + lax.rem(first, ids.shape[1])
    id_col = across(mine, own_ids)
    small[1].wait()
    unit_row = units_v[...]
    by_unit = (pages_dev, units)
    slot_col = across(whole(id_col, per_unit) == unit_row, numbers(by_unit, 1))
    target_col = whole(slot_col, U_DEV)
    target_row = down(k_sub == k_lane, target_col)
    rank_col = across((target_col == target_row) & (k_lane < k_sub), jnp.ones(square, jnp.int32))
    sent = target_col * capacity + rank_col == k_lane
    tables_v[in_order : in_order + 1, :] = index_row(down(sent, k_sub), pages_dev)
    id_row = down(sent, id_col)
    tables_v[of_target : of_target + 1, :] = down(sent, slot_col - target_col * U_DEV)
    sent_unit = whole(id_row, per_unit)
    sent_request = whole(sent_unit, KVH)
    small[3].wait()
    sent_length = jnp.zeros_like(id_row)
    for r in range(requests):
        sent_length = jnp.where(sent_request == r, lengths[0, r], sent_length)
    tables_v[of_query : of_query + 1, :] = index_row(
        (sent_unit - sent_request * KVH) * requests + sent_request, units
    )
    tables_v[of_left : of_left + 1, :] = sent_length - (id_row - sent_unit * per_unit) * PAGE
    u_square = (units, units)
    u_sub, u_lane = numbers(u_square, 0), numbers(u_square, 1)
    unit_col = across(u_sub == u_lane, unit_row)
    tables_v[of_slot : of_slot + 1, :] = index_row(down(unit_col == u_lane, u_sub), units)
    to_table = pltpu.make_async_copy(tables_v, table, table_sem.at[0])
    to_table.start()

    load_pages.wait()
    to_table.wait()

    @pl.loop(0, pages_dev)
    def _(i):
        pages[i] = unsorted[table[in_order, i]]

    pl.semaphore_wait(barrier, devices - 1)
    send_pages(0)

    small[2].wait()
    row_at = lax.broadcasted_iota(jnp.int32, (rows, HD), 0)
    lane_at = lax.broadcasted_iota(jnp.int32, (rows, HD), 1)
    positions = jnp.zeros((rows, HD), jnp.float32)
    for r in range(requests):
        positions = jnp.where(row_at // 2 == r, lengths[0, r].astype(jnp.float32), positions)
    positions = positions + (row_at % 2).astype(jnp.float32)
    power = (lane_at % (HD // 2)).astype(jnp.float32) * (2.0 / HD)
    angles = positions * jnp.exp(power * -math.log(rope_base))
    cos_ref[...] = jnp.cos(angles)
    sin_ref[...] = jnp.where(lane_at < HD // 2, -jnp.sin(angles), jnp.sin(angles))
    load_hidden.wait()
    for r in range(requests):
        hidden_wide[2 * r : 2 * r + 2, :] = hidden_in[r].astype(jnp.float32)
    hidden_ref[...] = hidden_wide[...].astype(jnp.bfloat16)

    for c in range(heads):
        loads[c].wait()
        part = lax.dot_general(
            hidden_ref[...], qkv_w[c], NT, preferred_element_type=jnp.float32
        ).astype(jnp.bfloat16).astype(jnp.float32)
        turned = part * cos_ref[...] + pltpu.roll(part, HD // 2, 1) * sin_ref[...]
        is_value = lax.rem(me * heads + c, head_rows) == head_rows - 1
        rows_all[me, c] = jnp.where(is_value, part, turned).astype(jnp.bfloat16)

    row_copy(0, 0, me, partner).start()

    @pl.loop(1, half)
    def _(offset):
        row_copy(0, offset, me, near(offset)).start()

    send_pages(1)
    for load in loads[heads:]:
        load.start()
    own_pages = pltpu.make_async_copy(
        pages.at[pl.ds(me * capacity, capacity)],
        arrived_hbm.at[pl.ds(me * capacity, capacity)],
        self_sem,
    )
    own_pages.start()

    row_copy(0, 0, partner, partner).wait_recv()

    @pl.loop(1, half)
    def _(offset):
        row_copy(1, offset, partner, near(offset)).start()

    send_pages(2)

    @pl.loop(1, half)
    def _(offset):
        source = near_sender(offset)
        row_copy(0, offset, source, source).wait_recv()
        row_copy(1, offset, lax.rem(source + half, devices), source).wait_recv()

    for h in range(KVH):
        for g in range(group_count):
            at = h * head_rows + g
            spread[pl.ds(h * span + g, rows, stride=group_count), :] = rows_all[
                at // heads, at % heads
            ].astype(jnp.float32)
        at = h * head_rows + group_count
        new_keys[h] = rows_all[at // heads, at % heads]
        new_values[h] = rows_all[(at + 1) // heads, (at + 1) % heads]
        for r in range(requests):
            start = h * span + r * 2 * group_count
            queries[h * requests + r] = spread[start : start + 2 * group_count, :].astype(
                jnp.bfloat16
            )

    @pl.loop(0, devices)
    def _(target):
        zero = jnp.zeros((2 * group_count, PAGE), jnp.float32)
        sums, totals = [zero] * U_DEV, [zero[:, :1]] * U_DEV
        for rank in range(capacity):
            query = queries[table[of_query, target * capacity + rank]]
            left = table[of_left, target * capacity + rank]
            page = pages[target * capacity + rank]
            scores = lax.dot_general(
                query, page[:, :HD], NT, preferred_element_type=jnp.float32
            ) * score_scale
            weights = jnp.where(lane < left, jnp.exp(scores), 0.0)
            total = jnp.sum(weights, axis=-1, keepdims=True)
            weighted = jnp.dot(
                weights.astype(jnp.bfloat16), page[:, HD:], preferred_element_type=jnp.float32
            )
            slot = table[of_target, target * capacity + rank]
            for j in range(U_DEV):
                sums[j] = sums[j] + jnp.where(slot == j, weighted, 0.0)
                totals[j] = totals[j] + jnp.where(slot == j, total, 0.0)
        place, which = lax.rem(target, half), target // half
        for j in range(U_DEV):
            part_out[place, which, j] = sums[j].astype(jnp.bfloat16)
        part_out[place, which, U_DEV] = pack_totals(totals)

    @pl.loop(1, half)
    def _(offset):
        part_copy(offset, lax.rem(here + offset, half), here, near(offset)).start()

    send_pages(3)

    own_sums, own_totals = [], []
    row = lax.broadcasted_iota(jnp.int32, (2 * group_count, rows), 0)
    col = lax.broadcasted_iota(jnp.int32, (2 * group_count, rows), 1)
    line = lax.broadcasted_iota(jnp.int32, (rows, HD), 0)
    for j in range(U_DEV):
        unit = units_s[0, me * U_DEV + j]
        request, head = unit // KVH, unit % KVH
        keys = new_keys[head]
        values = new_values[head]
        scores = lax.dot_general(
            queries[head * requests + request], keys, NT, preferred_element_type=jnp.float32
        ) * score_scale
        seen = (col // 2 == request) & (col % 2 <= row // group_count)
        weights = jnp.where(seen, jnp.exp(scores), 0.0)
        own_totals.append(jnp.sum(weights, axis=-1, keepdims=True))
        own_sums.append(
            jnp.dot(weights.astype(jnp.bfloat16), values, preferred_element_type=jnp.float32)
        )
        for step in range(2):
            mine = line == request * 2 + step
            for part, kind in ((0, keys), (1, values)):
                fresh_ref[j, step : step + 1, part * HD : (part + 1) * HD] = jnp.sum(
                    jnp.where(mine, kind.astype(jnp.float32), 0.0), axis=0, keepdims=True
                )

    slot_at = numbers((pages_dev, 1), 0)
    wanted = jnp.zeros((pages_dev, 1), jnp.int32)
    for j in range(U_DEV):
        first_page = units_s[0, me * U_DEV + j] * per_unit - j * per_unit
        wanted = jnp.where(whole(slot_at, per_unit) == j, slot_at + first_page, wanted)
    found = jnp.zeros(wide, jnp.int32)
    for b in range(ids.shape[0]):
        found = found + jnp.where(
            wanted == ids[b : b + 1, :], numbers(wide, 1) + b * wide[1], 0
        )
    source_col = jnp.sum(found, axis=1, keepdims=True)
    source_row = down(k_sub == k_lane, source_col)
    holder_col, holder_row = whole(source_col, pages_dev), whole(source_row, pages_dev)
    rank_col = across(
        (holder_col == holder_row) & (source_row < source_col), jnp.ones(square, jnp.int32)
    )
    place_ref[0:1, :] = index_row(
        down(k_sub == k_lane, holder_col * capacity + rank_col), pages_dev
    )
    own_lengths = jnp.zeros((1, pages_dev), jnp.int32)
    for j in range(U_DEV):
        own_lengths = jnp.where(
            lax.broadcasted_iota(jnp.int32, (1, pages_dev), 1) == j,
            lengths[0, units_s[0, me * U_DEV + j] // KVH], own_lengths,
        )
    place_ref[1:2, :] = own_lengths

    @pl.loop(1, half)
    def _(offset):
        source = near_sender(offset)
        part_copy(offset, here, lax.rem(here + half - offset, half), source).wait_recv()

    def half_sum(which):
        def add(offset, carry):
            block = part_in.at[lax.rem(here + offset, half), which]
            return tuple(c + block[j].astype(jnp.float32) for j, c in enumerate(carry))

        first = tuple(
            part_out[here, which, j].astype(jnp.float32) for j in range(U_DEV + 1)
        )
        return lax.fori_loop(1, half, add, first)

    away = half_sum(1 - side)
    for j in range(U_DEV):
        swap_out[j] = away[j].astype(jnp.bfloat16)
    swap_out[U_DEV] = pack_totals([unpack_total(away[U_DEV], j) for j in range(U_DEV)])
    kept = half_sum(side)
    swap_copy().start()
    send_pages(4)
    swap_copy().wait_recv()
    packed = kept[U_DEV] + swap_in[U_DEV].astype(jnp.float32)
    for j in range(U_DEV):
        total = own_totals[j] + unpack_total(packed, j)
        weighted = own_sums[j] + kept[j] + swap_in[j].astype(jnp.float32)
        att_all[me * U_DEV + j] = (weighted / total).astype(jnp.bfloat16)

    att_copy(0, 0, me, partner).start()

    @pl.loop(1, half)
    def _(offset):
        att_copy(0, offset, me, near(offset)).start()

    send_pages(5)
    att_copy(0, 0, partner, partner).wait_recv()

    @pl.loop(1, half)
    def _(offset):
        att_copy(1, offset, partner, near(offset)).start()

    for batch in range(6, batches):
        send_pages(batch)

    @pl.loop(1, half)
    def _(offset):
        source = near_sender(offset)
        att_copy(0, offset, source, source).wait_recv()
        att_copy(1, offset, lax.rem(source + half, devices), source).wait_recv()

    for r in range(requests):
        for h in range(KVH):
            slot = table[of_slot, r * KVH + h]
            spread[h * span + r * 2 * group_count : h * span + (r + 1) * 2 * group_count, :] = (
                att_all[slot].astype(jnp.float32)
            )
    for h in range(KVH):
        for g in range(group_count):
            at = (h * group_count + g) * HD
            flat[:, at : at + HD] = spread[
                pl.ds(h * span + g, rows, stride=group_count), :
            ].astype(jnp.bfloat16)
    for c in range(tiles):
        loads[heads + c].wait()
        mixed_ref[:, c * HD : (c + 1) * HD] = lax.dot_general(
            flat[...], out_w[c], NT, preferred_element_type=jnp.float32
        ).astype(jnp.bfloat16)

    own_pages.wait()

    row_copy(0, 0, me, partner).wait_send()
    att_copy(0, 0, me, partner).wait_send()
    swap_copy().wait_send()

    @pl.loop(1, half)
    def _(offset):
        for stage, owner in ((0, me), (1, partner)):
            row_copy(stage, offset, owner, near(offset)).wait_send()
            att_copy(stage, offset, owner, near(offset)).wait_send()
        part_copy(offset, lax.rem(here + offset, half), here, near(offset)).wait_send()

    for rank in range(capacity):
        page_copy(rank, 0, partner).wait_send()
        page_arrival(rank, 0, partner).wait_recv()

        @pl.loop(1, half)
        def _(offset):
            page_copy(rank, offset, far(offset)).wait_send()
            page_arrival(rank, offset, far_sender(offset)).wait_recv()
            page_copy(rank, half + offset, near(offset)).wait_send()
            page_arrival(rank, half + offset, near_sender(offset)).wait_recv()


def fused_body(hidden_states, qkv_weight, out_weight, cache_pages, context_lengths, new_units, old_pages):
    devices = lax.axis_size("tp")
    requests = hidden_states.shape[0]
    rows = requests * 2
    pages_dev = cache_pages.shape[0]
    capacity = pages_dev // devices
    heads = qkv_weight.shape[0] // HD
    tiles = out_weight.shape[0] // HD
    group_count = HEADS // KVH
    units = new_units.shape[0]
    hbm = pl.BlockSpec(memory_space=pl.ANY)
    vmem = pl.BlockSpec(memory_space=pltpu.VMEM)
    smem = pl.BlockSpec(memory_space=pltpu.SMEM)
    dma = pltpu.SemaphoreType.DMA
    lengths = context_lengths.reshape(1, requests)
    unit_table = new_units.reshape(1, units)
    page_table = old_pages.reshape(-1, PAGE)
    tile = (2 * group_count, HD)
    f32, bf16, i32 = jnp.float32, jnp.bfloat16, jnp.int32
    arrived, mixed, fresh, place = pl.pallas_call(
        lambda *refs: layer_kernel(devices, capacity, *refs),
        out_shape=(
            jax.ShapeDtypeStruct(cache_pages.shape, bf16),
            jax.ShapeDtypeStruct((rows, out_weight.shape[0]), bf16),
            jax.ShapeDtypeStruct((U_DEV, 2, 2 * HD), f32),
            jax.ShapeDtypeStruct((2, pages_dev), i32),
        ),
        in_specs=[pl.BlockSpec(memory_space=pltpu.HBM)] * 7,
        out_specs=(hbm, vmem, vmem, vmem),
        scratch_shapes=[
            pltpu.SMEM(lengths.shape, i32),
            pltpu.SMEM(unit_table.shape, i32),
            pltpu.VMEM(unit_table.shape, i32),
            pltpu.VMEM(page_table.shape, i32),
            pltpu.VMEM((8, pages_dev), i32),
            pltpu.SMEM((8, pages_dev), i32),
            pltpu.VMEM(hidden_states.shape, bf16),
            pltpu.VMEM((rows, D), f32),
            pltpu.VMEM((rows, D), bf16),
            pltpu.VMEM((rows, HD), f32),
            pltpu.VMEM((rows, HD), f32),
            pltpu.VMEM((heads, HD, D), bf16),
            pltpu.VMEM((tiles, HD, HEADS * HD), bf16),
            pltpu.VMEM(cache_pages.shape, bf16),
            pltpu.VMEM(cache_pages.shape, bf16),
            pltpu.VMEM((devices, heads, rows, HD), bf16),
            pltpu.VMEM((units * 2 * group_count, HD), f32),
            pltpu.VMEM((units,) + tile, bf16),
            pltpu.VMEM((KVH, rows, HD), bf16),
            pltpu.VMEM((KVH, rows, HD), bf16),
            pltpu.VMEM((devices // 2, 2, U_DEV + 1) + tile, bf16),
            pltpu.VMEM((devices // 2, 2, U_DEV + 1) + tile, bf16),
            pltpu.VMEM((U_DEV + 1,) + tile, bf16),
            pltpu.VMEM((U_DEV + 1,) + tile, bf16),
            pltpu.VMEM((units,) + tile, bf16),
            pltpu.VMEM((rows, HEADS * HD), bf16),
            dma((heads + tiles,)),
            dma((capacity, devices)), dma((capacity, devices)),
            dma((2, devices // 2)), dma((2, devices // 2)),
            dma((devices // 2,)), dma((devices // 2,)),
            dma((2, devices // 2)), dma((2, devices // 2)),
            dma(()), dma((6,)), dma((1,)),
        ],
        compiler_params=pltpu.CompilerParams(
            collective_id=0, has_side_effects=True, vmem_limit_bytes=44 << 20
        ),
        name="layer",
    )(*[pltpu.with_memory_space_constraint(x, pltpu.HBM) for x in (lengths, unit_table, page_table, hidden_states, qkv_weight, out_weight, cache_pages)])
    mixed_shape = (requests, 2, out_weight.shape[0])
    placed, mixed = pl.pallas_call(
        place_kernel,
        out_shape=(
            jax.ShapeDtypeStruct(cache_pages.shape, bf16),
            jax.ShapeDtypeStruct(mixed_shape, bf16),
        ),
        in_specs=[smem, vmem, vmem, vmem],
        out_specs=(hbm, hbm),
        scratch_shapes=[
            pltpu.VMEM((U_DEV, 2) + cache_pages.shape[1:], bf16),
            pltpu.VMEM(mixed_shape, bf16),
            dma((pages_dev,)), dma(()),
        ],
        compiler_params=pltpu.CompilerParams(vmem_limit_bytes=8 << 20),
        name="place_pages",
    )(place, arrived, fresh, mixed)
    return (mixed, placed)


def body(hidden_states, qkv_weight, out_weight, cache_pages, context_lengths, new_units, old_pages):
    devices = lax.axis_size("tp")
    whole_heads = qkv_weight.shape[0] % HD == 0 and out_weight.shape[0] % HD == 0
    pages_dev = cache_pages.shape[0]
    whole_shares = pages_dev % devices == 0 and devices % 4 == 0 and hidden_states.shape[0] == KVH
    whole_shares = whole_shares and new_units.shape[0] == pages_dev and PAGE % pages_dev == 0
    chosen = fused_body if whole_heads and whole_shares else plain_body
    return chosen(
        hidden_states, qkv_weight, out_weight, cache_pages, context_lengths, new_units, old_pages
    )


def solution(mesh):
    in_specs = (
        P("group", None, None),
        P("tp", None),
        P("tp", None),
        P(("group", "tp"), None, None),
        P("group"),
        P("group"),
        P("group"),
    )
    out_specs = (P("group", None, "tp"), P(("group", "tp"), None, None))
    return jax.shard_map(body, mesh=mesh, in_specs=in_specs, out_specs=out_specs, check_vma=False)
```

```python
import math

import jax
import jax.numpy as jnp
from jax import lax
from jax.experimental import pallas as pl
from jax.experimental.pallas import tpu as pltpu
from jax.sharding import PartitionSpec as P

D = 8192
HEADS = 64
KVH = 8
HD = 128
U_DEV = 4
MAXCTX = 2048
PAGE = 128


rope_base = 10000.0


def rotate_positions(values, positions):
    half_dim = values.shape[-1] // 2
    frequency = rope_base ** (-(jnp.arange(half_dim, dtype=jnp.float32) * 2.0 / values.shape[-1]))
    angles = positions.astype(jnp.float32)[..., None] * frequency
    cosine = jnp.concatenate([jnp.cos(angles), jnp.cos(angles)], axis=-1)
    sine_table = jnp.concatenate([jnp.sin(angles), jnp.sin(angles)], axis=-1)
    turned = jnp.concatenate([-values[..., half_dim:], values[..., :half_dim]], axis=-1)
    return values * cosine + turned * sine_table


def prepare(unit_qkv, base_lengths):
    group_count = HEADS // KVH
    count_units = unit_qkv.shape[0]
    positions = base_lengths[:, None] + jnp.arange(2, dtype=jnp.int32)[None, :]
    widened = unit_qkv.astype(jnp.float32)
    queries = widened[..., : group_count * HD].reshape(count_units, 2, group_count, HD)
    queries = rotate_positions(queries, positions[:, :, None]).astype(jnp.bfloat16)
    new_keys = rotate_positions(
        widened[..., group_count * HD : (group_count + 1) * HD], positions
    ).astype(jnp.bfloat16)
    new_values = unit_qkv[..., (group_count + 1) * HD :]
    return (queries, new_keys, new_values)


def context_terms(context, queries, valid_count):
    score_scale = 1.0 / math.sqrt(HD)
    cached_keys = context[..., :HD]
    cached_values = context[..., HD:]
    scores = (
        jnp.einsum("psgd,ptd->psgt", queries, cached_keys, preferred_element_type=jnp.float32)
        * score_scale
    )
    visible = jnp.arange(context.shape[1], dtype=jnp.int32)[None, :] < valid_count[:, None]
    weights = jnp.where(visible[:, None, None, :], jnp.exp(scores), 0.0)
    totals = jnp.sum(weights, axis=-1)
    weighted = jnp.einsum(
        "psgt,ptd->psgd",
        weights.astype(jnp.bfloat16),
        cached_values,
        preferred_element_type=jnp.float32,
    )
    return (weighted, totals)


def own_terms(queries, new_keys, new_values):
    score_scale = 1.0 / math.sqrt(HD)
    scores = (
        jnp.einsum("usgd,ujd->usgj", queries, new_keys, preferred_element_type=jnp.float32)
        * score_scale
    )
    recent = jnp.arange(2, dtype=jnp.int32)[None, :] <= jnp.arange(2, dtype=jnp.int32)[:, None]
    weights = jnp.where(recent[None, :, None, :], jnp.exp(scores), 0.0)
    totals = jnp.sum(weights, axis=-1)
    weighted = jnp.einsum(
        "usgj,ujd->usgd",
        weights.astype(jnp.bfloat16),
        new_values,
        preferred_element_type=jnp.float32,
    )
    return (weighted, totals)


def plain_body(hidden_states, qkv_weight, out_weight, cache_pages, context_lengths, new_units, old_pages):
    devices = lax.axis_size("tp")
    device = lax.axis_index("tp")
    requests = hidden_states.shape[0]
    rows_dev = qkv_weight.shape[0]
    pages_dev, page_rows, page_width = cache_pages.shape
    group_count = HEADS // KVH
    unit_rows = (group_count + 2) * HD
    per_unit = MAXCTX // PAGE
    unit_slots = U_DEV
    capacity = max(1, pages_dev // devices)
    total_units = new_units.shape[0]
    total_pages = old_pages.shape[0]
    flat_rows = hidden_states.reshape(requests * 2, D)
    partial_qkv = lax.dot_general(
        flat_rows, qkv_weight, (((1,), (1,)), ((), ())), preferred_element_type=jnp.float32
    )
    partial_qkv = partial_qkv.astype(jnp.bfloat16).reshape(requests, 2, rows_dev)
    slot_index = (
        jnp.zeros((total_units,), jnp.int32)
        .at[new_units]
        .set(jnp.arange(total_units, dtype=jnp.int32))
    )
    own_units = lax.dynamic_slice_in_dim(new_units, device * unit_slots, unit_slots)
    own_requests = own_units // KVH
    own_heads = own_units % KVH
    own_lengths = context_lengths[own_requests]
    local_ids = lax.dynamic_slice_in_dim(old_pages, device * pages_dev, pages_dev)
    local_units = local_ids // per_unit
    local_index = local_ids % per_unit
    target_dev = (slot_index[local_units] * per_unit + local_index) // pages_dev
    local_order = jnp.arange(pages_dev, dtype=jnp.int32)
    send_rank = jnp.sum(
        (
            (target_dev[:, None] == target_dev[None, :])
            & (local_order[None, :] < local_order[:, None])
        ).astype(jnp.int32),
        axis=1,
    )
    outgoing = (
        jnp.zeros((devices, capacity, page_rows, page_width), jnp.bfloat16)
        .at[target_dev, send_rank]
        .set(cache_pages)
    )
    arrived = lax.all_to_all(outgoing, "tp", split_axis=0, concat_axis=0, tiled=True)
    stored_position = (
        jnp.zeros((total_pages,), jnp.int32)
        .at[old_pages]
        .set(jnp.arange(total_pages, dtype=jnp.int32))
    )
    wanted = (
        own_units[:, None] * per_unit + jnp.arange(per_unit, dtype=jnp.int32)[None, :]
    ).reshape(pages_dev)
    source_pos = stored_position[wanted]
    source_dev = source_pos // pages_dev
    source_slot = source_pos % pages_dev
    arrival_rank = jnp.sum(
        (
            (source_dev[:, None] == source_dev[None, :])
            & (source_slot[None, :] < source_slot[:, None])
        ).astype(jnp.int32),
        axis=1,
    )
    relaid = arrived[source_dev, arrival_rank]
    contexts = relaid.reshape(unit_slots, MAXCTX, page_width)
    sources_per_head = unit_rows // rows_dev
    request_table = (new_units // KVH).reshape(devices, unit_slots)
    outgoing_rows = partial_qkv[request_table]
    incoming = lax.all_to_all(outgoing_rows, "tp", split_axis=0, concat_axis=0, tiled=True)
    grouped = jnp.moveaxis(incoming.reshape(KVH, sources_per_head, unit_slots, 2, rows_dev), 2, 0)
    chosen = jnp.take_along_axis(grouped, own_heads[:, None, None, None, None], axis=1)[:, 0]
    own_rows = chosen.transpose(0, 2, 1, 3).reshape(unit_slots, 2, unit_rows)
    queries, new_keys, new_values = prepare(own_rows, own_lengths)
    cache_sums, cache_totals = context_terms(contexts, queries, own_lengths)
    own_sums, own_totals = own_terms(queries, new_keys, new_values)
    attended = ((cache_sums + own_sums) / (cache_totals + own_totals)[..., None]).astype(
        jnp.bfloat16
    )
    attended = attended.reshape(unit_slots, 2, group_count * HD)
    all_heads = lax.all_gather(attended, "tp", axis=0, tiled=True)
    logical = (
        all_heads[slot_index]
        .reshape(requests, KVH, 2, group_count * HD)
        .transpose(0, 2, 1, 3)
        .reshape(requests * 2, HEADS * HD)
    )
    mixed_rows = lax.dot_general(
        logical, out_weight, (((1,), (1,)), ((), ())), preferred_element_type=jnp.float32
    )
    mixed_rows = mixed_rows.astype(jnp.bfloat16).reshape(requests, 2, out_weight.shape[0])
    fresh_rows = jnp.concatenate([new_keys, new_values], axis=-1)
    positions = jnp.arange(MAXCTX, dtype=jnp.int32)[None, :]
    contexts = jnp.where(
        (positions == own_lengths[:, None])[..., None], fresh_rows[:, 0:1], contexts
    )
    contexts = jnp.where(
        (positions == own_lengths[:, None] + 1)[..., None], fresh_rows[:, 1:2], contexts
    )
    return (mixed_rows, contexts.reshape(pages_dev, page_rows, page_width))


def place_kernel(
    table_ref, arrived_ref, fresh_ref, mixed_ref, out_ref, rows_ref, patched, rows, sem, rows_sem
):
    per_unit = MAXCTX // PAGE
    steps = fresh_ref.shape[1]

    def outward(at, src):
        return pltpu.make_async_copy(src, out_ref.at[at], sem)

    def place_of(slot, page):
        return slot * per_unit + lax.rem(table_ref[1, slot] // PAGE + page, per_unit)

    for slot in range(U_DEV):
        for page in range(steps, per_unit):
            at = place_of(slot, page)
            outward(at, arrived_ref.at[table_ref[0, at]]).start()

    for slot in range(U_DEV):
        for page in range(steps):
            at = place_of(slot, page)
            block = patched.at[slot, page]
            block[...] = arrived_ref[table_ref[0, at]]
            for step in range(steps):
                row = table_ref[1, slot] + step - (at - slot * per_unit) * PAGE

                @pl.when((row >= 0) & (row < PAGE))
                def _():
                    base = pl.multiple_of((row // 16) * 16, 16)
                    tile = block[pl.ds(base, 16), :]
                    line = lax.broadcasted_iota(jnp.int32, tile.shape, 0)
                    new = jnp.broadcast_to(fresh_ref[slot, step : step + 1, :], tile.shape)
                    mixed = jnp.where(line == row - base, new, tile.astype(jnp.float32))
                    block[pl.ds(base, 16), :] = mixed.astype(jnp.bfloat16)

            outward(at, block).start()

    mixed = mixed_ref[...].astype(jnp.float32)
    for r in range(rows.shape[0]):
        rows[r] = mixed[2 * r : 2 * r + 2].astype(jnp.bfloat16)
    rows_out = pltpu.make_async_copy(rows, rows_ref, rows_sem)
    rows_out.start()
    pltpu.make_async_copy(arrived_ref, out_ref, sem).wait()
    rows_out.wait()


NT = (((1,), (1,)), ((), ()))
PLAN = (4, 8, 12, 18, 24)


def layer_kernel(
    devices, capacity,
    lengths_hbm, units_hbm, ids_hbm, hidden_hbm, qkv_hbm, out_hbm, pages_hbm,
    arrived_hbm, mixed_hbm, fresh_hbm, place_hbm,
    lengths, units_s, units_v, ids, tables_v, table, hidden_in, hidden_wide, hidden_ref, cos_ref, sin_ref,
    qkv_w, out_w, unsorted, pages, rows_all, spread, queries, new_keys, new_values, part_out, part_in, swap_out, swap_in, att_all, flat,
    load_sem, page_send, page_recv, row_send, row_recv, part_send, part_recv, swap_send, swap_recv, att_send, att_recv,
    small_sem, table_sem, mixed_ref, fresh_ref, place_ref, result_sem,
):
    me = lax.axis_index("tp")
    pages_dev = pages.shape[0]
    rows = hidden_ref.shape[0]
    requests = rows // 2
    units = requests * KVH
    per_unit = MAXCTX // PAGE
    heads = qkv_w.shape[0]
    tiles = out_w.shape[0]
    group_count = HEADS // KVH
    head_rows = group_count + 2
    score_scale = 1.0 / math.sqrt(HD)
    span = requests * 2 * group_count
    in_order, of_query, of_left, of_target, of_slot = range(5)

    half, quarter = devices // 2, devices // 4
    here, side = lax.rem(me, half), me // half
    partner = lax.rem(me + half, devices)

    def near(offset):
        return side * half + lax.rem(here + offset, half)

    def far(turn):
        return (1 - side) * half + (turn // quarter) * quarter + lax.rem(turn + me, quarter)

    def remote(src, dst, send, recv, device):
        return pltpu.make_async_remote_copy(
            src_ref=src, dst_ref=dst, send_sem=send, recv_sem=recv,
            device_id={"tp": device}, device_id_type=pl.DeviceIdType.MESH,
        )

    def page_copy(rank, device):
        return remote(
            pages.at[device * capacity + rank], arrived_hbm.at[me * capacity + rank],
            page_send, page_recv, device,
        )

    def row_copy(kind, owner, device):
        block = rows_all.at[owner]
        return remote(block, block, row_send, row_recv.at[kind], device)

    def many_rows(count):
        blocks = rows_all.at[pl.ds(0, count)]
        return remote(blocks, blocks, row_send, row_recv.at[1], partner)

    def att_copy(device):
        block = att_all.at[here]
        return remote(block, block, att_send, att_recv, device)

    def many_att(count):
        blocks = att_all.at[pl.ds(0, count)]
        return remote(blocks, blocks, att_send, att_recv, partner)

    def part_copy(src, dst, device):
        return remote(part_out.at[src], part_in.at[dst], part_send, part_recv, device)

    def many_parts(count):
        return remote(
            part_out.at[pl.ds(0, count)], part_in.at[pl.ds(0, count)], part_send, part_recv, partner
        )

    def swap_copy():
        return remote(swap_out, swap_in, swap_send, swap_recv, partner)

    turns = half * capacity

    def send_pages(start, stop):
        @pl.loop(start, stop)
        def _(turn):
            rank, place = turn // half, lax.rem(turn, half)
            page_copy(rank, far(place)).start()

            @pl.when(place > 0)
            def _():
                page_copy(rank, near(place)).start()

    def share(numerator):
        return turns * numerator // 32

    def pack_totals(values):
        packed = jnp.zeros((2 * group_count, PAGE), jnp.float32)
        for j, total in enumerate(values):
            top = total.astype(jnp.bfloat16).astype(jnp.float32)
            packed = jnp.where(lane == j * strip, top, packed)
            packed = jnp.where(lane == j * strip + strip // 2, total - top, packed)
        return packed.astype(jnp.bfloat16)

    def unpack_total(packed, j):
        return jnp.sum(jnp.where(lane // strip == j, packed, 0.0), axis=-1, keepdims=True)

    lane = lax.broadcasted_iota(jnp.int32, (2 * group_count, PAGE), 1)
    strip = PAGE // U_DEV

    barrier = pltpu.get_barrier_semaphore()

    @pl.loop(1, devices)
    def _(offset):
        pl.semaphore_signal(
            barrier, inc=1, device_id={"tp": lax.rem(me + offset, devices)}, device_id_type=pl.DeviceIdType.MESH
        )

    small = [
        pltpu.make_async_copy(ids_hbm, ids, small_sem.at[0]),
        pltpu.make_async_copy(units_hbm, units_v, small_sem.at[1]),
        pltpu.make_async_copy(units_hbm, units_s, small_sem.at[2]),
        pltpu.make_async_copy(lengths_hbm, lengths, small_sem.at[3]),
    ]
    load_pages = pltpu.make_async_copy(pages_hbm, unsorted, small_sem.at[4])
    load_hidden = pltpu.make_async_copy(hidden_hbm, hidden_in, small_sem.at[5])
    loads = [
        pltpu.make_async_copy(qkv_hbm.at[pl.ds(c * HD, HD)], qkv_w.at[c], load_sem.at[c])
        for c in range(heads)
    ]
    loads += [
        pltpu.make_async_copy(
            out_hbm.at[pl.ds(c * HD, HD)], out_w.at[c], load_sem.at[heads + c]
        )
        for c in range(tiles)
    ]
    for load in small + [load_pages]:
        load.start()

    def numbers(shape, axis):
        return lax.broadcasted_iota(jnp.int32, shape, axis)

    def whole(values, size):
        return lax.shift_right_logical(values, jnp.full_like(values, size.bit_length() - 1))

    def index_row(values, size):
        return jnp.clip(values, 0, size - 1)

    def down(hit, values):
        return jnp.sum(jnp.where(hit, values, 0), axis=0, keepdims=True)

    def across(hit, values):
        return jnp.sum(jnp.where(hit, values, 0), axis=1, keepdims=True)

    square = (pages_dev, pages_dev)
    k_sub, k_lane = numbers(square, 0), numbers(square, 1)
    small[0].wait()
    first = me * pages_dev
    wide = (pages_dev, ids.shape[1])
    own_ids = ids[pl.ds(first // ids.shape[1], 1), :]
    mine = numbers(wide, 1) == numbers(wide, 0) + lax.rem(first, ids.shape[1])
    id_col = across(mine, own_ids)
    small[1].wait()
    unit_row = units_v[...]
    by_unit = (pages_dev, units)
    slot_col = across(whole(id_col, per_unit) == unit_row, numbers(by_unit, 1))
    target_col = whole(slot_col, U_DEV)
    target_row = down(k_sub == k_lane, target_col)
    rank_col = across((target_col == target_row) & (k_lane < k_sub), jnp.ones(square, jnp.int32))
    sent = target_col * capacity + rank_col == k_lane
    tables_v[in_order : in_order + 1, :] = index_row(down(sent, k_sub), pages_dev)
    id_row = down(sent, id_col)
    tables_v[of_target : of_target + 1, :] = down(sent, slot_col - target_col * U_DEV)
    sent_unit = whole(id_row, per_unit)
    sent_request = whole(sent_unit, KVH)
    small[3].wait()
    sent_length = jnp.zeros_like(id_row)
    for r in range(requests):
        sent_length = jnp.where(sent_request == r, lengths[0, r], sent_length)
    tables_v[of_query : of_query + 1, :] = index_row(
        (sent_unit - sent_request * KVH) * requests + sent_request, units
    )
    tables_v[of_left : of_left + 1, :] = sent_length - (id_row - sent_unit * per_unit) * PAGE
    u_square = (units, units)
    u_sub, u_lane = numbers(u_square, 0), numbers(u_square, 1)
    unit_col = across(u_sub == u_lane, unit_row)
    u_device = whole(u_sub, U_DEV)
    u_side = whole(u_device, half)
    u_place = (u_device - u_side * half) * (2 * U_DEV) + u_side * U_DEV + (u_sub - u_device * U_DEV)
    tables_v[of_slot : of_slot + 1, :] = index_row(down(unit_col == u_lane, u_place), units)
    to_table = pltpu.make_async_copy(tables_v, table, table_sem.at[0])
    to_table.start()

    load_pages.wait()
    for load in [load_hidden] + loads[:heads]:
        load.start()
    to_table.wait()

    @pl.loop(0, pages_dev)
    def _(i):
        pages[i] = unsorted[table[in_order, i]]

    pl.semaphore_wait(barrier, devices - 1)
    send_pages(0, share(PLAN[0]))

    small[2].wait()
    row_at = lax.broadcasted_iota(jnp.int32, (rows, HD), 0)
    lane_at = lax.broadcasted_iota(jnp.int32, (rows, HD), 1)
    positions = jnp.zeros((rows, HD), jnp.float32)
    for r in range(requests):
        positions = jnp.where(row_at // 2 == r, lengths[0, r].astype(jnp.float32), positions)
    positions = positions + (row_at % 2).astype(jnp.float32)
    power = (lane_at % (HD // 2)).astype(jnp.float32) * (2.0 / HD)
    angles = positions * jnp.exp(power * -math.log(rope_base))
    cos_ref[...] = jnp.cos(angles)
    sin_ref[...] = jnp.where(lane_at < HD // 2, -jnp.sin(angles), jnp.sin(angles))
    load_hidden.wait()
    for r in range(requests):
        hidden_wide[2 * r : 2 * r + 2, :] = hidden_in[r].astype(jnp.float32)
    hidden_ref[...] = hidden_wide[...].astype(jnp.bfloat16)

    for c in range(heads):
        loads[c].wait()
        part = lax.dot_general(
            hidden_ref[...], qkv_w[c], NT, preferred_element_type=jnp.float32
        ).astype(jnp.bfloat16).astype(jnp.float32)
        turned = part * cos_ref[...] + pltpu.roll(part, HD // 2, 1) * sin_ref[...]
        is_value = lax.rem(me * heads + c, head_rows) == head_rows - 1
        rows_all[me, c] = jnp.where(is_value, part, turned).astype(jnp.bfloat16)

    row_copy(0, me, partner).start()

    @pl.loop(1, half)
    def _(offset):
        row_copy(1, me, near(offset)).start()

    send_pages(share(PLAN[0]), share(PLAN[1]))
    for load in loads[heads:]:
        load.start()
    own_pages = pltpu.make_async_copy(
        pages.at[pl.ds(me * capacity, capacity)],
        arrived_hbm.at[pl.ds(me * capacity, capacity)],
        page_recv,
    )
    own_pages.start()

    row_copy(0, partner, partner).wait_recv()

    @pl.loop(1, half)
    def _(offset):
        row_copy(1, partner, near(offset)).start()

    send_pages(share(PLAN[1]), share(PLAN[2]))

    many_rows(devices - 2).wait_recv()

    for h in range(KVH):
        for g in range(group_count):
            at = h * head_rows + g
            spread[pl.ds(h * span + g, rows, stride=group_count), :] = rows_all[
                at // heads, at % heads
            ].astype(jnp.float32)
        at = h * head_rows + group_count
        new_keys[h] = rows_all[at // heads, at % heads]
        new_values[h] = rows_all[(at + 1) // heads, (at + 1) % heads]
        for r in range(requests):
            start = h * span + r * 2 * group_count
            queries[h * requests + r] = spread[start : start + 2 * group_count, :].astype(
                jnp.bfloat16
            )

    @pl.loop(0, devices)
    def _(target):
        spent = share(PLAN[3]) - share(PLAN[2])
        send_pages(
            share(PLAN[2]) + target * spent // devices,
            share(PLAN[2]) + (target + 1) * spent // devices,
        )
        zero = jnp.zeros((2 * group_count, PAGE), jnp.float32)
        sums, totals = [zero] * U_DEV, [zero[:, :1]] * U_DEV
        for rank in range(capacity):
            query = queries[table[of_query, target * capacity + rank]]
            left = table[of_left, target * capacity + rank]
            page = pages[target * capacity + rank]
            scores = lax.dot_general(
                query, page[:, :HD], NT, preferred_element_type=jnp.float32
            ) * score_scale
            weights = jnp.where(lane < left, jnp.exp(scores), 0.0)
            total = jnp.sum(weights, axis=-1, keepdims=True)
            weighted = jnp.dot(
                weights.astype(jnp.bfloat16), page[:, HD:], preferred_element_type=jnp.float32
            )
            slot = table[of_target, target * capacity + rank]
            for j in range(U_DEV):
                sums[j] = sums[j] + jnp.where(slot == j, weighted, 0.0)
                totals[j] = totals[j] + jnp.where(slot == j, total, 0.0)
        place, which = lax.rem(target, half), target // half
        for j in range(U_DEV):
            part_out[place, which, j] = sums[j].astype(jnp.bfloat16)
        part_out[place, which, U_DEV] = pack_totals(totals)

    @pl.loop(1, half)
    def _(offset):
        part_copy(lax.rem(here + offset, half), here, near(offset)).start()

    own_sums, own_totals = [], []
    row = lax.broadcasted_iota(jnp.int32, (2 * group_count, rows), 0)
    col = lax.broadcasted_iota(jnp.int32, (2 * group_count, rows), 1)
    line = lax.broadcasted_iota(jnp.int32, (rows, HD), 0)
    for j in range(2 * U_DEV):
        unit = units_s[0, (j // U_DEV * half + here) * U_DEV + j % U_DEV]
        request, head = unit // KVH, unit % KVH
        scores = lax.dot_general(
            queries[head * requests + request], new_keys[head], NT, preferred_element_type=jnp.float32
        ) * score_scale
        seen = (col // 2 == request) & (col % 2 <= row // group_count)
        weights = jnp.where(seen, jnp.exp(scores), 0.0)
        own_totals.append(jnp.sum(weights, axis=-1, keepdims=True))
        own_sums.append(
            jnp.dot(weights.astype(jnp.bfloat16), new_values[head], preferred_element_type=jnp.float32)
        )
    for j in range(U_DEV):
        unit = units_s[0, me * U_DEV + j]
        request, head = unit // KVH, unit % KVH
        for step in range(2):
            mine = line == request * 2 + step
            for part, kind in ((0, new_keys[head]), (1, new_values[head])):
                fresh_ref[j, step : step + 1, part * HD : (part + 1) * HD] = jnp.sum(
                    jnp.where(mine, kind.astype(jnp.float32), 0.0), axis=0, keepdims=True
                )

    slot_at = numbers((pages_dev, 1), 0)
    wanted = jnp.zeros((pages_dev, 1), jnp.int32)
    for j in range(U_DEV):
        first_page = units_s[0, me * U_DEV + j] * per_unit - j * per_unit
        wanted = jnp.where(whole(slot_at, per_unit) == j, slot_at + first_page, wanted)
    found = jnp.zeros(wide, jnp.int32)
    for b in range(ids.shape[0]):
        found = found + jnp.where(
            wanted == ids[b : b + 1, :], numbers(wide, 1) + b * wide[1], 0
        )
    source_col = jnp.sum(found, axis=1, keepdims=True)
    source_row = down(k_sub == k_lane, source_col)
    holder_col, holder_row = whole(source_col, pages_dev), whole(source_row, pages_dev)
    rank_col = across(
        (holder_col == holder_row) & (source_row < source_col), jnp.ones(square, jnp.int32)
    )
    place_ref[0:1, :] = index_row(
        down(k_sub == k_lane, holder_col * capacity + rank_col), pages_dev
    )
    own_lengths = jnp.zeros((1, pages_dev), jnp.int32)
    for j in range(U_DEV):
        own_lengths = jnp.where(
            lax.broadcasted_iota(jnp.int32, (1, pages_dev), 1) == j,
            lengths[0, units_s[0, me * U_DEV + j] // KVH], own_lengths,
        )
    place_ref[1:2, :] = own_lengths

    many_parts(half - 1).wait_recv()

    def half_sum(which):
        def add(offset, carry):
            block = part_in.at[lax.rem(here + offset, half), which]
            return tuple(c + block[j].astype(jnp.float32) for j, c in enumerate(carry))

        first = tuple(
            part_out[here, which, j].astype(jnp.float32) for j in range(U_DEV + 1)
        )
        return lax.fori_loop(1, half, add, first)

    kept = half_sum(0) + half_sum(1)
    blocks = U_DEV + 1
    for which in range(2):
        for j in range(U_DEV):
            swap_out[which * blocks + j] = kept[which * blocks + j].astype(jnp.bfloat16)
        packed = kept[which * blocks + U_DEV]
        swap_out[which * blocks + U_DEV] = pack_totals(
            [unpack_total(packed, j) for j in range(U_DEV)]
        )
    swap_copy().start()
    send_pages(share(PLAN[3]), share(PLAN[4]))
    swap_copy().wait_recv()
    for which in range(2):
        last = which * blocks + U_DEV
        packed = kept[last] + swap_in[last].astype(jnp.float32)
        for j in range(U_DEV):
            at = which * blocks + j
            total = own_totals[which * U_DEV + j] + unpack_total(packed, j)
            weighted = own_sums[which * U_DEV + j] + kept[at] + swap_in[at].astype(jnp.float32)
            att_all[here, which * U_DEV + j] = (weighted / total).astype(jnp.bfloat16)

    @pl.loop(1, half)
    def _(offset):
        att_copy(near(offset)).start()

    send_pages(share(PLAN[4]), turns)
    many_att(half - 1).wait_recv()

    for r in range(requests):
        for h in range(KVH):
            slot = table[of_slot, r * KVH + h]
            spread[h * span + r * 2 * group_count : h * span + (r + 1) * 2 * group_count, :] = (
                att_all[slot // (2 * U_DEV), slot % (2 * U_DEV)].astype(jnp.float32)
            )
    for h in range(KVH):
        for g in range(group_count):
            at = (h * group_count + g) * HD
            flat[:, at : at + HD] = spread[
                pl.ds(h * span + g, rows, stride=group_count), :
            ].astype(jnp.bfloat16)
    for c in range(tiles):
        loads[heads + c].wait()
        mixed_ref[:, c * HD : (c + 1) * HD] = lax.dot_general(
            flat[...], out_w[c], NT, preferred_element_type=jnp.float32
        ).astype(jnp.bfloat16)

    results = [
        pltpu.make_async_copy(src, dst, result_sem.at[i])
        for i, (src, dst) in enumerate(
            ((mixed_ref, mixed_hbm), (fresh_ref, fresh_hbm), (place_ref, place_hbm))
        )
    ]
    for result in results:
        result.start()
    for result in results:
        result.wait()
    remote(arrived_hbm, arrived_hbm, page_send, page_recv, partner).wait_recv()
    sent_pages = pages.at[pl.ds(0, (devices - 1) * capacity)]
    remote(sent_pages, sent_pages, page_send, page_recv, partner).wait_send()
    many_rows(devices - 1).wait_send()
    many_parts(half - 1).wait_send()
    swap_copy().wait_send()
    many_att(half - 1).wait_send()


def fused_body(hidden_states, qkv_weight, out_weight, cache_pages, context_lengths, new_units, old_pages):
    devices = lax.axis_size("tp")
    requests = hidden_states.shape[0]
    rows = requests * 2
    pages_dev = cache_pages.shape[0]
    capacity = pages_dev // devices
    heads = qkv_weight.shape[0] // HD
    tiles = out_weight.shape[0] // HD
    group_count = HEADS // KVH
    units = new_units.shape[0]
    hbm = pl.BlockSpec(memory_space=pl.ANY)
    vmem = pl.BlockSpec(memory_space=pltpu.VMEM)
    smem = pl.BlockSpec(memory_space=pltpu.SMEM)
    dma = pltpu.SemaphoreType.DMA
    lengths = context_lengths.reshape(1, requests)
    unit_table = new_units.reshape(1, units)
    page_table = old_pages.reshape(-1, PAGE)
    tile = (2 * group_count, HD)
    f32, bf16, i32 = jnp.float32, jnp.bfloat16, jnp.int32
    arrived, mixed, fresh, place = pl.pallas_call(
        lambda *refs: layer_kernel(devices, capacity, *refs),
        out_shape=(
            jax.ShapeDtypeStruct(cache_pages.shape, bf16),
            jax.ShapeDtypeStruct((rows, out_weight.shape[0]), bf16),
            jax.ShapeDtypeStruct((U_DEV, 2, 2 * HD), f32),
            jax.ShapeDtypeStruct((2, pages_dev), i32),
        ),
        in_specs=[pl.BlockSpec(memory_space=pltpu.HBM)] * 7,
        out_specs=(hbm, hbm, hbm, hbm),
        scratch_shapes=[
            pltpu.SMEM(lengths.shape, i32),
            pltpu.SMEM(unit_table.shape, i32),
            pltpu.VMEM(unit_table.shape, i32),
            pltpu.VMEM(page_table.shape, i32),
            pltpu.VMEM((8, pages_dev), i32),
            pltpu.SMEM((8, pages_dev), i32),
            pltpu.VMEM(hidden_states.shape, bf16),
            pltpu.VMEM((rows, D), f32),
            pltpu.VMEM((rows, D), bf16),
            pltpu.VMEM((rows, HD), f32),
            pltpu.VMEM((rows, HD), f32),
            pltpu.VMEM((heads, HD, D), bf16),
            pltpu.VMEM((tiles, HD, HEADS * HD), bf16),
            pltpu.VMEM(cache_pages.shape, bf16),
            pltpu.VMEM(cache_pages.shape, bf16),
            pltpu.VMEM((devices, heads, rows, HD), bf16),
            pltpu.VMEM((units * 2 * group_count, HD), f32),
            pltpu.VMEM((units,) + tile, bf16),
            pltpu.VMEM((KVH, rows, HD), bf16),
            pltpu.VMEM((KVH, rows, HD), bf16),
            pltpu.VMEM((devices // 2, 2, U_DEV + 1) + tile, bf16),
            pltpu.VMEM((devices // 2, 2, U_DEV + 1) + tile, bf16),
            pltpu.VMEM((2 * (U_DEV + 1),) + tile, bf16),
            pltpu.VMEM((2 * (U_DEV + 1),) + tile, bf16),
            pltpu.VMEM((devices // 2, 2 * U_DEV) + tile, bf16),
            pltpu.VMEM((rows, HEADS * HD), bf16),
            dma((heads + tiles,)),
            dma(()), dma(()),
            dma(()), dma((2,)),
            dma(()), dma(()), dma(()), dma(()),
            dma(()), dma(()),
            dma((6,)), dma((1,)),
            pltpu.VMEM((rows, out_weight.shape[0]), bf16),
            pltpu.VMEM((U_DEV, 2, 2 * HD), f32),
            pltpu.VMEM((2, pages_dev), i32),
            dma((3,)),
        ],
        compiler_params=pltpu.CompilerParams(
            collective_id=0, has_side_effects=True, vmem_limit_bytes=44 << 20
        ),
        name="layer",
    )(*[pltpu.with_memory_space_constraint(x, pltpu.HBM) for x in (lengths, unit_table, page_table, hidden_states, qkv_weight, out_weight, cache_pages)])
    mixed_shape = (requests, 2, out_weight.shape[0])
    placed, mixed = pl.pallas_call(
        place_kernel,
        out_shape=(
            jax.ShapeDtypeStruct(cache_pages.shape, bf16),
            jax.ShapeDtypeStruct(mixed_shape, bf16),
        ),
        in_specs=[smem, vmem, vmem, vmem],
        out_specs=(hbm, hbm),
        scratch_shapes=[
            pltpu.VMEM((U_DEV, 2) + cache_pages.shape[1:], bf16),
            pltpu.VMEM(mixed_shape, bf16),
            dma(()), dma(()),
        ],
        compiler_params=pltpu.CompilerParams(vmem_limit_bytes=8 << 20),
        name="place_pages",
    )(place, arrived, fresh, mixed)
    return (mixed, placed)


def body(hidden_states, qkv_weight, out_weight, cache_pages, context_lengths, new_units, old_pages):
    devices = lax.axis_size("tp")
    whole_heads = qkv_weight.shape[0] % HD == 0 and out_weight.shape[0] % HD == 0
    pages_dev = cache_pages.shape[0]
    whole_shares = pages_dev % devices == 0 and devices % 4 == 0 and hidden_states.shape[0] == KVH
    whole_shares = whole_shares and new_units.shape[0] == pages_dev and PAGE % pages_dev == 0
    chosen = fused_body if whole_heads and whole_shares else plain_body
    return chosen(
        hidden_states, qkv_weight, out_weight, cache_pages, context_lengths, new_units, old_pages
    )


def solution(mesh):
    in_specs = (
        P("group", None, None),
        P("tp", None),
        P("tp", None),
        P(("group", "tp"), None, None),
        P("group"),
        P("group"),
        P("group"),
    )
    out_specs = (P("group", None, "tp"), P(("group", "tp"), None, None))
    return jax.shard_map(body, mesh=mesh, in_specs=in_specs, out_specs=out_specs, check_vma=False)
```

```python
import math

import jax
import jax.numpy as jnp
from jax import lax
from jax.experimental import pallas as pl
from jax.experimental.pallas import tpu as pltpu
from jax.sharding import PartitionSpec as P

D = 8192
HEADS = 64
KVH = 8
HD = 128
U_DEV = 4
MAXCTX = 2048
PAGE = 128


rope_base = 10000.0


def rotate_positions(values, positions):
    half_dim = values.shape[-1] // 2
    frequency = rope_base ** (-(jnp.arange(half_dim, dtype=jnp.float32) * 2.0 / values.shape[-1]))
    angles = positions.astype(jnp.float32)[..., None] * frequency
    cosine = jnp.concatenate([jnp.cos(angles), jnp.cos(angles)], axis=-1)
    sine_table = jnp.concatenate([jnp.sin(angles), jnp.sin(angles)], axis=-1)
    turned = jnp.concatenate([-values[..., half_dim:], values[..., :half_dim]], axis=-1)
    return values * cosine + turned * sine_table


def prepare(unit_qkv, base_lengths):
    group_count = HEADS // KVH
    count_units = unit_qkv.shape[0]
    positions = base_lengths[:, None] + jnp.arange(2, dtype=jnp.int32)[None, :]
    widened = unit_qkv.astype(jnp.float32)
    queries = widened[..., : group_count * HD].reshape(count_units, 2, group_count, HD)
    queries = rotate_positions(queries, positions[:, :, None]).astype(jnp.bfloat16)
    new_keys = rotate_positions(
        widened[..., group_count * HD : (group_count + 1) * HD], positions
    ).astype(jnp.bfloat16)
    new_values = unit_qkv[..., (group_count + 1) * HD :]
    return (queries, new_keys, new_values)


def context_terms(context, queries, valid_count):
    score_scale = 1.0 / math.sqrt(HD)
    cached_keys = context[..., :HD]
    cached_values = context[..., HD:]
    scores = (
        jnp.einsum("psgd,ptd->psgt", queries, cached_keys, preferred_element_type=jnp.float32)
        * score_scale
    )
    visible = jnp.arange(context.shape[1], dtype=jnp.int32)[None, :] < valid_count[:, None]
    weights = jnp.where(visible[:, None, None, :], jnp.exp(scores), 0.0)
    totals = jnp.sum(weights, axis=-1)
    weighted = jnp.einsum(
        "psgt,ptd->psgd",
        weights.astype(jnp.bfloat16),
        cached_values,
        preferred_element_type=jnp.float32,
    )
    return (weighted, totals)


def own_terms(queries, new_keys, new_values):
    score_scale = 1.0 / math.sqrt(HD)
    scores = (
        jnp.einsum("usgd,ujd->usgj", queries, new_keys, preferred_element_type=jnp.float32)
        * score_scale
    )
    recent = jnp.arange(2, dtype=jnp.int32)[None, :] <= jnp.arange(2, dtype=jnp.int32)[:, None]
    weights = jnp.where(recent[None, :, None, :], jnp.exp(scores), 0.0)
    totals = jnp.sum(weights, axis=-1)
    weighted = jnp.einsum(
        "usgj,ujd->usgd",
        weights.astype(jnp.bfloat16),
        new_values,
        preferred_element_type=jnp.float32,
    )
    return (weighted, totals)


def plain_body(hidden_states, qkv_weight, out_weight, cache_pages, context_lengths, new_units, old_pages):
    devices = lax.axis_size("tp")
    device = lax.axis_index("tp")
    requests = hidden_states.shape[0]
    rows_dev = qkv_weight.shape[0]
    pages_dev, page_rows, page_width = cache_pages.shape
    group_count = HEADS // KVH
    unit_rows = (group_count + 2) * HD
    per_unit = MAXCTX // PAGE
    unit_slots = U_DEV
    capacity = max(1, pages_dev // devices)
    total_units = new_units.shape[0]
    total_pages = old_pages.shape[0]
    flat_rows = hidden_states.reshape(requests * 2, D)
    partial_qkv = lax.dot_general(
        flat_rows, qkv_weight, (((1,), (1,)), ((), ())), preferred_element_type=jnp.float32
    )
    partial_qkv = partial_qkv.astype(jnp.bfloat16).reshape(requests, 2, rows_dev)
    slot_index = (
        jnp.zeros((total_units,), jnp.int32)
        .at[new_units]
        .set(jnp.arange(total_units, dtype=jnp.int32))
    )
    own_units = lax.dynamic_slice_in_dim(new_units, device * unit_slots, unit_slots)
    own_requests = own_units // KVH
    own_heads = own_units % KVH
    own_lengths = context_lengths[own_requests]
    local_ids = lax.dynamic_slice_in_dim(old_pages, device * pages_dev, pages_dev)
    local_units = local_ids // per_unit
    local_index = local_ids % per_unit
    target_dev = (slot_index[local_units] * per_unit + local_index) // pages_dev
    local_order = jnp.arange(pages_dev, dtype=jnp.int32)
    send_rank = jnp.sum(
        (
            (target_dev[:, None] == target_dev[None, :])
            & (local_order[None, :] < local_order[:, None])
        ).astype(jnp.int32),
        axis=1,
    )
    outgoing = (
        jnp.zeros((devices, capacity, page_rows, page_width), jnp.bfloat16)
        .at[target_dev, send_rank]
        .set(cache_pages)
    )
    arrived = lax.all_to_all(outgoing, "tp", split_axis=0, concat_axis=0, tiled=True)
    stored_position = (
        jnp.zeros((total_pages,), jnp.int32)
        .at[old_pages]
        .set(jnp.arange(total_pages, dtype=jnp.int32))
    )
    wanted = (
        own_units[:, None] * per_unit + jnp.arange(per_unit, dtype=jnp.int32)[None, :]
    ).reshape(pages_dev)
    source_pos = stored_position[wanted]
    source_dev = source_pos // pages_dev
    source_slot = source_pos % pages_dev
    arrival_rank = jnp.sum(
        (
            (source_dev[:, None] == source_dev[None, :])
            & (source_slot[None, :] < source_slot[:, None])
        ).astype(jnp.int32),
        axis=1,
    )
    relaid = arrived[source_dev, arrival_rank]
    contexts = relaid.reshape(unit_slots, MAXCTX, page_width)
    sources_per_head = unit_rows // rows_dev
    request_table = (new_units // KVH).reshape(devices, unit_slots)
    outgoing_rows = partial_qkv[request_table]
    incoming = lax.all_to_all(outgoing_rows, "tp", split_axis=0, concat_axis=0, tiled=True)
    grouped = jnp.moveaxis(incoming.reshape(KVH, sources_per_head, unit_slots, 2, rows_dev), 2, 0)
    chosen = jnp.take_along_axis(grouped, own_heads[:, None, None, None, None], axis=1)[:, 0]
    own_rows = chosen.transpose(0, 2, 1, 3).reshape(unit_slots, 2, unit_rows)
    queries, new_keys, new_values = prepare(own_rows, own_lengths)
    cache_sums, cache_totals = context_terms(contexts, queries, own_lengths)
    own_sums, own_totals = own_terms(queries, new_keys, new_values)
    attended = ((cache_sums + own_sums) / (cache_totals + own_totals)[..., None]).astype(
        jnp.bfloat16
    )
    attended = attended.reshape(unit_slots, 2, group_count * HD)
    all_heads = lax.all_gather(attended, "tp", axis=0, tiled=True)
    logical = (
        all_heads[slot_index]
        .reshape(requests, KVH, 2, group_count * HD)
        .transpose(0, 2, 1, 3)
        .reshape(requests * 2, HEADS * HD)
    )
    mixed_rows = lax.dot_general(
        logical, out_weight, (((1,), (1,)), ((), ())), preferred_element_type=jnp.float32
    )
    mixed_rows = mixed_rows.astype(jnp.bfloat16).reshape(requests, 2, out_weight.shape[0])
    fresh_rows = jnp.concatenate([new_keys, new_values], axis=-1)
    positions = jnp.arange(MAXCTX, dtype=jnp.int32)[None, :]
    contexts = jnp.where(
        (positions == own_lengths[:, None])[..., None], fresh_rows[:, 0:1], contexts
    )
    contexts = jnp.where(
        (positions == own_lengths[:, None] + 1)[..., None], fresh_rows[:, 1:2], contexts
    )
    return (mixed_rows, contexts.reshape(pages_dev, page_rows, page_width))


def place_kernel(
    table_ref, arrived_ref, fresh_ref, mixed_ref, out_ref, rows_ref, patched, rows, sem, rows_sem
):
    per_unit = MAXCTX // PAGE
    steps = fresh_ref.shape[1]

    def outward(at, src):
        return pltpu.make_async_copy(src, out_ref.at[at], sem)

    def place_of(slot, page):
        return slot * per_unit + lax.rem(table_ref[1, slot] // PAGE + page, per_unit)

    for slot in range(U_DEV):
        for page in range(steps, per_unit):
            at = place_of(slot, page)
            outward(at, arrived_ref.at[table_ref[0, at]]).start()

    for slot in range(U_DEV):
        for page in range(steps):
            at = place_of(slot, page)
            block = patched.at[slot, page]
            block[...] = arrived_ref[table_ref[0, at]]
            for step in range(steps):
                row = table_ref[1, slot] + step - (at - slot * per_unit) * PAGE

                @pl.when((row >= 0) & (row < PAGE))
                def _():
                    base = pl.multiple_of((row // 16) * 16, 16)
                    tile = block[pl.ds(base, 16), :]
                    line = lax.broadcasted_iota(jnp.int32, tile.shape, 0)
                    new = jnp.broadcast_to(fresh_ref[slot, step : step + 1, :], tile.shape)
                    mixed = jnp.where(line == row - base, new, tile.astype(jnp.float32))
                    block[pl.ds(base, 16), :] = mixed.astype(jnp.bfloat16)

            outward(at, block).start()

    mixed = mixed_ref[...].astype(jnp.float32)
    for r in range(rows.shape[0]):
        rows[r] = mixed[2 * r : 2 * r + 2].astype(jnp.bfloat16)
    rows_out = pltpu.make_async_copy(rows, rows_ref, rows_sem)
    rows_out.start()
    pltpu.make_async_copy(arrived_ref, out_ref, sem).wait()
    rows_out.wait()


NT = (((1,), (1,)), ((), ()))
PLAN = (4, 8, 12, 18, 24)


def layer_kernel(
    devices, capacity,
    lengths_hbm, units_hbm, ids_hbm, hidden_hbm, qkv_hbm, out_hbm, pages_hbm,
    arrived_hbm, mixed_hbm, fresh_hbm, place_hbm,
    lengths, units_s, units_v, ids, tables_v, table, hidden_in, hidden_wide, hidden_ref, cos_ref, sin_ref,
    qkv_w, out_w, unsorted, pages, rows_all, spread, queries, new_keys, new_values, part_out, part_in, swap_out, swap_in, att_all, flat,
    load_sem, page_send, page_recv, row_send, row_recv, part_send, part_recv, swap_send, swap_recv, att_send, att_recv,
    small_sem, table_sem, mixed_ref, fresh_ref, place_ref, result_sem,
):
    me = lax.axis_index("tp")
    pages_dev = pages.shape[0]
    rows = hidden_ref.shape[0]
    requests = rows // 2
    units = requests * KVH
    per_unit = MAXCTX // PAGE
    heads = qkv_w.shape[0]
    tiles = out_w.shape[0]
    group_count = HEADS // KVH
    head_rows = group_count + 2
    score_scale = 1.0 / math.sqrt(HD)
    span = requests * 2 * group_count
    in_order, of_query, of_left, of_target, of_slot = range(5)

    half, quarter = devices // 2, devices // 4
    here, side = lax.rem(me, half), me // half
    partner = lax.rem(me + half, devices)

    def near(offset):
        return side * half + lax.rem(here + offset, half)

    def far(turn):
        return (1 - side) * half + (turn // quarter) * quarter + lax.rem(turn + me, quarter)

    def remote(src, dst, send, recv, device):
        return pltpu.make_async_remote_copy(
            src_ref=src, dst_ref=dst, send_sem=send, recv_sem=recv,
            device_id={"tp": device}, device_id_type=pl.DeviceIdType.MESH,
        )

    def page_copy(rank, device):
        return remote(
            pages.at[device * capacity + rank], arrived_hbm.at[me * capacity + rank],
            page_send, page_recv, device,
        )

    def row_copy(kind, owner, device):
        block = rows_all.at[owner]
        return remote(block, block, row_send, row_recv.at[kind], device)

    def many_rows(count):
        blocks = rows_all.at[pl.ds(0, count)]
        return remote(blocks, blocks, row_send, row_recv.at[1], partner)

    def att_copy(device):
        block = att_all.at[here]
        return remote(block, block, att_send, att_recv, device)

    def many_att(count):
        blocks = att_all.at[pl.ds(0, count)]
        return remote(blocks, blocks, att_send, att_recv, partner)

    def part_copy(src, dst, device):
        return remote(part_out.at[src], part_in.at[dst], part_send, part_recv, device)

    def many_parts(count):
        return remote(
            part_out.at[pl.ds(0, count)], part_in.at[pl.ds(0, count)], part_send, part_recv, partner
        )

    def swap_copy():
        return remote(swap_out, swap_in, swap_send, swap_recv, partner)

    turns = half * capacity

    def send_pages(start, stop):
        @pl.loop(start, stop)
        def _(turn):
            rank, place = turn // half, lax.rem(turn, half)
            page_copy(rank, far(place)).start()

            @pl.when(place > 0)
            def _():
                page_copy(rank, near(place)).start()

    def share(numerator):
        return turns * numerator // 32

    def pack_totals(values):
        packed = jnp.zeros((2 * group_count, PAGE), jnp.float32)
        for j, total in enumerate(values):
            top = total.astype(jnp.bfloat16).astype(jnp.float32)
            packed = jnp.where(lane == j * strip, top, packed)
            packed = jnp.where(lane == j * strip + strip // 2, total - top, packed)
        return packed.astype(jnp.bfloat16)

    def unpack_total(packed, j):
        return jnp.sum(jnp.where(lane // strip == j, packed, 0.0), axis=-1, keepdims=True)

    lane = lax.broadcasted_iota(jnp.int32, (2 * group_count, PAGE), 1)
    strip = PAGE // U_DEV

    small = [
        pltpu.make_async_copy(ids_hbm, ids, small_sem.at[0]),
        pltpu.make_async_copy(units_hbm, units_v, small_sem.at[1]),
        pltpu.make_async_copy(units_hbm, units_s, small_sem.at[2]),
        pltpu.make_async_copy(lengths_hbm, lengths, small_sem.at[3]),
    ]
    load_pages = pltpu.make_async_copy(pages_hbm, unsorted, small_sem.at[4])
    load_hidden = pltpu.make_async_copy(hidden_hbm, hidden_in, small_sem.at[5])
    loads = [
        pltpu.make_async_copy(qkv_hbm.at[pl.ds(c * HD, HD)], qkv_w.at[c], load_sem.at[c])
        for c in range(heads)
    ]
    loads += [
        pltpu.make_async_copy(
            out_hbm.at[pl.ds(c * HD, HD)], out_w.at[c], load_sem.at[heads + c]
        )
        for c in range(tiles)
    ]
    for load in small + [load_pages]:
        load.start()

    barrier = pltpu.get_barrier_semaphore()

    @pl.loop(1, devices)
    def _(offset):
        pl.semaphore_signal(
            barrier, inc=1, device_id={"tp": lax.rem(me + offset, devices)}, device_id_type=pl.DeviceIdType.MESH
        )

    def numbers(shape, axis):
        return lax.broadcasted_iota(jnp.int32, shape, axis)

    def whole(values, size):
        return lax.shift_right_logical(values, jnp.full_like(values, size.bit_length() - 1))

    def index_row(values, size):
        return jnp.clip(values, 0, size - 1)

    def down(hit, values):
        return jnp.sum(jnp.where(hit, values, 0), axis=0, keepdims=True)

    def across(hit, values):
        return jnp.sum(jnp.where(hit, values, 0), axis=1, keepdims=True)

    square = (pages_dev, pages_dev)
    k_sub, k_lane = numbers(square, 0), numbers(square, 1)
    small[0].wait()
    first = me * pages_dev
    wide = (pages_dev, ids.shape[1])
    own_ids = ids[pl.ds(first // ids.shape[1], 1), :]
    mine = numbers(wide, 1) == numbers(wide, 0) + lax.rem(first, ids.shape[1])
    id_col = across(mine, own_ids)
    small[1].wait()
    unit_row = units_v[...]
    by_unit = (pages_dev, units)
    slot_col = across(whole(id_col, per_unit) == unit_row, numbers(by_unit, 1))
    target_col = whole(slot_col, U_DEV)
    target_row = down(k_sub == k_lane, target_col)
    rank_col = across((target_col == target_row) & (k_lane < k_sub), jnp.ones(square, jnp.int32))
    sent = target_col * capacity + rank_col == k_lane
    tables_v[in_order : in_order + 1, :] = index_row(down(sent, k_sub), pages_dev)
    id_row = down(sent, id_col)
    tables_v[of_target : of_target + 1, :] = down(sent, slot_col - target_col * U_DEV)
    sent_unit = whole(id_row, per_unit)
    sent_request = whole(sent_unit, KVH)
    small[3].wait()
    sent_length = jnp.zeros_like(id_row)
    for r in range(requests):
        sent_length = jnp.where(sent_request == r, lengths[0, r], sent_length)
    tables_v[of_query : of_query + 1, :] = index_row(
        (sent_unit - sent_request * KVH) * requests + sent_request, units
    )
    tables_v[of_left : of_left + 1, :] = sent_length - (id_row - sent_unit * per_unit) * PAGE
    u_square = (units, units)
    u_sub, u_lane = numbers(u_square, 0), numbers(u_square, 1)
    unit_col = across(u_sub == u_lane, unit_row)
    u_device = whole(u_sub, U_DEV)
    u_side = whole(u_device, half)
    u_place = (u_device - u_side * half) * (2 * U_DEV) + u_side * U_DEV + (u_sub - u_device * U_DEV)
    tables_v[of_slot : of_slot + 1, :] = index_row(down(unit_col == u_lane, u_place), units)
    to_table = pltpu.make_async_copy(tables_v, table, table_sem.at[0])
    to_table.start()

    load_pages.wait()
    for load in [load_hidden] + loads[:heads]:
        load.start()
    to_table.wait()

    def sort_page(at):
        pages[at] = unsorted[table[in_order, at]]

    def sort_turns(start, stop):
        @pl.loop(start, stop)
        def _(turn):
            rank, place = turn // half, lax.rem(turn, half)
            sort_page(far(place) * capacity + rank)
            sort_page(near(place) * capacity + rank)

    sort_turns(0, share(PLAN[0]))
    pl.semaphore_wait(barrier, devices - 1)
    send_pages(0, share(PLAN[0]))
    sort_turns(share(PLAN[0]), turns)

    small[2].wait()
    row_at = lax.broadcasted_iota(jnp.int32, (rows, HD), 0)
    lane_at = lax.broadcasted_iota(jnp.int32, (rows, HD), 1)
    positions = jnp.zeros((rows, HD), jnp.float32)
    for r in range(requests):
        positions = jnp.where(row_at // 2 == r, lengths[0, r].astype(jnp.float32), positions)
    positions = positions + (row_at % 2).astype(jnp.float32)
    power = (lane_at % (HD // 2)).astype(jnp.float32) * (2.0 / HD)
    angles = positions * jnp.exp(power * -math.log(rope_base))
    cos_ref[...] = jnp.cos(angles)
    sin_ref[...] = jnp.where(lane_at < HD // 2, -jnp.sin(angles), jnp.sin(angles))
    load_hidden.wait()
    for r in range(requests):
        hidden_wide[2 * r : 2 * r + 2, :] = hidden_in[r].astype(jnp.float32)
    hidden_ref[...] = hidden_wide[...].astype(jnp.bfloat16)

    for c in range(heads):
        loads[c].wait()
        part = lax.dot_general(
            hidden_ref[...], qkv_w[c], NT, preferred_element_type=jnp.float32
        ).astype(jnp.bfloat16).astype(jnp.float32)
        turned = part * cos_ref[...] + pltpu.roll(part, HD // 2, 1) * sin_ref[...]
        is_value = lax.rem(me * heads + c, head_rows) == head_rows - 1
        rows_all[me, c] = jnp.where(is_value, part, turned).astype(jnp.bfloat16)

    row_copy(0, me, partner).start()

    @pl.loop(1, half)
    def _(offset):
        row_copy(1, me, near(offset)).start()

    send_pages(share(PLAN[0]), share(PLAN[1]))
    for load in loads[heads:]:
        load.start()
    own_pages = pltpu.make_async_copy(
        pages.at[pl.ds(me * capacity, capacity)],
        arrived_hbm.at[pl.ds(me * capacity, capacity)],
        page_recv,
    )
    own_pages.start()

    row_copy(0, partner, partner).wait_recv()

    @pl.loop(1, half)
    def _(offset):
        row_copy(1, partner, near(offset)).start()

    send_pages(share(PLAN[1]), share(PLAN[2]))

    many_rows(devices - 2).wait_recv()

    for h in range(KVH):
        for g in range(group_count):
            at = h * head_rows + g
            spread[pl.ds(h * span + g, rows, stride=group_count), :] = rows_all[
                at // heads, at % heads
            ].astype(jnp.float32)
        at = h * head_rows + group_count
        new_keys[h] = rows_all[at // heads, at % heads]
        new_values[h] = rows_all[(at + 1) // heads, (at + 1) % heads]
        for r in range(requests):
            start = h * span + r * 2 * group_count
            queries[h * requests + r] = spread[start : start + 2 * group_count, :].astype(
                jnp.bfloat16
            )

    @pl.loop(0, devices)
    def _(target):
        spent = share(PLAN[3]) - share(PLAN[2])
        send_pages(
            share(PLAN[2]) + target * spent // devices,
            share(PLAN[2]) + (target + 1) * spent // devices,
        )
        zero = jnp.zeros((2 * group_count, PAGE), jnp.float32)
        sums, totals = [zero] * U_DEV, [zero[:, :1]] * U_DEV
        for rank in range(capacity):
            query = queries[table[of_query, target * capacity + rank]]
            left = table[of_left, target * capacity + rank]
            page = pages[target * capacity + rank]
            scores = lax.dot_general(
                query, page[:, :HD], NT, preferred_element_type=jnp.float32
            ) * score_scale
            weights = jnp.where(lane < left, jnp.exp(scores), 0.0)
            total = jnp.sum(weights, axis=-1, keepdims=True)
            weighted = jnp.dot(
                weights.astype(jnp.bfloat16), page[:, HD:], preferred_element_type=jnp.float32
            )
            slot = table[of_target, target * capacity + rank]
            for j in range(U_DEV):
                sums[j] = sums[j] + jnp.where(slot == j, weighted, 0.0)
                totals[j] = totals[j] + jnp.where(slot == j, total, 0.0)
        place, which = lax.rem(target, half), target // half
        for j in range(U_DEV):
            part_out[place, which, j] = sums[j].astype(jnp.bfloat16)
        part_out[place, which, U_DEV] = pack_totals(totals)

    @pl.loop(1, half)
    def _(offset):
        part_copy(lax.rem(here + offset, half), here, near(offset)).start()

    own_sums, own_totals = [], []
    row = lax.broadcasted_iota(jnp.int32, (2 * group_count, rows), 0)
    col = lax.broadcasted_iota(jnp.int32, (2 * group_count, rows), 1)
    line = lax.broadcasted_iota(jnp.int32, (rows, HD), 0)
    for j in range(2 * U_DEV):
        unit = units_s[0, (j // U_DEV * half + here) * U_DEV + j % U_DEV]
        request, head = unit // KVH, unit % KVH
        scores = lax.dot_general(
            queries[head * requests + request], new_keys[head], NT, preferred_element_type=jnp.float32
        ) * score_scale
        seen = (col // 2 == request) & (col % 2 <= row // group_count)
        weights = jnp.where(seen, jnp.exp(scores), 0.0)
        own_totals.append(jnp.sum(weights, axis=-1, keepdims=True))
        own_sums.append(
            jnp.dot(weights.astype(jnp.bfloat16), new_values[head], preferred_element_type=jnp.float32)
        )
    for j in range(U_DEV):
        unit = units_s[0, me * U_DEV + j]
        request, head = unit // KVH, unit % KVH
        for step in range(2):
            mine = line == request * 2 + step
            for part, kind in ((0, new_keys[head]), (1, new_values[head])):
                fresh_ref[j, step : step + 1, part * HD : (part + 1) * HD] = jnp.sum(
                    jnp.where(mine, kind.astype(jnp.float32), 0.0), axis=0, keepdims=True
                )

    slot_at = numbers((pages_dev, 1), 0)
    wanted = jnp.zeros((pages_dev, 1), jnp.int32)
    for j in range(U_DEV):
        first_page = units_s[0, me * U_DEV + j] * per_unit - j * per_unit
        wanted = jnp.where(whole(slot_at, per_unit) == j, slot_at + first_page, wanted)
    found = jnp.zeros(wide, jnp.int32)
    for b in range(ids.shape[0]):
        found = found + jnp.where(
            wanted == ids[b : b + 1, :], numbers(wide, 1) + b * wide[1], 0
        )
    source_col = jnp.sum(found, axis=1, keepdims=True)
    source_row = down(k_sub == k_lane, source_col)
    holder_col, holder_row = whole(source_col, pages_dev), whole(source_row, pages_dev)
    rank_col = across(
        (holder_col == holder_row) & (source_row < source_col), jnp.ones(square, jnp.int32)
    )
    place_ref[0:1, :] = index_row(
        down(k_sub == k_lane, holder_col * capacity + rank_col), pages_dev
    )
    own_lengths = jnp.zeros((1, pages_dev), jnp.int32)
    for j in range(U_DEV):
        own_lengths = jnp.where(
            lax.broadcasted_iota(jnp.int32, (1, pages_dev), 1) == j,
            lengths[0, units_s[0, me * U_DEV + j] // KVH], own_lengths,
        )
    place_ref[1:2, :] = own_lengths

    many_parts(half - 1).wait_recv()

    def half_sum(which):
        def add(offset, carry):
            block = part_in.at[lax.rem(here + offset, half), which]
            return tuple(c + block[j].astype(jnp.float32) for j, c in enumerate(carry))

        first = tuple(
            part_out[here, which, j].astype(jnp.float32) for j in range(U_DEV + 1)
        )
        return lax.fori_loop(1, half, add, first)

    kept = half_sum(0) + half_sum(1)
    blocks = U_DEV + 1
    for which in range(2):
        for j in range(U_DEV):
            swap_out[which * blocks + j] = kept[which * blocks + j].astype(jnp.bfloat16)
        packed = kept[which * blocks + U_DEV]
        swap_out[which * blocks + U_DEV] = pack_totals(
            [unpack_total(packed, j) for j in range(U_DEV)]
        )
    swap_copy().start()
    send_pages(share(PLAN[3]), share(PLAN[4]))
    swap_copy().wait_recv()
    for which in range(2):
        last = which * blocks + U_DEV
        packed = kept[last] + swap_in[last].astype(jnp.float32)
        for j in range(U_DEV):
            at = which * blocks + j
            total = own_totals[which * U_DEV + j] + unpack_total(packed, j)
            weighted = own_sums[which * U_DEV + j] + kept[at] + swap_in[at].astype(jnp.float32)
            att_all[here, which * U_DEV + j] = (weighted / total).astype(jnp.bfloat16)

    @pl.loop(1, half)
    def _(offset):
        att_copy(near(offset)).start()

    send_pages(share(PLAN[4]), turns)
    many_att(half - 1).wait_recv()

    for r in range(requests):
        for h in range(KVH):
            slot = table[of_slot, r * KVH + h]
            spread[h * span + r * 2 * group_count : h * span + (r + 1) * 2 * group_count, :] = (
                att_all[slot // (2 * U_DEV), slot % (2 * U_DEV)].astype(jnp.float32)
            )
    for h in range(KVH):
        for g in range(group_count):
            at = (h * group_count + g) * HD
            flat[:, at : at + HD] = spread[
                pl.ds(h * span + g, rows, stride=group_count), :
            ].astype(jnp.bfloat16)
    for c in range(tiles):
        loads[heads + c].wait()
        mixed_ref[:, c * HD : (c + 1) * HD] = lax.dot_general(
            flat[...], out_w[c], NT, preferred_element_type=jnp.float32
        ).astype(jnp.bfloat16)

    results = [
        pltpu.make_async_copy(src, dst, result_sem.at[i])
        for i, (src, dst) in enumerate(
            ((mixed_ref, mixed_hbm), (fresh_ref, fresh_hbm), (place_ref, place_hbm))
        )
    ]
    for result in results:
        result.start()
    for result in results:
        result.wait()
    remote(arrived_hbm, arrived_hbm, page_send, page_recv, partner).wait_recv()
    sent_pages = pages.at[pl.ds(0, (devices - 1) * capacity)]
    remote(sent_pages, sent_pages, page_send, page_recv, partner).wait_send()
    many_rows(devices - 1).wait_send()
    many_parts(half - 1).wait_send()
    swap_copy().wait_send()
    many_att(half - 1).wait_send()


def fused_body(hidden_states, qkv_weight, out_weight, cache_pages, context_lengths, new_units, old_pages):
    devices = lax.axis_size("tp")
    requests = hidden_states.shape[0]
    rows = requests * 2
    pages_dev = cache_pages.shape[0]
    capacity = pages_dev // devices
    heads = qkv_weight.shape[0] // HD
    tiles = out_weight.shape[0] // HD
    group_count = HEADS // KVH
    units = new_units.shape[0]
    hbm = pl.BlockSpec(memory_space=pl.ANY)
    vmem = pl.BlockSpec(memory_space=pltpu.VMEM)
    smem = pl.BlockSpec(memory_space=pltpu.SMEM)
    dma = pltpu.SemaphoreType.DMA
    lengths = context_lengths.reshape(1, requests)
    unit_table = new_units.reshape(1, units)
    page_table = old_pages.reshape(-1, PAGE)
    tile = (2 * group_count, HD)
    f32, bf16, i32 = jnp.float32, jnp.bfloat16, jnp.int32
    arrived, mixed, fresh, place = pl.pallas_call(
        lambda *refs: layer_kernel(devices, capacity, *refs),
        out_shape=(
            jax.ShapeDtypeStruct(cache_pages.shape, bf16),
            jax.ShapeDtypeStruct((rows, out_weight.shape[0]), bf16),
            jax.ShapeDtypeStruct((U_DEV, 2, 2 * HD), f32),
            jax.ShapeDtypeStruct((2, pages_dev), i32),
        ),
        in_specs=[pl.BlockSpec(memory_space=pltpu.HBM)] * 7,
        out_specs=(hbm, hbm, hbm, hbm),
        scratch_shapes=[
            pltpu.SMEM(lengths.shape, i32),
            pltpu.SMEM(unit_table.shape, i32),
            pltpu.VMEM(unit_table.shape, i32),
            pltpu.VMEM(page_table.shape, i32),
            pltpu.VMEM((8, pages_dev), i32),
            pltpu.SMEM((8, pages_dev), i32),
            pltpu.VMEM(hidden_states.shape, bf16),
            pltpu.VMEM((rows, D), f32),
            pltpu.VMEM((rows, D), bf16),
            pltpu.VMEM((rows, HD), f32),
            pltpu.VMEM((rows, HD), f32),
            pltpu.VMEM((heads, HD, D), bf16),
            pltpu.VMEM((tiles, HD, HEADS * HD), bf16),
            pltpu.VMEM(cache_pages.shape, bf16),
            pltpu.VMEM(cache_pages.shape, bf16),
            pltpu.VMEM((devices, heads, rows, HD), bf16),
            pltpu.VMEM((units * 2 * group_count, HD), f32),
            pltpu.VMEM((units,) + tile, bf16),
            pltpu.VMEM((KVH, rows, HD), bf16),
            pltpu.VMEM((KVH, rows, HD), bf16),
            pltpu.VMEM((devices // 2, 2, U_DEV + 1) + tile, bf16),
            pltpu.VMEM((devices // 2, 2, U_DEV + 1) + tile, bf16),
            pltpu.VMEM((2 * (U_DEV + 1),) + tile, bf16),
            pltpu.VMEM((2 * (U_DEV + 1),) + tile, bf16),
            pltpu.VMEM((devices // 2, 2 * U_DEV) + tile, bf16),
            pltpu.VMEM((rows, HEADS * HD), bf16),
            dma((heads + tiles,)),
            dma(()), dma(()),
            dma(()), dma((2,)),
            dma(()), dma(()), dma(()), dma(()),
            dma(()), dma(()),
            dma((6,)), dma((1,)),
            pltpu.VMEM((rows, out_weight.shape[0]), bf16),
            pltpu.VMEM((U_DEV, 2, 2 * HD), f32),
            pltpu.VMEM((2, pages_dev), i32),
            dma((3,)),
        ],
        compiler_params=pltpu.CompilerParams(
            collective_id=0, has_side_effects=True, vmem_limit_bytes=44 << 20
        ),
        name="layer",
    )(*[pltpu.with_memory_space_constraint(x, pltpu.HBM) for x in (lengths, unit_table, page_table, hidden_states, qkv_weight, out_weight, cache_pages)])
    mixed_shape = (requests, 2, out_weight.shape[0])
    placed, mixed = pl.pallas_call(
        place_kernel,
        out_shape=(
            jax.ShapeDtypeStruct(cache_pages.shape, bf16),
            jax.ShapeDtypeStruct(mixed_shape, bf16),
        ),
        in_specs=[smem, vmem, vmem, vmem],
        out_specs=(hbm, hbm),
        scratch_shapes=[
            pltpu.VMEM((U_DEV, 2) + cache_pages.shape[1:], bf16),
            pltpu.VMEM(mixed_shape, bf16),
            dma(()), dma(()),
        ],
        compiler_params=pltpu.CompilerParams(vmem_limit_bytes=8 << 20),
        name="place_pages",
    )(place, arrived, fresh, mixed)
    return (mixed, placed)


def body(hidden_states, qkv_weight, out_weight, cache_pages, context_lengths, new_units, old_pages):
    devices = lax.axis_size("tp")
    whole_heads = qkv_weight.shape[0] % HD == 0 and out_weight.shape[0] % HD == 0
    pages_dev = cache_pages.shape[0]
    whole_shares = pages_dev % devices == 0 and devices % 4 == 0 and hidden_states.shape[0] == KVH
    whole_shares = whole_shares and new_units.shape[0] == pages_dev and PAGE % pages_dev == 0
    chosen = fused_body if whole_heads and whole_shares else plain_body
    return chosen(
        hidden_states, qkv_weight, out_weight, cache_pages, context_lengths, new_units, old_pages
    )


def solution(mesh):
    in_specs = (
        P("group", None, None),
        P("tp", None),
        P("tp", None),
        P(("group", "tp"), None, None),
        P("group"),
        P("group"),
        P("group"),
    )
    out_specs = (P("group", None, "tp"), P(("group", "tp"), None, None))
    return jax.shard_map(body, mesh=mesh, in_specs=in_specs, out_specs=out_specs, check_vma=False)
```

```python
import math

import jax
import jax.numpy as jnp
from jax import lax
from jax.experimental import pallas as pl
from jax.experimental.pallas import tpu as pltpu
from jax.sharding import PartitionSpec as P

D = 8192
HEADS = 64
KVH = 8
HD = 128
U_DEV = 4
MAXCTX = 2048
PAGE = 128


rope_base = 10000.0


def rotate_positions(values, positions):
    half_dim = values.shape[-1] // 2
    frequency = rope_base ** (-(jnp.arange(half_dim, dtype=jnp.float32) * 2.0 / values.shape[-1]))
    angles = positions.astype(jnp.float32)[..., None] * frequency
    cosine = jnp.concatenate([jnp.cos(angles), jnp.cos(angles)], axis=-1)
    sine_table = jnp.concatenate([jnp.sin(angles), jnp.sin(angles)], axis=-1)
    turned = jnp.concatenate([-values[..., half_dim:], values[..., :half_dim]], axis=-1)
    return values * cosine + turned * sine_table


def prepare(unit_qkv, base_lengths):
    group_count = HEADS // KVH
    count_units = unit_qkv.shape[0]
    positions = base_lengths[:, None] + jnp.arange(2, dtype=jnp.int32)[None, :]
    widened = unit_qkv.astype(jnp.float32)
    queries = widened[..., : group_count * HD].reshape(count_units, 2, group_count, HD)
    queries = rotate_positions(queries, positions[:, :, None]).astype(jnp.bfloat16)
    new_keys = rotate_positions(
        widened[..., group_count * HD : (group_count + 1) * HD], positions
    ).astype(jnp.bfloat16)
    new_values = unit_qkv[..., (group_count + 1) * HD :]
    return (queries, new_keys, new_values)


def context_terms(context, queries, valid_count):
    score_scale = 1.0 / math.sqrt(HD)
    cached_keys = context[..., :HD]
    cached_values = context[..., HD:]
    scores = (
        jnp.einsum("psgd,ptd->psgt", queries, cached_keys, preferred_element_type=jnp.float32)
        * score_scale
    )
    visible = jnp.arange(context.shape[1], dtype=jnp.int32)[None, :] < valid_count[:, None]
    weights = jnp.where(visible[:, None, None, :], jnp.exp(scores), 0.0)
    totals = jnp.sum(weights, axis=-1)
    weighted = jnp.einsum(
        "psgt,ptd->psgd",
        weights.astype(jnp.bfloat16),
        cached_values,
        preferred_element_type=jnp.float32,
    )
    return (weighted, totals)


def own_terms(queries, new_keys, new_values):
    score_scale = 1.0 / math.sqrt(HD)
    scores = (
        jnp.einsum("usgd,ujd->usgj", queries, new_keys, preferred_element_type=jnp.float32)
        * score_scale
    )
    recent = jnp.arange(2, dtype=jnp.int32)[None, :] <= jnp.arange(2, dtype=jnp.int32)[:, None]
    weights = jnp.where(recent[None, :, None, :], jnp.exp(scores), 0.0)
    totals = jnp.sum(weights, axis=-1)
    weighted = jnp.einsum(
        "usgj,ujd->usgd",
        weights.astype(jnp.bfloat16),
        new_values,
        preferred_element_type=jnp.float32,
    )
    return (weighted, totals)


def plain_body(hidden_states, qkv_weight, out_weight, cache_pages, context_lengths, new_units, old_pages):
    devices = lax.axis_size("tp")
    device = lax.axis_index("tp")
    requests = hidden_states.shape[0]
    rows_dev = qkv_weight.shape[0]
    pages_dev, page_rows, page_width = cache_pages.shape
    group_count = HEADS // KVH
    unit_rows = (group_count + 2) * HD
    per_unit = MAXCTX // PAGE
    unit_slots = U_DEV
    capacity = max(1, pages_dev // devices)
    total_units = new_units.shape[0]
    total_pages = old_pages.shape[0]
    flat_rows = hidden_states.reshape(requests * 2, D)
    partial_qkv = lax.dot_general(
        flat_rows, qkv_weight, (((1,), (1,)), ((), ())), preferred_element_type=jnp.float32
    )
    partial_qkv = partial_qkv.astype(jnp.bfloat16).reshape(requests, 2, rows_dev)
    slot_index = (
        jnp.zeros((total_units,), jnp.int32)
        .at[new_units]
        .set(jnp.arange(total_units, dtype=jnp.int32))
    )
    own_units = lax.dynamic_slice_in_dim(new_units, device * unit_slots, unit_slots)
    own_requests = own_units // KVH
    own_heads = own_units % KVH
    own_lengths = context_lengths[own_requests]
    local_ids = lax.dynamic_slice_in_dim(old_pages, device * pages_dev, pages_dev)
    local_units = local_ids // per_unit
    local_index = local_ids % per_unit
    target_dev = (slot_index[local_units] * per_unit + local_index) // pages_dev
    local_order = jnp.arange(pages_dev, dtype=jnp.int32)
    send_rank = jnp.sum(
        (
            (target_dev[:, None] == target_dev[None, :])
            & (local_order[None, :] < local_order[:, None])
        ).astype(jnp.int32),
        axis=1,
    )
    outgoing = (
        jnp.zeros((devices, capacity, page_rows, page_width), jnp.bfloat16)
        .at[target_dev, send_rank]
        .set(cache_pages)
    )
    arrived = lax.all_to_all(outgoing, "tp", split_axis=0, concat_axis=0, tiled=True)
    stored_position = (
        jnp.zeros((total_pages,), jnp.int32)
        .at[old_pages]
        .set(jnp.arange(total_pages, dtype=jnp.int32))
    )
    wanted = (
        own_units[:, None] * per_unit + jnp.arange(per_unit, dtype=jnp.int32)[None, :]
    ).reshape(pages_dev)
    source_pos = stored_position[wanted]
    source_dev = source_pos // pages_dev
    source_slot = source_pos % pages_dev
    arrival_rank = jnp.sum(
        (
            (source_dev[:, None] == source_dev[None, :])
            & (source_slot[None, :] < source_slot[:, None])
        ).astype(jnp.int32),
        axis=1,
    )
    relaid = arrived[source_dev, arrival_rank]
    contexts = relaid.reshape(unit_slots, MAXCTX, page_width)
    sources_per_head = unit_rows // rows_dev
    request_table = (new_units // KVH).reshape(devices, unit_slots)
    outgoing_rows = partial_qkv[request_table]
    incoming = lax.all_to_all(outgoing_rows, "tp", split_axis=0, concat_axis=0, tiled=True)
    grouped = jnp.moveaxis(incoming.reshape(KVH, sources_per_head, unit_slots, 2, rows_dev), 2, 0)
    chosen = jnp.take_along_axis(grouped, own_heads[:, None, None, None, None], axis=1)[:, 0]
    own_rows = chosen.transpose(0, 2, 1, 3).reshape(unit_slots, 2, unit_rows)
    queries, new_keys, new_values = prepare(own_rows, own_lengths)
    cache_sums, cache_totals = context_terms(contexts, queries, own_lengths)
    own_sums, own_totals = own_terms(queries, new_keys, new_values)
    attended = ((cache_sums + own_sums) / (cache_totals + own_totals)[..., None]).astype(
        jnp.bfloat16
    )
    attended = attended.reshape(unit_slots, 2, group_count * HD)
    all_heads = lax.all_gather(attended, "tp", axis=0, tiled=True)
    logical = (
        all_heads[slot_index]
        .reshape(requests, KVH, 2, group_count * HD)
        .transpose(0, 2, 1, 3)
        .reshape(requests * 2, HEADS * HD)
    )
    mixed_rows = lax.dot_general(
        logical, out_weight, (((1,), (1,)), ((), ())), preferred_element_type=jnp.float32
    )
    mixed_rows = mixed_rows.astype(jnp.bfloat16).reshape(requests, 2, out_weight.shape[0])
    fresh_rows = jnp.concatenate([new_keys, new_values], axis=-1)
    positions = jnp.arange(MAXCTX, dtype=jnp.int32)[None, :]
    contexts = jnp.where(
        (positions == own_lengths[:, None])[..., None], fresh_rows[:, 0:1], contexts
    )
    contexts = jnp.where(
        (positions == own_lengths[:, None] + 1)[..., None], fresh_rows[:, 1:2], contexts
    )
    return (mixed_rows, contexts.reshape(pages_dev, page_rows, page_width))


def place_kernel(
    table_ref, arrived_ref, fresh_ref, mixed_ref, out_ref, rows_ref, patched, rows, sem, rows_sem
):
    per_unit = MAXCTX // PAGE
    steps = fresh_ref.shape[1]

    def outward(at, src):
        return pltpu.make_async_copy(src, out_ref.at[at], sem)

    def place_of(slot, page):
        return slot * per_unit + lax.rem(table_ref[1, slot] // PAGE + page, per_unit)

    for slot in range(U_DEV):
        for page in range(steps, per_unit):
            at = place_of(slot, page)
            outward(at, arrived_ref.at[table_ref[0, at]]).start()

    for slot in range(U_DEV):
        for page in range(steps):
            at = place_of(slot, page)
            block = patched.at[slot, page]
            block[...] = arrived_ref[table_ref[0, at]]
            for step in range(steps):
                row = table_ref[1, slot] + step - (at - slot * per_unit) * PAGE

                @pl.when((row >= 0) & (row < PAGE))
                def _():
                    base = pl.multiple_of((row // 16) * 16, 16)
                    tile = block[pl.ds(base, 16), :]
                    line = lax.broadcasted_iota(jnp.int32, tile.shape, 0)
                    new = jnp.broadcast_to(fresh_ref[slot, step : step + 1, :], tile.shape)
                    mixed = jnp.where(line == row - base, new, tile.astype(jnp.float32))
                    block[pl.ds(base, 16), :] = mixed.astype(jnp.bfloat16)

            outward(at, block).start()

    mixed = mixed_ref[...].astype(jnp.float32)
    for r in range(rows.shape[0]):
        rows[r] = mixed[2 * r : 2 * r + 2].astype(jnp.bfloat16)
    rows_out = pltpu.make_async_copy(rows, rows_ref, rows_sem)
    rows_out.start()
    pltpu.make_async_copy(arrived_ref, out_ref, sem).wait()
    rows_out.wait()


NT = (((1,), (1,)), ((), ()))
PLAN = (8,12,16,22,28)
FIRST = 32


def layer_kernel(
    devices, capacity,
    lengths_hbm, units_hbm, ids_hbm, hidden_hbm, qkv_hbm, out_hbm, pages_hbm,
    arrived_hbm, mixed_hbm, fresh_hbm, place_hbm,
    lengths, units_s, units_v, ids, order_v, order, tables_v, table, hidden_in, hidden_wide, hidden_ref, cos_ref, sin_ref,
    qkv_w, out_w, unsorted_head, unsorted_tail, pages, rows_all, spread, queries, new_keys, new_values, part_out, part_in, swap_out, swap_in, att_all, flat,
    load_sem, page_send, page_recv, row_send, row_recv, part_send, part_recv, swap_send, swap_recv, att_send, att_recv,
    small_sem, table_sem, settled, mixed_ref, fresh_ref, place_ref, result_sem,
):
    me = lax.axis_index("tp")
    pages_dev = pages.shape[0]
    rows = hidden_ref.shape[0]
    requests = rows // 2
    units = requests * KVH
    per_unit = MAXCTX // PAGE
    heads = qkv_w.shape[0]
    tiles = out_w.shape[0]
    group_count = HEADS // KVH
    head_rows = group_count + 2
    score_scale = 1.0 / math.sqrt(HD)
    span = requests * 2 * group_count
    of_query, of_left, of_target, of_slot = range(4)

    half, quarter = devices // 2, devices // 4
    here, side = lax.rem(me, half), me // half
    partner = lax.rem(me + half, devices)

    def near(offset):
        return side * half + lax.rem(here + offset, half)

    def far(turn):
        return (1 - side) * half + (turn // quarter) * quarter + lax.rem(turn + me, quarter)

    def remote(src, dst, send, recv, device):
        return pltpu.make_async_remote_copy(
            src_ref=src, dst_ref=dst, send_sem=send, recv_sem=recv,
            device_id={"tp": device}, device_id_type=pl.DeviceIdType.MESH,
        )

    def page_copy(rank, device, start=0, size=PAGE):
        return remote(
            pages.at[device * capacity + rank, pl.ds(start, size)],
            arrived_hbm.at[me * capacity + rank, pl.ds(start, size)],
            page_send, page_recv, device,
        )

    def row_copy(kind, owner, device):
        block = rows_all.at[owner]
        return remote(block, block, row_send, row_recv.at[kind], device)

    def many_rows(count):
        blocks = rows_all.at[pl.ds(0, count)]
        return remote(blocks, blocks, row_send, row_recv.at[1], partner)

    def att_copy(device):
        block = att_all.at[here]
        return remote(block, block, att_send, att_recv, device)

    def many_att(count):
        blocks = att_all.at[pl.ds(0, count)]
        return remote(blocks, blocks, att_send, att_recv, partner)

    def part_copy(src, dst, device):
        return remote(part_out.at[src], part_in.at[dst], part_send, part_recv, device)

    def many_parts(count):
        return remote(
            part_out.at[pl.ds(0, count)], part_in.at[pl.ds(0, count)], part_send, part_recv, partner
        )

    def swap_copy():
        return remote(swap_out, swap_in, swap_send, swap_recv, partner)

    turns = half * capacity

    def turn_of(turn):
        rank, place = turn // half, lax.rem(turn, half)
        if capacity == 1:
            return rank, place
        head = turn < 2 * half
        rank = jnp.where(head, lax.rem(turn // quarter, 2), rank)
        return rank, jnp.where(head, turn // half * quarter + lax.rem(turn, quarter), place)

    def send_far(start, stop, *part):
        @pl.loop(start, stop)
        def _(turn):
            rank, place = turn_of(turn)
            page_copy(rank, far(place), *part).start()

    def send_near(start, stop):
        @pl.loop(start, stop)
        def _(turn):
            rank, place = turn_of(turn)

            @pl.when(place > 0)
            def _():
                page_copy(rank, near(place)).start()

    def send_pages(start, stop):
        @pl.loop(start, stop)
        def _(turn):
            send_far(turn, turn + 1)
            send_near(turn, turn + 1)

    def share(numerator):
        return turns * numerator // 32

    def pack_totals(values):
        packed = jnp.zeros((2 * group_count, PAGE), jnp.float32)
        for j, total in enumerate(values):
            top = total.astype(jnp.bfloat16).astype(jnp.float32)
            packed = jnp.where(lane == j * strip, top, packed)
            packed = jnp.where(lane == j * strip + strip // 2, total - top, packed)
        return packed.astype(jnp.bfloat16)

    def unpack_total(packed, j):
        return jnp.sum(jnp.where(lane // strip == j, packed, 0.0), axis=-1, keepdims=True)

    lane = lax.broadcasted_iota(jnp.int32, (2 * group_count, PAGE), 1)
    strip = PAGE // U_DEV

    small = [
        pltpu.make_async_copy(ids_hbm, ids, small_sem.at[0]),
        pltpu.make_async_copy(units_hbm, units_v, small_sem.at[1]),
        pltpu.make_async_copy(units_hbm, units_s, small_sem.at[2]),
        pltpu.make_async_copy(lengths_hbm, lengths, small_sem.at[3]),
    ]
    load_pages = [
        pltpu.make_async_copy(
            pages_hbm.at[:, pl.ds(start, part.shape[1])], part, small_sem.at[sem]
        )
        for start, part, sem in ((0, unsorted_head, 4), (FIRST, unsorted_tail, 6))
    ]
    load_hidden = pltpu.make_async_copy(hidden_hbm, hidden_in, small_sem.at[5])
    loads = [
        pltpu.make_async_copy(qkv_hbm.at[pl.ds(c * HD, HD)], qkv_w.at[c], load_sem.at[c])
        for c in range(heads)
    ]
    loads += [
        pltpu.make_async_copy(
            out_hbm.at[pl.ds(c * HD, HD)], out_w.at[c], load_sem.at[heads + c]
        )
        for c in range(tiles)
    ]
    for load in small + load_pages:
        load.start()

    barrier = pltpu.get_barrier_semaphore()

    def greet(semaphore, device):
        pl.semaphore_signal(
            semaphore, inc=1, device_id={"tp": device}, device_id_type=pl.DeviceIdType.MESH
        )

    @pl.when(side == 0)
    def _():
        @pl.loop(half, devices)
        def _(device):
            greet(barrier, device)

    @pl.when(me // quarter == 2)
    def _():
        @pl.loop(0, half)
        def _(device):
            greet(barrier, device)

    def numbers(shape, axis):
        return lax.broadcasted_iota(jnp.int32, shape, axis)

    def whole(values, size):
        return lax.shift_right_logical(values, jnp.full_like(values, size.bit_length() - 1))

    def index_row(values, size):
        return jnp.clip(values, 0, size - 1)

    def down(hit, values):
        return jnp.sum(jnp.where(hit, values, 0), axis=0, keepdims=True)

    def across(hit, values):
        return jnp.sum(jnp.where(hit, values, 0), axis=1, keepdims=True)

    square = (pages_dev, pages_dev)
    k_sub, k_lane = numbers(square, 0), numbers(square, 1)
    small[0].wait()
    first = me * pages_dev
    wide = (pages_dev, ids.shape[1])
    own_ids = ids[pl.ds(first // ids.shape[1], 1), :]
    mine = numbers(wide, 1) == numbers(wide, 0) + lax.rem(first, ids.shape[1])
    id_col = across(mine, own_ids)
    small[1].wait()
    unit_row = units_v[...]
    by_unit = (pages_dev, units)
    slot_col = across(whole(id_col, per_unit) == unit_row, numbers(by_unit, 1))
    target_col = whole(slot_col, U_DEV)
    target_row = down(k_sub == k_lane, target_col)
    rank_col = across((target_col == target_row) & (k_lane < k_sub), jnp.ones(square, jnp.int32))
    sent = target_col * capacity + rank_col == k_lane
    order_v[...] = index_row(down(sent, k_sub), pages_dev)
    to_order = pltpu.make_async_copy(order_v, order, table_sem.at[1])
    to_order.start()
    id_row = down(sent, id_col)
    tables_v[of_target : of_target + 1, :] = down(sent, slot_col - target_col * U_DEV)
    sent_unit = whole(id_row, per_unit)
    sent_request = whole(sent_unit, KVH)
    small[3].wait()
    sent_length = jnp.zeros_like(id_row)
    for r in range(requests):
        sent_length = jnp.where(sent_request == r, lengths[0, r], sent_length)
    tables_v[of_query : of_query + 1, :] = index_row(
        (sent_unit - sent_request * KVH) * requests + sent_request, units
    )
    tables_v[of_left : of_left + 1, :] = sent_length - (id_row - sent_unit * per_unit) * PAGE
    u_square = (units, units)
    u_sub, u_lane = numbers(u_square, 0), numbers(u_square, 1)
    unit_col = across(u_sub == u_lane, unit_row)
    u_device = whole(u_sub, U_DEV)
    u_side = whole(u_device, half)
    u_place = (u_device - u_side * half) * (2 * U_DEV) + u_side * U_DEV + (u_sub - u_device * U_DEV)
    tables_v[of_slot : of_slot + 1, :] = index_row(down(unit_col == u_lane, u_place), units)
    to_table = pltpu.make_async_copy(tables_v, table, table_sem.at[0])
    to_table.start()

    to_order.wait()

    def sort_page(at, head=True, tail=True):
        if head:
            pages[at, pl.ds(0, FIRST)] = unsorted_head[order[0, at]]
        if tail:
            pages[at, pl.ds(FIRST, PAGE - FIRST)] = unsorted_tail[order[0, at]]

    def sort_far(start, stop, *part):
        @pl.loop(start, stop)
        def _(turn):
            rank, place = turn_of(turn)
            sort_page(far(place) * capacity + rank, *part)

    def sort_near(start, stop):
        @pl.loop(start, stop)
        def _(turn):
            rank, place = turn_of(turn)
            sort_page(near(place) * capacity + rank)

    early = min(share(PLAN[0]), min(capacity, 2) * quarter)
    load_pages[0].wait()
    sort_far(0, early, True, False)
    pl.semaphore_wait(barrier, jnp.where(side == 0, quarter, half))
    send_far(0, early, 0, FIRST)
    load_pages[1].wait()
    sort_far(0, early, False, True)
    send_far(0, early, FIRST, PAGE - FIRST)
    for load in [load_hidden] + loads[:heads]:
        load.start()

    @pl.when(side == 1)
    def _():
        @pl.loop(0, half)
        def _(device):
            greet(settled, device)

    sort_near(0, early)
    sort_far(early, turns)
    sort_near(early, turns)
    to_table.wait()

    small[2].wait()
    row_at = lax.broadcasted_iota(jnp.int32, (rows, HD), 0)
    lane_at = lax.broadcasted_iota(jnp.int32, (rows, HD), 1)
    positions = jnp.zeros((rows, HD), jnp.float32)
    for r in range(requests):
        positions = jnp.where(row_at // 2 == r, lengths[0, r].astype(jnp.float32), positions)
    positions = positions + (row_at % 2).astype(jnp.float32)
    power = (lane_at % (HD // 2)).astype(jnp.float32) * (2.0 / HD)
    angles = positions * jnp.exp(power * -math.log(rope_base))
    cos_ref[...] = jnp.cos(angles)
    sin_ref[...] = jnp.where(lane_at < HD // 2, -jnp.sin(angles), jnp.sin(angles))
    load_hidden.wait()
    for r in range(requests):
        hidden_wide[2 * r : 2 * r + 2, :] = hidden_in[r].astype(jnp.float32)
    hidden_ref[...] = hidden_wide[...].astype(jnp.bfloat16)

    @pl.when(side == 0)
    def _():
        pl.semaphore_wait(settled, half)
        greet(settled, partner)

    for c in range(heads):
        loads[c].wait()
        part = lax.dot_general(
            hidden_ref[...], qkv_w[c], NT, preferred_element_type=jnp.float32
        ).astype(jnp.bfloat16).astype(jnp.float32)
        turned = part * cos_ref[...] + pltpu.roll(part, HD // 2, 1) * sin_ref[...]
        is_value = lax.rem(me * heads + c, head_rows) == head_rows - 1
        rows_all[me, c] = jnp.where(is_value, part, turned).astype(jnp.bfloat16)

    row_copy(0, me, partner).start()

    @pl.when(side == 1)
    def _():
        pl.semaphore_wait(settled, 1)

    @pl.loop(1, half)
    def _(offset):
        row_copy(1, me, near(offset)).start()

    late = share(PLAN[1]) - early

    @pl.loop(0, late)
    def _(turn):
        send_far(early + turn, early + turn + 1)
        send_near(turn * early // late, (turn + 1) * early // late)

    send_near(early, share(PLAN[1]))
    for load in loads[heads:]:
        load.start()
    own_pages = pltpu.make_async_copy(
        pages.at[pl.ds(me * capacity, capacity)],
        arrived_hbm.at[pl.ds(me * capacity, capacity)],
        page_recv,
    )
    own_pages.start()

    row_copy(0, partner, partner).wait_recv()

    @pl.loop(1, half)
    def _(offset):
        row_copy(1, partner, near(offset)).start()

    send_pages(share(PLAN[1]), share(PLAN[2]))

    many_rows(devices - 2).wait_recv()

    for h in range(KVH):
        for g in range(group_count):
            at = h * head_rows + g
            spread[pl.ds(h * span + g, rows, stride=group_count), :] = rows_all[
                at // heads, at % heads
            ].astype(jnp.float32)
        at = h * head_rows + group_count
        new_keys[h] = rows_all[at // heads, at % heads]
        new_values[h] = rows_all[(at + 1) // heads, (at + 1) % heads]
        for r in range(requests):
            start = h * span + r * 2 * group_count
            queries[h * requests + r] = spread[start : start + 2 * group_count, :].astype(
                jnp.bfloat16
            )

    @pl.loop(0, devices)
    def _(target):
        spent = share(PLAN[3]) - share(PLAN[2])
        send_pages(
            share(PLAN[2]) + target * spent // devices,
            share(PLAN[2]) + (target + 1) * spent // devices,
        )
        zero = jnp.zeros((2 * group_count, PAGE), jnp.float32)
        sums, totals = [zero] * U_DEV, [zero[:, :1]] * U_DEV
        for rank in range(capacity):
            query = queries[table[of_query, target * capacity + rank]]
            left = table[of_left, target * capacity + rank]
            page = pages[target * capacity + rank]
            scores = lax.dot_general(
                query, page[:, :HD], NT, preferred_element_type=jnp.float32
            ) * score_scale
            weights = jnp.where(lane < left, jnp.exp(scores), 0.0)
            total = jnp.sum(weights, axis=-1, keepdims=True)
            weighted = jnp.dot(
                weights.astype(jnp.bfloat16), page[:, HD:], preferred_element_type=jnp.float32
            )
            slot = table[of_target, target * capacity + rank]
            for j in range(U_DEV):
                sums[j] = sums[j] + jnp.where(slot == j, weighted, 0.0)
                totals[j] = totals[j] + jnp.where(slot == j, total, 0.0)
        place, which = lax.rem(target, half), target // half
        for j in range(U_DEV):
            part_out[place, which, j] = sums[j].astype(jnp.bfloat16)
        part_out[place, which, U_DEV] = pack_totals(totals)

    @pl.loop(1, half)
    def _(offset):
        part_copy(lax.rem(here + offset, half), here, near(offset)).start()

    own_sums, own_totals = [], []
    row = lax.broadcasted_iota(jnp.int32, (2 * group_count, rows), 0)
    col = lax.broadcasted_iota(jnp.int32, (2 * group_count, rows), 1)
    line = lax.broadcasted_iota(jnp.int32, (rows, HD), 0)
    for j in range(2 * U_DEV):
        unit = units_s[0, (j // U_DEV * half + here) * U_DEV + j % U_DEV]
        request, head = unit // KVH, unit % KVH
        scores = lax.dot_general(
            queries[head * requests + request], new_keys[head], NT, preferred_element_type=jnp.float32
        ) * score_scale
        seen = (col // 2 == request) & (col % 2 <= row // group_count)
        weights = jnp.where(seen, jnp.exp(scores), 0.0)
        own_totals.append(jnp.sum(weights, axis=-1, keepdims=True))
        own_sums.append(
            jnp.dot(weights.astype(jnp.bfloat16), new_values[head], preferred_element_type=jnp.float32)
        )
    for j in range(U_DEV):
        unit = units_s[0, me * U_DEV + j]
        request, head = unit // KVH, unit % KVH
        for step in range(2):
            mine = line == request * 2 + step
            for part, kind in ((0, new_keys[head]), (1, new_values[head])):
                fresh_ref[j, step : step + 1, part * HD : (part + 1) * HD] = jnp.sum(
                    jnp.where(mine, kind.astype(jnp.float32), 0.0), axis=0, keepdims=True
                )

    slot_at = numbers((pages_dev, 1), 0)
    wanted = jnp.zeros((pages_dev, 1), jnp.int32)
    for j in range(U_DEV):
        first_page = units_s[0, me * U_DEV + j] * per_unit - j * per_unit
        wanted = jnp.where(whole(slot_at, per_unit) == j, slot_at + first_page, wanted)
    found = jnp.zeros(wide, jnp.int32)
    for b in range(ids.shape[0]):
        found = found + jnp.where(
            wanted == ids[b : b + 1, :], numbers(wide, 1) + b * wide[1], 0
        )
    source_col = jnp.sum(found, axis=1, keepdims=True)
    source_row = down(k_sub == k_lane, source_col)
    holder_col, holder_row = whole(source_col, pages_dev), whole(source_row, pages_dev)
    rank_col = across(
        (holder_col == holder_row) & (source_row < source_col), jnp.ones(square, jnp.int32)
    )
    place_ref[0:1, :] = index_row(
        down(k_sub == k_lane, holder_col * capacity + rank_col), pages_dev
    )
    own_lengths = jnp.zeros((1, pages_dev), jnp.int32)
    for j in range(U_DEV):
        own_lengths = jnp.where(
            lax.broadcasted_iota(jnp.int32, (1, pages_dev), 1) == j,
            lengths[0, units_s[0, me * U_DEV + j] // KVH], own_lengths,
        )
    place_ref[1:2, :] = own_lengths

    many_parts(half - 1).wait_recv()

    def half_sum(which):
        def add(offset, carry):
            block = part_in.at[lax.rem(here + offset, half), which]
            return tuple(c + block[j].astype(jnp.float32) for j, c in enumerate(carry))

        first = tuple(
            part_out[here, which, j].astype(jnp.float32) for j in range(U_DEV + 1)
        )
        return lax.fori_loop(1, half, add, first)

    kept = half_sum(0) + half_sum(1)
    blocks = U_DEV + 1
    for which in range(2):
        for j in range(U_DEV):
            swap_out[which * blocks + j] = kept[which * blocks + j].astype(jnp.bfloat16)
        packed = kept[which * blocks + U_DEV]
        swap_out[which * blocks + U_DEV] = pack_totals(
            [unpack_total(packed, j) for j in range(U_DEV)]
        )
    swap_copy().start()
    send_pages(share(PLAN[3]), share(PLAN[4]))
    swap_copy().wait_recv()
    for which in range(2):
        last = which * blocks + U_DEV
        packed = kept[last] + swap_in[last].astype(jnp.float32)
        for j in range(U_DEV):
            at = which * blocks + j
            total = own_totals[which * U_DEV + j] + unpack_total(packed, j)
            weighted = own_sums[which * U_DEV + j] + kept[at] + swap_in[at].astype(jnp.float32)
            att_all[here, which * U_DEV + j] = (weighted / total).astype(jnp.bfloat16)

    @pl.loop(1, half)
    def _(offset):
        att_copy(near(offset)).start()

    send_pages(share(PLAN[4]), turns)
    many_att(half - 1).wait_recv()

    for r in range(requests):
        for h in range(KVH):
            slot = table[of_slot, r * KVH + h]
            spread[h * span + r * 2 * group_count : h * span + (r + 1) * 2 * group_count, :] = (
                att_all[slot // (2 * U_DEV), slot % (2 * U_DEV)].astype(jnp.float32)
            )
    for h in range(KVH):
        for g in range(group_count):
            at = (h * group_count + g) * HD
            flat[:, at : at + HD] = spread[
                pl.ds(h * span + g, rows, stride=group_count), :
            ].astype(jnp.bfloat16)
    for c in range(tiles):
        loads[heads + c].wait()
        mixed_ref[:, c * HD : (c + 1) * HD] = lax.dot_general(
            flat[...], out_w[c], NT, preferred_element_type=jnp.float32
        ).astype(jnp.bfloat16)

    results = [
        pltpu.make_async_copy(src, dst, result_sem.at[i])
        for i, (src, dst) in enumerate(
            ((mixed_ref, mixed_hbm), (fresh_ref, fresh_hbm), (place_ref, place_hbm))
        )
    ]
    for result in results:
        result.start()
    for result in results:
        result.wait()
    remote(arrived_hbm, arrived_hbm, page_send, page_recv, partner).wait_recv()
    sent_pages = pages.at[pl.ds(0, (devices - 1) * capacity)]
    remote(sent_pages, sent_pages, page_send, page_recv, partner).wait_send()
    many_rows(devices - 1).wait_send()
    many_parts(half - 1).wait_send()
    swap_copy().wait_send()
    many_att(half - 1).wait_send()


def fused_body(hidden_states, qkv_weight, out_weight, cache_pages, context_lengths, new_units, old_pages):
    devices = lax.axis_size("tp")
    requests = hidden_states.shape[0]
    rows = requests * 2
    pages_dev = cache_pages.shape[0]
    capacity = pages_dev // devices
    heads = qkv_weight.shape[0] // HD
    tiles = out_weight.shape[0] // HD
    group_count = HEADS // KVH
    units = new_units.shape[0]
    hbm = pl.BlockSpec(memory_space=pl.ANY)
    vmem = pl.BlockSpec(memory_space=pltpu.VMEM)
    smem = pl.BlockSpec(memory_space=pltpu.SMEM)
    dma = pltpu.SemaphoreType.DMA
    lengths = context_lengths.reshape(1, requests)
    unit_table = new_units.reshape(1, units)
    page_table = old_pages.reshape(-1, PAGE)
    tile = (2 * group_count, HD)
    f32, bf16, i32 = jnp.float32, jnp.bfloat16, jnp.int32
    arrived, mixed, fresh, place = pl.pallas_call(
        lambda *refs: layer_kernel(devices, capacity, *refs),
        out_shape=(
            jax.ShapeDtypeStruct(cache_pages.shape, bf16),
            jax.ShapeDtypeStruct((rows, out_weight.shape[0]), bf16),
            jax.ShapeDtypeStruct((U_DEV, 2, 2 * HD), f32),
            jax.ShapeDtypeStruct((2, pages_dev), i32),
        ),
        in_specs=[pl.BlockSpec(memory_space=pltpu.HBM)] * 7,
        out_specs=(hbm, hbm, hbm, hbm),
        scratch_shapes=[
            pltpu.SMEM(lengths.shape, i32),
            pltpu.SMEM(unit_table.shape, i32),
            pltpu.VMEM(unit_table.shape, i32),
            pltpu.VMEM(page_table.shape, i32),
            pltpu.VMEM((1, pages_dev), i32),
            pltpu.SMEM((1, pages_dev), i32),
            pltpu.VMEM((8, pages_dev), i32),
            pltpu.SMEM((8, pages_dev), i32),
            pltpu.VMEM(hidden_states.shape, bf16),
            pltpu.VMEM((rows, D), f32),
            pltpu.VMEM((rows, D), bf16),
            pltpu.VMEM((rows, HD), f32),
            pltpu.VMEM((rows, HD), f32),
            pltpu.VMEM((heads, HD, D), bf16),
            pltpu.VMEM((tiles, HD, HEADS * HD), bf16),
            pltpu.VMEM((pages_dev, FIRST, 2 * HD), bf16),
            pltpu.VMEM((pages_dev, PAGE - FIRST, 2 * HD), bf16),
            pltpu.VMEM(cache_pages.shape, bf16),
            pltpu.VMEM((devices, heads, rows, HD), bf16),
            pltpu.VMEM((units * 2 * group_count, HD), f32),
            pltpu.VMEM((units,) + tile, bf16),
            pltpu.VMEM((KVH, rows, HD), bf16),
            pltpu.VMEM((KVH, rows, HD), bf16),
            pltpu.VMEM((devices // 2, 2, U_DEV + 1) + tile, bf16),
            pltpu.VMEM((devices // 2, 2, U_DEV + 1) + tile, bf16),
            pltpu.VMEM((2 * (U_DEV + 1),) + tile, bf16),
            pltpu.VMEM((2 * (U_DEV + 1),) + tile, bf16),
            pltpu.VMEM((devices // 2, 2 * U_DEV) + tile, bf16),
            pltpu.VMEM((rows, HEADS * HD), bf16),
            dma((heads + tiles,)),
            dma(()), dma(()),
            dma(()), dma((2,)),
            dma(()), dma(()), dma(()), dma(()),
            dma(()), dma(()),
            dma((7,)), dma((2,)), pltpu.SemaphoreType.REGULAR,
            pltpu.VMEM((rows, out_weight.shape[0]), bf16),
            pltpu.VMEM((U_DEV, 2, 2 * HD), f32),
            pltpu.VMEM((2, pages_dev), i32),
            dma((3,)),
        ],
        compiler_params=pltpu.CompilerParams(
            collective_id=0, has_side_effects=True, vmem_limit_bytes=44 << 20
        ),
        name="layer",
    )(*[pltpu.with_memory_space_constraint(x, pltpu.HBM) for x in (lengths, unit_table, page_table, hidden_states, qkv_weight, out_weight, cache_pages)])
    mixed_shape = (requests, 2, out_weight.shape[0])
    placed, mixed = pl.pallas_call(
        place_kernel,
        out_shape=(
            jax.ShapeDtypeStruct(cache_pages.shape, bf16),
            jax.ShapeDtypeStruct(mixed_shape, bf16),
        ),
        in_specs=[smem, vmem, vmem, vmem],
        out_specs=(hbm, hbm),
        scratch_shapes=[
            pltpu.VMEM((U_DEV, 2) + cache_pages.shape[1:], bf16),
            pltpu.VMEM(mixed_shape, bf16),
            dma(()), dma(()),
        ],
        compiler_params=pltpu.CompilerParams(vmem_limit_bytes=8 << 20),
        name="place_pages",
    )(place, arrived, fresh, mixed)
    return (mixed, placed)


def body(hidden_states, qkv_weight, out_weight, cache_pages, context_lengths, new_units, old_pages):
    devices = lax.axis_size("tp")
    whole_heads = qkv_weight.shape[0] % HD == 0 and out_weight.shape[0] % HD == 0
    pages_dev = cache_pages.shape[0]
    whole_shares = pages_dev % devices == 0 and devices % 4 == 0 and hidden_states.shape[0] == KVH
    whole_shares = whole_shares and new_units.shape[0] == pages_dev and PAGE % pages_dev == 0
    chosen = fused_body if whole_heads and whole_shares else plain_body
    return chosen(
        hidden_states, qkv_weight, out_weight, cache_pages, context_lengths, new_units, old_pages
    )


def solution(mesh):
    in_specs = (
        P("group", None, None),
        P("tp", None),
        P("tp", None),
        P(("group", "tp"), None, None),
        P("group"),
        P("group"),
        P("group"),
    )
    out_specs = (P("group", None, "tp"), P(("group", "tp"), None, None))
    return jax.shard_map(body, mesh=mesh, in_specs=in_specs, out_specs=out_specs, check_vma=False)
```

```python
import math

import jax
import jax.numpy as jnp
from jax import lax
from jax.experimental import pallas as pl
from jax.experimental.pallas import tpu as pltpu
from jax.sharding import PartitionSpec as P

D = 8192
HEADS = 64
KVH = 8
HD = 128
U_DEV = 4
MAXCTX = 2048
PAGE = 128


rope_base = 10000.0


def rotate_positions(values, positions):
    half_dim = values.shape[-1] // 2
    frequency = rope_base ** (-(jnp.arange(half_dim, dtype=jnp.float32) * 2.0 / values.shape[-1]))
    angles = positions.astype(jnp.float32)[..., None] * frequency
    cosine = jnp.concatenate([jnp.cos(angles), jnp.cos(angles)], axis=-1)
    sine_table = jnp.concatenate([jnp.sin(angles), jnp.sin(angles)], axis=-1)
    turned = jnp.concatenate([-values[..., half_dim:], values[..., :half_dim]], axis=-1)
    return values * cosine + turned * sine_table


def prepare(unit_qkv, base_lengths):
    group_count = HEADS // KVH
    count_units = unit_qkv.shape[0]
    positions = base_lengths[:, None] + jnp.arange(2, dtype=jnp.int32)[None, :]
    widened = unit_qkv.astype(jnp.float32)
    queries = widened[..., : group_count * HD].reshape(count_units, 2, group_count, HD)
    queries = rotate_positions(queries, positions[:, :, None]).astype(jnp.bfloat16)
    new_keys = rotate_positions(
        widened[..., group_count * HD : (group_count + 1) * HD], positions
    ).astype(jnp.bfloat16)
    new_values = unit_qkv[..., (group_count + 1) * HD :]
    return (queries, new_keys, new_values)


def context_terms(context, queries, valid_count):
    score_scale = 1.0 / math.sqrt(HD)
    cached_keys = context[..., :HD]
    cached_values = context[..., HD:]
    scores = (
        jnp.einsum("psgd,ptd->psgt", queries, cached_keys, preferred_element_type=jnp.float32)
        * score_scale
    )
    visible = jnp.arange(context.shape[1], dtype=jnp.int32)[None, :] < valid_count[:, None]
    weights = jnp.where(visible[:, None, None, :], jnp.exp(scores), 0.0)
    totals = jnp.sum(weights, axis=-1)
    weighted = jnp.einsum(
        "psgt,ptd->psgd",
        weights.astype(jnp.bfloat16),
        cached_values,
        preferred_element_type=jnp.float32,
    )
    return (weighted, totals)


def own_terms(queries, new_keys, new_values):
    score_scale = 1.0 / math.sqrt(HD)
    scores = (
        jnp.einsum("usgd,ujd->usgj", queries, new_keys, preferred_element_type=jnp.float32)
        * score_scale
    )
    recent = jnp.arange(2, dtype=jnp.int32)[None, :] <= jnp.arange(2, dtype=jnp.int32)[:, None]
    weights = jnp.where(recent[None, :, None, :], jnp.exp(scores), 0.0)
    totals = jnp.sum(weights, axis=-1)
    weighted = jnp.einsum(
        "usgj,ujd->usgd",
        weights.astype(jnp.bfloat16),
        new_values,
        preferred_element_type=jnp.float32,
    )
    return (weighted, totals)


def plain_body(hidden_states, qkv_weight, out_weight, cache_pages, context_lengths, new_units, old_pages):
    devices = lax.axis_size("tp")
    device = lax.axis_index("tp")
    requests = hidden_states.shape[0]
    rows_dev = qkv_weight.shape[0]
    pages_dev, page_rows, page_width = cache_pages.shape
    group_count = HEADS // KVH
    unit_rows = (group_count + 2) * HD
    per_unit = MAXCTX // PAGE
    unit_slots = U_DEV
    capacity = max(1, pages_dev // devices)
    total_units = new_units.shape[0]
    total_pages = old_pages.shape[0]
    flat_rows = hidden_states.reshape(requests * 2, D)
    partial_qkv = lax.dot_general(
        flat_rows, qkv_weight, (((1,), (1,)), ((), ())), preferred_element_type=jnp.float32
    )
    partial_qkv = partial_qkv.astype(jnp.bfloat16).reshape(requests, 2, rows_dev)
    slot_index = (
        jnp.zeros((total_units,), jnp.int32)
        .at[new_units]
        .set(jnp.arange(total_units, dtype=jnp.int32))
    )
    own_units = lax.dynamic_slice_in_dim(new_units, device * unit_slots, unit_slots)
    own_requests = own_units // KVH
    own_heads = own_units % KVH
    own_lengths = context_lengths[own_requests]
    local_ids = lax.dynamic_slice_in_dim(old_pages, device * pages_dev, pages_dev)
    local_units = local_ids // per_unit
    local_index = local_ids % per_unit
    target_dev = (slot_index[local_units] * per_unit + local_index) // pages_dev
    local_order = jnp.arange(pages_dev, dtype=jnp.int32)
    send_rank = jnp.sum(
        (
            (target_dev[:, None] == target_dev[None, :])
            & (local_order[None, :] < local_order[:, None])
        ).astype(jnp.int32),
        axis=1,
    )
    outgoing = (
        jnp.zeros((devices, capacity, page_rows, page_width), jnp.bfloat16)
        .at[target_dev, send_rank]
        .set(cache_pages)
    )
    arrived = lax.all_to_all(outgoing, "tp", split_axis=0, concat_axis=0, tiled=True)
    stored_position = (
        jnp.zeros((total_pages,), jnp.int32)
        .at[old_pages]
        .set(jnp.arange(total_pages, dtype=jnp.int32))
    )
    wanted = (
        own_units[:, None] * per_unit + jnp.arange(per_unit, dtype=jnp.int32)[None, :]
    ).reshape(pages_dev)
    source_pos = stored_position[wanted]
    source_dev = source_pos // pages_dev
    source_slot = source_pos % pages_dev
    arrival_rank = jnp.sum(
        (
            (source_dev[:, None] == source_dev[None, :])
            & (source_slot[None, :] < source_slot[:, None])
        ).astype(jnp.int32),
        axis=1,
    )
    relaid = arrived[source_dev, arrival_rank]
    contexts = relaid.reshape(unit_slots, MAXCTX, page_width)
    sources_per_head = unit_rows // rows_dev
    request_table = (new_units // KVH).reshape(devices, unit_slots)
    outgoing_rows = partial_qkv[request_table]
    incoming = lax.all_to_all(outgoing_rows, "tp", split_axis=0, concat_axis=0, tiled=True)
    grouped = jnp.moveaxis(incoming.reshape(KVH, sources_per_head, unit_slots, 2, rows_dev), 2, 0)
    chosen = jnp.take_along_axis(grouped, own_heads[:, None, None, None, None], axis=1)[:, 0]
    own_rows = chosen.transpose(0, 2, 1, 3).reshape(unit_slots, 2, unit_rows)
    queries, new_keys, new_values = prepare(own_rows, own_lengths)
    cache_sums, cache_totals = context_terms(contexts, queries, own_lengths)
    own_sums, own_totals = own_terms(queries, new_keys, new_values)
    attended = ((cache_sums + own_sums) / (cache_totals + own_totals)[..., None]).astype(
        jnp.bfloat16
    )
    attended = attended.reshape(unit_slots, 2, group_count * HD)
    all_heads = lax.all_gather(attended, "tp", axis=0, tiled=True)
    logical = (
        all_heads[slot_index]
        .reshape(requests, KVH, 2, group_count * HD)
        .transpose(0, 2, 1, 3)
        .reshape(requests * 2, HEADS * HD)
    )
    mixed_rows = lax.dot_general(
        logical, out_weight, (((1,), (1,)), ((), ())), preferred_element_type=jnp.float32
    )
    mixed_rows = mixed_rows.astype(jnp.bfloat16).reshape(requests, 2, out_weight.shape[0])
    fresh_rows = jnp.concatenate([new_keys, new_values], axis=-1)
    positions = jnp.arange(MAXCTX, dtype=jnp.int32)[None, :]
    contexts = jnp.where(
        (positions == own_lengths[:, None])[..., None], fresh_rows[:, 0:1], contexts
    )
    contexts = jnp.where(
        (positions == own_lengths[:, None] + 1)[..., None], fresh_rows[:, 1:2], contexts
    )
    return (mixed_rows, contexts.reshape(pages_dev, page_rows, page_width))


def place_kernel(
    table_ref, arrived_ref, fresh_ref, mixed_ref, out_ref, rows_ref, patched, rows, sem, rows_sem
):
    per_unit = MAXCTX // PAGE
    steps = fresh_ref.shape[1]

    def outward(at, src):
        return pltpu.make_async_copy(src, out_ref.at[at], sem)

    def place_of(slot, page):
        return slot * per_unit + lax.rem(table_ref[1, slot] // PAGE + page, per_unit)

    for slot in range(U_DEV):
        for page in range(steps, per_unit):
            at = place_of(slot, page)
            outward(at, arrived_ref.at[table_ref[0, at]]).start()

    for slot in range(U_DEV):
        for page in range(steps):
            at = place_of(slot, page)
            block = patched.at[slot, page]
            block[...] = arrived_ref[table_ref[0, at]]
            for step in range(steps):
                row = table_ref[1, slot] + step - (at - slot * per_unit) * PAGE

                @pl.when((row >= 0) & (row < PAGE))
                def _():
                    base = pl.multiple_of((row // 16) * 16, 16)
                    tile = block[pl.ds(base, 16), :]
                    line = lax.broadcasted_iota(jnp.int32, tile.shape, 0)
                    new = jnp.broadcast_to(fresh_ref[slot, step : step + 1, :], tile.shape)
                    mixed = jnp.where(line == row - base, new, tile.astype(jnp.float32))
                    block[pl.ds(base, 16), :] = mixed.astype(jnp.bfloat16)

            outward(at, block).start()

    mixed = mixed_ref[...].astype(jnp.float32)
    for r in range(rows.shape[0]):
        rows[r] = mixed[2 * r : 2 * r + 2].astype(jnp.bfloat16)
    rows_out = pltpu.make_async_copy(rows, rows_ref, rows_sem)
    rows_out.start()
    pltpu.make_async_copy(arrived_ref, out_ref, sem).wait()
    rows_out.wait()


NT = (((1,), (1,)), ((), ()))
PLAN = (8,12,16,22,28)
FIRST = 32


def layer_kernel(
    devices, capacity,
    lengths_hbm, units_hbm, ids_hbm, hidden_hbm, qkv_hbm, out_hbm, pages_hbm,
    arrived_hbm, mixed_hbm, fresh_hbm, place_hbm,
    lengths, units_s, units_v, ids, order_v, order, tables_v, table, hidden_in, hidden_wide, hidden_ref, cos_ref, sin_ref,
    qkv_w, out_w, unsorted_head, unsorted_tail, pages, rows_all, spread, queries, new_keys, new_values, part_out, part_in, swap_out, swap_in, att_all, flat,
    load_sem, page_send, page_recv, row_send, row_recv, part_send, part_recv, swap_send, swap_recv, att_send, att_recv,
    small_sem, table_sem, settled, mixed_ref, fresh_ref, place_ref, result_sem,
):
    me = lax.axis_index("tp")
    pages_dev = pages.shape[0]
    rows = hidden_ref.shape[0]
    requests = rows // 2
    units = requests * KVH
    per_unit = MAXCTX // PAGE
    heads = qkv_w.shape[0]
    tiles = out_w.shape[0]
    group_count = HEADS // KVH
    head_rows = group_count + 2
    score_scale = 1.0 / math.sqrt(HD)
    span = requests * 2 * group_count
    of_query, of_left, of_target, of_slot = range(4)

    half, quarter = devices // 2, devices // 4
    here, side = lax.rem(me, half), me // half
    partner = lax.rem(me + half, devices)

    def near(offset):
        return side * half + lax.rem(here + offset, half)

    def far(turn):
        return (1 - side) * half + (turn // quarter) * quarter + lax.rem(turn + me + 1, quarter)

    def remote(src, dst, send, recv, device):
        return pltpu.make_async_remote_copy(
            src_ref=src, dst_ref=dst, send_sem=send, recv_sem=recv,
            device_id={"tp": device}, device_id_type=pl.DeviceIdType.MESH,
        )

    def page_copy(rank, device, start=0, size=PAGE):
        return remote(
            pages.at[device * capacity + rank, pl.ds(start, size)],
            arrived_hbm.at[me * capacity + rank, pl.ds(start, size)],
            page_send, page_recv, device,
        )

    def row_copy(kind, owner, device):
        block = rows_all.at[owner]
        return remote(block, block, row_send, row_recv.at[kind], device)

    def many_rows(count):
        blocks = rows_all.at[pl.ds(0, count)]
        return remote(blocks, blocks, row_send, row_recv.at[1], partner)

    def att_copy(device):
        block = att_all.at[here]
        return remote(block, block, att_send, att_recv, device)

    def many_att(count):
        blocks = att_all.at[pl.ds(0, count)]
        return remote(blocks, blocks, att_send, att_recv, partner)

    def part_copy(src, dst, device):
        return remote(part_out.at[src], part_in.at[dst], part_send, part_recv, device)

    def many_parts(count):
        return remote(
            part_out.at[pl.ds(0, count)], part_in.at[pl.ds(0, count)], part_send, part_recv, partner
        )

    def swap_copy():
        return remote(swap_out, swap_in, swap_send, swap_recv, partner)

    turns = half * capacity

    def turn_of(turn):
        rank, place = turn // half, lax.rem(turn, half)
        if capacity == 1:
            return rank, place
        head = turn < 2 * half
        rank = jnp.where(head, lax.rem(turn // quarter, 2), rank)
        return rank, jnp.where(head, turn // half * quarter + lax.rem(turn, quarter), place)

    def send_far(start, stop, *part):
        @pl.loop(start, stop)
        def _(turn):
            rank, place = turn_of(turn)
            page_copy(rank, far(place), *part).start()

    def send_near(start, stop):
        @pl.loop(start, stop)
        def _(turn):
            rank, place = turn_of(turn)

            @pl.when(place > 0)
            def _():
                page_copy(rank, near(place)).start()

    def send_pages(start, stop):
        @pl.loop(start, stop)
        def _(turn):
            send_far(turn, turn + 1)
            send_near(turn, turn + 1)

    def share(numerator):
        return turns * numerator // 32

    def pack_totals(values):
        strip = PAGE // len(values)
        packed = jnp.zeros((2 * group_count, PAGE), jnp.float32)
        for j, total in enumerate(values):
            top = total.astype(jnp.bfloat16).astype(jnp.float32)
            packed = jnp.where(lane == j * strip, top, packed)
            packed = jnp.where(lane == j * strip + strip // 2, total - top, packed)
        return packed.astype(jnp.bfloat16)

    def unpack_total(packed, j, count=U_DEV):
        return jnp.sum(jnp.where(lane // (PAGE // count) == j, packed, 0.0), axis=-1, keepdims=True)

    lane = lax.broadcasted_iota(jnp.int32, (2 * group_count, PAGE), 1)

    small = [
        pltpu.make_async_copy(ids_hbm, ids, small_sem.at[0]),
        pltpu.make_async_copy(units_hbm, units_v, small_sem.at[1]),
        pltpu.make_async_copy(units_hbm, units_s, small_sem.at[2]),
        pltpu.make_async_copy(lengths_hbm, lengths, small_sem.at[3]),
    ]
    load_pages = [
        pltpu.make_async_copy(
            pages_hbm.at[:, pl.ds(start, part.shape[1])], part, small_sem.at[sem]
        )
        for start, part, sem in ((0, unsorted_head, 4), (FIRST, unsorted_tail, 6))
    ]
    load_hidden = pltpu.make_async_copy(hidden_hbm, hidden_in, small_sem.at[5])
    loads = [
        pltpu.make_async_copy(qkv_hbm.at[pl.ds(c * HD, HD)], qkv_w.at[c], load_sem.at[c])
        for c in range(heads)
    ]
    loads += [
        pltpu.make_async_copy(
            out_hbm.at[pl.ds(c * HD, HD)], out_w.at[c], load_sem.at[heads + c]
        )
        for c in range(tiles)
    ]
    for load in small + load_pages:
        load.start()

    barrier = pltpu.get_barrier_semaphore()

    def greet(semaphore, device):
        pl.semaphore_signal(
            semaphore, inc=1, device_id={"tp": device}, device_id_type=pl.DeviceIdType.MESH
        )

    @pl.when(side == 0)
    def _():
        @pl.loop(half, devices)
        def _(device):
            greet(barrier, device)

    @pl.when(me // quarter == 2)
    def _():
        @pl.loop(0, half)
        def _(device):
            greet(barrier, device)

    def numbers(shape, axis):
        return lax.broadcasted_iota(jnp.int32, shape, axis)

    def whole(values, size):
        return lax.shift_right_logical(values, jnp.full_like(values, size.bit_length() - 1))

    def index_row(values, size):
        return jnp.clip(values, 0, size - 1)

    def down(hit, values):
        return jnp.sum(jnp.where(hit, values, 0), axis=0, keepdims=True)

    def across(hit, values):
        return jnp.sum(jnp.where(hit, values, 0), axis=1, keepdims=True)

    square = (pages_dev, pages_dev)
    k_sub, k_lane = numbers(square, 0), numbers(square, 1)
    small[0].wait()
    first = me * pages_dev
    wide = (pages_dev, ids.shape[1])
    own_ids = ids[pl.ds(first // ids.shape[1], 1), :]
    mine = numbers(wide, 1) == numbers(wide, 0) + lax.rem(first, ids.shape[1])
    id_col = across(mine, own_ids)
    small[1].wait()
    unit_row = units_v[...]
    by_unit = (pages_dev, units)
    slot_col = across(whole(id_col, per_unit) == unit_row, numbers(by_unit, 1))
    target_col = whole(slot_col, U_DEV)
    target_row = down(k_sub == k_lane, target_col)
    rank_col = across((target_col == target_row) & (k_lane < k_sub), jnp.ones(square, jnp.int32))
    sent = target_col * capacity + rank_col == k_lane
    order_v[...] = index_row(down(sent, k_sub), pages_dev)
    to_order = pltpu.make_async_copy(order_v, order, table_sem.at[1])
    to_order.start()
    id_row = down(sent, id_col)
    tables_v[of_target : of_target + 1, :] = down(sent, slot_col - target_col * U_DEV)
    sent_unit = whole(id_row, per_unit)
    sent_request = whole(sent_unit, KVH)
    small[3].wait()
    sent_length = jnp.zeros_like(id_row)
    for r in range(requests):
        sent_length = jnp.where(sent_request == r, lengths[0, r], sent_length)
    tables_v[of_query : of_query + 1, :] = index_row(
        (sent_unit - sent_request * KVH) * requests + sent_request, units
    )
    tables_v[of_left : of_left + 1, :] = sent_length - (id_row - sent_unit * per_unit) * PAGE
    u_square = (units, units)
    u_sub, u_lane = numbers(u_square, 0), numbers(u_square, 1)
    unit_col = across(u_sub == u_lane, unit_row)
    u_device = whole(u_sub, U_DEV)
    u_side = whole(u_device, half)
    u_place = (u_device - u_side * half) * (2 * U_DEV) + u_side * U_DEV + (u_sub - u_device * U_DEV)
    tables_v[of_slot : of_slot + 1, :] = index_row(down(unit_col == u_lane, u_place), units)
    to_table = pltpu.make_async_copy(tables_v, table, table_sem.at[0])
    to_table.start()

    to_order.wait()

    def sort_page(at, head=True, tail=True):
        if head:
            pages[at, pl.ds(0, FIRST)] = unsorted_head[order[0, at]]
        if tail:
            pages[at, pl.ds(FIRST, PAGE - FIRST)] = unsorted_tail[order[0, at]]

    def sort_far(start, stop, *part):
        @pl.loop(start, stop)
        def _(turn):
            rank, place = turn_of(turn)
            sort_page(far(place) * capacity + rank, *part)

    def sort_near(start, stop):
        @pl.loop(start, stop)
        def _(turn):
            rank, place = turn_of(turn)
            sort_page(near(place) * capacity + rank)

    early = min(share(PLAN[0]), min(capacity, 2) * quarter)
    load_pages[0].wait()
    sort_far(0, early, True, False)
    pl.semaphore_wait(barrier, jnp.where(side == 0, quarter, half))
    send_far(0, early, 0, FIRST)
    load_pages[1].wait()
    sort_far(0, early, False, True)
    send_far(0, early, FIRST, PAGE - FIRST)
    for load in [load_hidden] + loads[:heads]:
        load.start()

    @pl.when(side == 1)
    def _():
        @pl.loop(0, half)
        def _(device):
            greet(settled, device)

    sort_near(0, early)
    sort_far(early, turns)
    sort_near(early, turns)
    to_table.wait()

    small[2].wait()
    row_at = lax.broadcasted_iota(jnp.int32, (rows, HD), 0)
    lane_at = lax.broadcasted_iota(jnp.int32, (rows, HD), 1)
    positions = jnp.zeros((rows, HD), jnp.float32)
    for r in range(requests):
        positions = jnp.where(row_at // 2 == r, lengths[0, r].astype(jnp.float32), positions)
    positions = positions + (row_at % 2).astype(jnp.float32)
    power = (lane_at % (HD // 2)).astype(jnp.float32) * (2.0 / HD)
    angles = positions * jnp.exp(power * -math.log(rope_base))
    cos_ref[...] = jnp.cos(angles)
    sin_ref[...] = jnp.where(lane_at < HD // 2, -jnp.sin(angles), jnp.sin(angles))
    load_hidden.wait()
    for r in range(requests):
        hidden_wide[2 * r : 2 * r + 2, :] = hidden_in[r].astype(jnp.float32)
    hidden_ref[...] = hidden_wide[...].astype(jnp.bfloat16)

    @pl.when(side == 0)
    def _():
        pl.semaphore_wait(settled, half)
        greet(settled, partner)

    for c in range(heads):
        loads[c].wait()
        part = lax.dot_general(
            hidden_ref[...], qkv_w[c], NT, preferred_element_type=jnp.float32
        ).astype(jnp.bfloat16).astype(jnp.float32)
        turned = part * cos_ref[...] + pltpu.roll(part, HD // 2, 1) * sin_ref[...]
        is_value = lax.rem(me * heads + c, head_rows) == head_rows - 1
        rows_all[me, c] = jnp.where(is_value, part, turned).astype(jnp.bfloat16)

    row_copy(0, me, partner).start()

    @pl.when(side == 1)
    def _():
        pl.semaphore_wait(settled, 1)

    @pl.loop(1, half)
    def _(offset):
        row_copy(1, me, near(offset)).start()

    late = share(PLAN[1]) - early

    @pl.loop(0, late)
    def _(turn):
        send_far(early + turn, early + turn + 1)
        send_near(turn * early // late, (turn + 1) * early // late)

    send_near(early, share(PLAN[1]))
    for load in loads[heads:]:
        load.start()
    own_pages = pltpu.make_async_copy(
        pages.at[pl.ds(me * capacity, capacity)],
        arrived_hbm.at[pl.ds(me * capacity, capacity)],
        page_recv,
    )
    own_pages.start()

    row_copy(0, partner, partner).wait_recv()

    @pl.loop(1, half)
    def _(offset):
        row_copy(1, partner, near(offset)).start()

    send_pages(share(PLAN[1]), share(PLAN[2]))

    many_rows(devices - 2).wait_recv()

    for h in range(KVH):
        for g in range(group_count):
            at = h * head_rows + g
            spread[pl.ds(h * span + g, rows, stride=group_count), :] = rows_all[
                at // heads, at % heads
            ].astype(jnp.float32)
        at = h * head_rows + group_count
        new_keys[h] = rows_all[at // heads, at % heads]
        new_values[h] = rows_all[(at + 1) // heads, (at + 1) % heads]
        for r in range(requests):
            start = h * span + r * 2 * group_count
            queries[h * requests + r] = spread[start : start + 2 * group_count, :].astype(
                jnp.bfloat16
            )

    @pl.loop(0, devices)
    def _(target):
        spent = share(PLAN[3]) - share(PLAN[2])
        send_pages(
            share(PLAN[2]) + target * spent // devices,
            share(PLAN[2]) + (target + 1) * spent // devices,
        )
        zero = jnp.zeros((2 * group_count, PAGE), jnp.float32)
        sums, totals = [zero] * U_DEV, [zero[:, :1]] * U_DEV
        places = [target * capacity + rank for rank in range(capacity)]
        scores = [
            lax.dot_general(
                queries[table[of_query, at]], pages[at, :, :HD], NT, preferred_element_type=jnp.float32
            ) * score_scale
            for at in places
        ]
        weights = [
            jnp.where(lane < table[of_left, at], jnp.exp(score), 0.0)
            for at, score in zip(places, scores)
        ]
        weighted = [
            jnp.dot(weight.astype(jnp.bfloat16), pages[at, :, HD:], preferred_element_type=jnp.float32)
            for at, weight in zip(places, weights)
        ]
        for at, weight, added in zip(places, weights, weighted):
            slot, total = table[of_target, at], jnp.sum(weight, axis=-1, keepdims=True)
            for j in range(U_DEV):
                sums[j] = sums[j] + jnp.where(slot == j, added, 0.0)
                totals[j] = totals[j] + jnp.where(slot == j, total, 0.0)
        place, which = lax.rem(target, half), target // half
        for j in range(U_DEV):
            part_out[place, which, j] = sums[j].astype(jnp.bfloat16)
        part_out[place, which, U_DEV] = pack_totals(totals)

    @pl.loop(1, half)
    def _(offset):
        part_copy(lax.rem(here + offset, half), here, near(offset)).start()

    own_sums, own_totals = [], []
    row = lax.broadcasted_iota(jnp.int32, (2 * group_count, rows), 0)
    col = lax.broadcasted_iota(jnp.int32, (2 * group_count, rows), 1)
    line = lax.broadcasted_iota(jnp.int32, (rows, HD), 0)
    for j in range(2 * U_DEV):
        unit = units_s[0, (j // U_DEV * half + here) * U_DEV + j % U_DEV]
        request, head = unit // KVH, unit % KVH
        scores = lax.dot_general(
            queries[head * requests + request], new_keys[head], NT, preferred_element_type=jnp.float32
        ) * score_scale
        seen = (col // 2 == request) & (col % 2 <= row // group_count)
        weights = jnp.where(seen, jnp.exp(scores), 0.0)
        own_totals.append(jnp.sum(weights, axis=-1, keepdims=True))
        own_sums.append(
            jnp.dot(weights.astype(jnp.bfloat16), new_values[head], preferred_element_type=jnp.float32)
        )
    for j in range(U_DEV):
        unit = units_s[0, me * U_DEV + j]
        request, head = unit // KVH, unit % KVH
        for step in range(2):
            mine = line == request * 2 + step
            for part, kind in ((0, new_keys[head]), (1, new_values[head])):
                fresh_ref[j, step : step + 1, part * HD : (part + 1) * HD] = jnp.sum(
                    jnp.where(mine, kind.astype(jnp.float32), 0.0), axis=0, keepdims=True
                )

    slot_at = numbers((pages_dev, 1), 0)
    wanted = jnp.zeros((pages_dev, 1), jnp.int32)
    for j in range(U_DEV):
        first_page = units_s[0, me * U_DEV + j] * per_unit - j * per_unit
        wanted = jnp.where(whole(slot_at, per_unit) == j, slot_at + first_page, wanted)
    found = jnp.zeros(wide, jnp.int32)
    for b in range(ids.shape[0]):
        found = found + jnp.where(
            wanted == ids[b : b + 1, :], numbers(wide, 1) + b * wide[1], 0
        )
    source_col = jnp.sum(found, axis=1, keepdims=True)
    source_row = down(k_sub == k_lane, source_col)
    holder_col, holder_row = whole(source_col, pages_dev), whole(source_row, pages_dev)
    rank_col = across(
        (holder_col == holder_row) & (source_row < source_col), jnp.ones(square, jnp.int32)
    )
    place_ref[0:1, :] = index_row(
        down(k_sub == k_lane, holder_col * capacity + rank_col), pages_dev
    )
    own_lengths = jnp.zeros((1, pages_dev), jnp.int32)
    for j in range(U_DEV):
        own_lengths = jnp.where(
            lax.broadcasted_iota(jnp.int32, (1, pages_dev), 1) == j,
            lengths[0, units_s[0, me * U_DEV + j] // KVH], own_lengths,
        )
    place_ref[1:2, :] = own_lengths

    many_parts(half - 1).wait_recv()

    def half_sum(which):
        def add(offset, carry):
            block = part_in.at[lax.rem(here + offset, half), which]
            return tuple(c + block[j].astype(jnp.float32) for j, c in enumerate(carry))

        first = tuple(
            part_out[here, which, j].astype(jnp.float32) for j in range(U_DEV + 1)
        )
        return lax.fori_loop(1, half, add, first)

    halves = [half_sum(0), half_sum(1)]
    kept = [block for halved in halves for block in halved[:U_DEV]]
    kept_totals = [unpack_total(halved[U_DEV], j) for halved in halves for j in range(U_DEV)]
    for j in range(2 * U_DEV):
        swap_out[j] = kept[j].astype(jnp.bfloat16)
    swap_out[2 * U_DEV] = pack_totals(kept_totals)
    swap_copy().start()
    send_pages(share(PLAN[3]), share(PLAN[4]))
    swap_copy().wait_recv()
    packed = swap_in[2 * U_DEV].astype(jnp.float32)
    for j in range(2 * U_DEV):
        total = own_totals[j] + kept_totals[j] + unpack_total(packed, j, 2 * U_DEV)
        weighted = own_sums[j] + kept[j] + swap_in[j].astype(jnp.float32)
        att_all[here, j] = (weighted / total).astype(jnp.bfloat16)

    @pl.loop(1, half)
    def _(offset):
        att_copy(near(offset)).start()

    send_pages(share(PLAN[4]), turns)
    many_att(half - 1).wait_recv()

    for r in range(requests):
        for h in range(KVH):
            slot = table[of_slot, r * KVH + h]
            spread[h * span + r * 2 * group_count : h * span + (r + 1) * 2 * group_count, :] = (
                att_all[slot // (2 * U_DEV), slot % (2 * U_DEV)].astype(jnp.float32)
            )
    for h in range(KVH):
        for g in range(group_count):
            at = (h * group_count + g) * HD
            flat[:, at : at + HD] = spread[
                pl.ds(h * span + g, rows, stride=group_count), :
            ].astype(jnp.bfloat16)
    for c in range(tiles):
        loads[heads + c].wait()
        mixed_ref[:, c * HD : (c + 1) * HD] = lax.dot_general(
            flat[...], out_w[c], NT, preferred_element_type=jnp.float32
        ).astype(jnp.bfloat16)

    results = [
        pltpu.make_async_copy(src, dst, result_sem.at[i])
        for i, (src, dst) in enumerate(
            ((mixed_ref, mixed_hbm), (fresh_ref, fresh_hbm), (place_ref, place_hbm))
        )
    ]
    for result in results:
        result.start()
    for result in results:
        result.wait()
    remote(arrived_hbm, arrived_hbm, page_send, page_recv, partner).wait_recv()
    sent_pages = pages.at[pl.ds(0, (devices - 1) * capacity)]
    remote(sent_pages, sent_pages, page_send, page_recv, partner).wait_send()
    many_rows(devices - 1).wait_send()
    many_parts(half - 1).wait_send()
    swap_copy().wait_send()
    many_att(half - 1).wait_send()


def fused_body(hidden_states, qkv_weight, out_weight, cache_pages, context_lengths, new_units, old_pages):
    devices = lax.axis_size("tp")
    requests = hidden_states.shape[0]
    rows = requests * 2
    pages_dev = cache_pages.shape[0]
    capacity = pages_dev // devices
    heads = qkv_weight.shape[0] // HD
    tiles = out_weight.shape[0] // HD
    group_count = HEADS // KVH
    units = new_units.shape[0]
    hbm = pl.BlockSpec(memory_space=pl.ANY)
    vmem = pl.BlockSpec(memory_space=pltpu.VMEM)
    smem = pl.BlockSpec(memory_space=pltpu.SMEM)
    dma = pltpu.SemaphoreType.DMA
    lengths = context_lengths.reshape(1, requests)
    unit_table = new_units.reshape(1, units)
    page_table = old_pages.reshape(-1, PAGE)
    tile = (2 * group_count, HD)
    f32, bf16, i32 = jnp.float32, jnp.bfloat16, jnp.int32
    arrived, mixed, fresh, place = pl.pallas_call(
        lambda *refs: layer_kernel(devices, capacity, *refs),
        out_shape=(
            jax.ShapeDtypeStruct(cache_pages.shape, bf16),
            jax.ShapeDtypeStruct((rows, out_weight.shape[0]), bf16),
            jax.ShapeDtypeStruct((U_DEV, 2, 2 * HD), f32),
            jax.ShapeDtypeStruct((2, pages_dev), i32),
        ),
        in_specs=[pl.BlockSpec(memory_space=pltpu.HBM)] * 7,
        out_specs=(hbm, hbm, hbm, hbm),
        scratch_shapes=[
            pltpu.SMEM(lengths.shape, i32),
            pltpu.SMEM(unit_table.shape, i32),
            pltpu.VMEM(unit_table.shape, i32),
            pltpu.VMEM(page_table.shape, i32),
            pltpu.VMEM((1, pages_dev), i32),
            pltpu.SMEM((1, pages_dev), i32),
            pltpu.VMEM((8, pages_dev), i32),
            pltpu.SMEM((8, pages_dev), i32),
            pltpu.VMEM(hidden_states.shape, bf16),
            pltpu.VMEM((rows, D), f32),
            pltpu.VMEM((rows, D), bf16),
            pltpu.VMEM((rows, HD), f32),
            pltpu.VMEM((rows, HD), f32),
            pltpu.VMEM((heads, HD, D), bf16),
            pltpu.VMEM((tiles, HD, HEADS * HD), bf16),
            pltpu.VMEM((pages_dev, FIRST, 2 * HD), bf16),
            pltpu.VMEM((pages_dev, PAGE - FIRST, 2 * HD), bf16),
            pltpu.VMEM(cache_pages.shape, bf16),
            pltpu.VMEM((devices, heads, rows, HD), bf16),
            pltpu.VMEM((units * 2 * group_count, HD), f32),
            pltpu.VMEM((units,) + tile, bf16),
            pltpu.VMEM((KVH, rows, HD), bf16),
            pltpu.VMEM((KVH, rows, HD), bf16),
            pltpu.VMEM((devices // 2, 2, U_DEV + 1) + tile, bf16),
            pltpu.VMEM((devices // 2, 2, U_DEV + 1) + tile, bf16),
            pltpu.VMEM((2 * U_DEV + 1,) + tile, bf16),
            pltpu.VMEM((2 * U_DEV + 1,) + tile, bf16),
            pltpu.VMEM((devices // 2, 2 * U_DEV) + tile, bf16),
            pltpu.VMEM((rows, HEADS * HD), bf16),
            dma((heads + tiles,)),
            dma(()), dma(()),
            dma(()), dma((2,)),
            dma(()), dma(()), dma(()), dma(()),
            dma(()), dma(()),
            dma((7,)), dma((2,)), pltpu.SemaphoreType.REGULAR,
            pltpu.VMEM((rows, out_weight.shape[0]), bf16),
            pltpu.VMEM((U_DEV, 2, 2 * HD), f32),
            pltpu.VMEM((2, pages_dev), i32),
            dma((3,)),
        ],
        compiler_params=pltpu.CompilerParams(
            collective_id=0, has_side_effects=True, vmem_limit_bytes=44 << 20
        ),
        name="layer",
    )(*[pltpu.with_memory_space_constraint(x, pltpu.HBM) for x in (lengths, unit_table, page_table, hidden_states, qkv_weight, out_weight, cache_pages)])
    mixed_shape = (requests, 2, out_weight.shape[0])
    placed, mixed = pl.pallas_call(
        place_kernel,
        out_shape=(
            jax.ShapeDtypeStruct(cache_pages.shape, bf16),
            jax.ShapeDtypeStruct(mixed_shape, bf16),
        ),
        in_specs=[smem, vmem, vmem, vmem],
        out_specs=(hbm, hbm),
        scratch_shapes=[
            pltpu.VMEM((U_DEV, 2) + cache_pages.shape[1:], bf16),
            pltpu.VMEM(mixed_shape, bf16),
            dma(()), dma(()),
        ],
        compiler_params=pltpu.CompilerParams(vmem_limit_bytes=8 << 20),
        name="place_pages",
    )(place, arrived, fresh, mixed)
    return (mixed, placed)


def body(hidden_states, qkv_weight, out_weight, cache_pages, context_lengths, new_units, old_pages):
    devices = lax.axis_size("tp")
    whole_heads = qkv_weight.shape[0] % HD == 0 and out_weight.shape[0] % HD == 0
    pages_dev = cache_pages.shape[0]
    whole_shares = pages_dev % devices == 0 and devices % 4 == 0 and hidden_states.shape[0] == KVH
    whole_shares = whole_shares and new_units.shape[0] == pages_dev and PAGE % pages_dev == 0
    chosen = fused_body if whole_heads and whole_shares else plain_body
    return chosen(
        hidden_states, qkv_weight, out_weight, cache_pages, context_lengths, new_units, old_pages
    )


def solution(mesh):
    in_specs = (
        P("group", None, None),
        P("tp", None),
        P("tp", None),
        P(("group", "tp"), None, None),
        P("group"),
        P("group"),
        P("group"),
    )
    out_specs = (P("group", None, "tp"), P(("group", "tp"), None, None))
    return jax.shard_map(body, mesh=mesh, in_specs=in_specs, out_specs=out_specs, check_vma=False)
```

```python
import math

import jax
import jax.numpy as jnp
from jax import lax
from jax.experimental import pallas as pl
from jax.experimental.pallas import tpu as pltpu
from jax.sharding import PartitionSpec as P

D = 8192
HEADS = 64
KVH = 8
HD = 128
U_DEV = 4
MAXCTX = 2048
PAGE = 128


rope_base = 10000.0


def rotate_positions(values, positions):
    half_dim = values.shape[-1] // 2
    frequency = rope_base ** (-(jnp.arange(half_dim, dtype=jnp.float32) * 2.0 / values.shape[-1]))
    angles = positions.astype(jnp.float32)[..., None] * frequency
    cosine = jnp.concatenate([jnp.cos(angles), jnp.cos(angles)], axis=-1)
    sine_table = jnp.concatenate([jnp.sin(angles), jnp.sin(angles)], axis=-1)
    turned = jnp.concatenate([-values[..., half_dim:], values[..., :half_dim]], axis=-1)
    return values * cosine + turned * sine_table


def prepare(unit_qkv, base_lengths):
    group_count = HEADS // KVH
    count_units = unit_qkv.shape[0]
    positions = base_lengths[:, None] + jnp.arange(2, dtype=jnp.int32)[None, :]
    widened = unit_qkv.astype(jnp.float32)
    queries = widened[..., : group_count * HD].reshape(count_units, 2, group_count, HD)
    queries = rotate_positions(queries, positions[:, :, None]).astype(jnp.bfloat16)
    new_keys = rotate_positions(
        widened[..., group_count * HD : (group_count + 1) * HD], positions
    ).astype(jnp.bfloat16)
    new_values = unit_qkv[..., (group_count + 1) * HD :]
    return (queries, new_keys, new_values)


def context_terms(context, queries, valid_count):
    score_scale = 1.0 / math.sqrt(HD)
    cached_keys = context[..., :HD]
    cached_values = context[..., HD:]
    scores = (
        jnp.einsum("psgd,ptd->psgt", queries, cached_keys, preferred_element_type=jnp.float32)
        * score_scale
    )
    visible = jnp.arange(context.shape[1], dtype=jnp.int32)[None, :] < valid_count[:, None]
    weights = jnp.where(visible[:, None, None, :], jnp.exp(scores), 0.0)
    totals = jnp.sum(weights, axis=-1)
    weighted = jnp.einsum(
        "psgt,ptd->psgd",
        weights.astype(jnp.bfloat16),
        cached_values,
        preferred_element_type=jnp.float32,
    )
    return (weighted, totals)


def own_terms(queries, new_keys, new_values):
    score_scale = 1.0 / math.sqrt(HD)
    scores = (
        jnp.einsum("usgd,ujd->usgj", queries, new_keys, preferred_element_type=jnp.float32)
        * score_scale
    )
    recent = jnp.arange(2, dtype=jnp.int32)[None, :] <= jnp.arange(2, dtype=jnp.int32)[:, None]
    weights = jnp.where(recent[None, :, None, :], jnp.exp(scores), 0.0)
    totals = jnp.sum(weights, axis=-1)
    weighted = jnp.einsum(
        "usgj,ujd->usgd",
        weights.astype(jnp.bfloat16),
        new_values,
        preferred_element_type=jnp.float32,
    )
    return (weighted, totals)


def plain_body(hidden_states, qkv_weight, out_weight, cache_pages, context_lengths, new_units, old_pages):
    devices = lax.axis_size("tp")
    device = lax.axis_index("tp")
    requests = hidden_states.shape[0]
    rows_dev = qkv_weight.shape[0]
    pages_dev, page_rows, page_width = cache_pages.shape
    group_count = HEADS // KVH
    unit_rows = (group_count + 2) * HD
    per_unit = MAXCTX // PAGE
    unit_slots = U_DEV
    capacity = max(1, pages_dev // devices)
    total_units = new_units.shape[0]
    total_pages = old_pages.shape[0]
    flat_rows = hidden_states.reshape(requests * 2, D)
    partial_qkv = lax.dot_general(
        flat_rows, qkv_weight, (((1,), (1,)), ((), ())), preferred_element_type=jnp.float32
    )
    partial_qkv = partial_qkv.astype(jnp.bfloat16).reshape(requests, 2, rows_dev)
    slot_index = (
        jnp.zeros((total_units,), jnp.int32)
        .at[new_units]
        .set(jnp.arange(total_units, dtype=jnp.int32))
    )
    own_units = lax.dynamic_slice_in_dim(new_units, device * unit_slots, unit_slots)
    own_requests = own_units // KVH
    own_heads = own_units % KVH
    own_lengths = context_lengths[own_requests]
    local_ids = lax.dynamic_slice_in_dim(old_pages, device * pages_dev, pages_dev)
    local_units = local_ids // per_unit
    local_index = local_ids % per_unit
    target_dev = (slot_index[local_units] * per_unit + local_index) // pages_dev
    local_order = jnp.arange(pages_dev, dtype=jnp.int32)
    send_rank = jnp.sum(
        (
            (target_dev[:, None] == target_dev[None, :])
            & (local_order[None, :] < local_order[:, None])
        ).astype(jnp.int32),
        axis=1,
    )
    outgoing = (
        jnp.zeros((devices, capacity, page_rows, page_width), jnp.bfloat16)
        .at[target_dev, send_rank]
        .set(cache_pages)
    )
    arrived = lax.all_to_all(outgoing, "tp", split_axis=0, concat_axis=0, tiled=True)
    stored_position = (
        jnp.zeros((total_pages,), jnp.int32)
        .at[old_pages]
        .set(jnp.arange(total_pages, dtype=jnp.int32))
    )
    wanted = (
        own_units[:, None] * per_unit + jnp.arange(per_unit, dtype=jnp.int32)[None, :]
    ).reshape(pages_dev)
    source_pos = stored_position[wanted]
    source_dev = source_pos // pages_dev
    source_slot = source_pos % pages_dev
    arrival_rank = jnp.sum(
        (
            (source_dev[:, None] == source_dev[None, :])
            & (source_slot[None, :] < source_slot[:, None])
        ).astype(jnp.int32),
        axis=1,
    )
    relaid = arrived[source_dev, arrival_rank]
    contexts = relaid.reshape(unit_slots, MAXCTX, page_width)
    sources_per_head = unit_rows // rows_dev
    request_table = (new_units // KVH).reshape(devices, unit_slots)
    outgoing_rows = partial_qkv[request_table]
    incoming = lax.all_to_all(outgoing_rows, "tp", split_axis=0, concat_axis=0, tiled=True)
    grouped = jnp.moveaxis(incoming.reshape(KVH, sources_per_head, unit_slots, 2, rows_dev), 2, 0)
    chosen = jnp.take_along_axis(grouped, own_heads[:, None, None, None, None], axis=1)[:, 0]
    own_rows = chosen.transpose(0, 2, 1, 3).reshape(unit_slots, 2, unit_rows)
    queries, new_keys, new_values = prepare(own_rows, own_lengths)
    cache_sums, cache_totals = context_terms(contexts, queries, own_lengths)
    own_sums, own_totals = own_terms(queries, new_keys, new_values)
    attended = ((cache_sums + own_sums) / (cache_totals + own_totals)[..., None]).astype(
        jnp.bfloat16
    )
    attended = attended.reshape(unit_slots, 2, group_count * HD)
    all_heads = lax.all_gather(attended, "tp", axis=0, tiled=True)
    logical = (
        all_heads[slot_index]
        .reshape(requests, KVH, 2, group_count * HD)
        .transpose(0, 2, 1, 3)
        .reshape(requests * 2, HEADS * HD)
    )
    mixed_rows = lax.dot_general(
        logical, out_weight, (((1,), (1,)), ((), ())), preferred_element_type=jnp.float32
    )
    mixed_rows = mixed_rows.astype(jnp.bfloat16).reshape(requests, 2, out_weight.shape[0])
    fresh_rows = jnp.concatenate([new_keys, new_values], axis=-1)
    positions = jnp.arange(MAXCTX, dtype=jnp.int32)[None, :]
    contexts = jnp.where(
        (positions == own_lengths[:, None])[..., None], fresh_rows[:, 0:1], contexts
    )
    contexts = jnp.where(
        (positions == own_lengths[:, None] + 1)[..., None], fresh_rows[:, 1:2], contexts
    )
    return (mixed_rows, contexts.reshape(pages_dev, page_rows, page_width))


def place_kernel(
    table_ref, arrived_ref, fresh_ref, mixed_ref, out_ref, rows_ref, patched, rows, sem, rows_sem
):
    per_unit = MAXCTX // PAGE
    steps = fresh_ref.shape[1]

    def outward(at, src):
        return pltpu.make_async_copy(src, out_ref.at[at], sem)

    for slot in range(U_DEV):
        for page in range(steps, per_unit):
            k = slot * per_unit + page
            outward(table_ref[0, k], arrived_ref.at[table_ref[1, k]]).start()

    for slot in range(U_DEV):
        for page in range(steps):
            k = slot * per_unit + page
            at = table_ref[0, k]
            block = patched.at[slot, page]
            content = arrived_ref[table_ref[1, k]].astype(jnp.float32)
            line = lax.broadcasted_iota(jnp.int32, content.shape, 0)
            row = jnp.broadcast_to(table_ref[2:3, k : k + 1], content.shape)
            for step in range(steps):
                new = jnp.broadcast_to(fresh_ref[slot, step : step + 1, :], content.shape)
                content = jnp.where(line == row + step, new, content)
            block[...] = content.astype(jnp.bfloat16)
            outward(at, block).start()

    mixed = mixed_ref[...].astype(jnp.float32)
    for r in range(rows.shape[0]):
        rows[r] = mixed[2 * r : 2 * r + 2].astype(jnp.bfloat16)
    rows_out = pltpu.make_async_copy(rows, rows_ref, rows_sem)
    rows_out.start()
    pltpu.make_async_copy(arrived_ref, out_ref, sem).wait()
    rows_out.wait()


NT = (((1,), (1,)), ((), ()))
PLAN = (8,14,18,22,28)
FIRST = 32


def layer_kernel(
    devices, capacity,
    lengths_hbm, units_hbm, ids_hbm, hidden_hbm, qkv_hbm, out_hbm, pages_hbm,
    arrived_hbm, mixed_hbm, fresh_hbm, place_hbm,
    lengths, units_s, units_v, ids, order_v, order, tables_v, table, hidden_in, hidden_wide, hidden_ref, cos_ref, sin_ref,
    qkv_w, out_w, unsorted_head, unsorted_tail, pages, rows_all, spread, queries, new_keys, new_values, part_out, part_in, swap_out, swap_in, att_all, flat,
    load_sem, page_send, page_recv, row_send, row_recv, part_send, part_recv, swap_send, swap_recv, att_send, att_recv,
    small_sem, table_sem, settled, mixed_ref, fresh_ref, place_ref, result_sem,
):
    me = lax.axis_index("tp")
    pages_dev = pages.shape[0]
    rows = hidden_ref.shape[0]
    requests = rows // 2
    units = requests * KVH
    per_unit = MAXCTX // PAGE
    heads = qkv_w.shape[0]
    tiles = out_w.shape[0]
    group_count = HEADS // KVH
    head_rows = group_count + 2
    score_scale = 1.0 / math.sqrt(HD)
    span = requests * 2 * group_count
    of_query, of_left, of_target, of_slot = range(4)

    half, quarter = devices // 2, devices // 4
    here, side = lax.rem(me, half), me // half
    partner = lax.rem(me + half, devices)

    def near(offset):
        return side * half + lax.rem(here + offset, half)

    def far(turn):
        return (1 - side) * half + (turn // quarter) * quarter + lax.rem(turn + me + 1, quarter)

    def remote(src, dst, send, recv, device):
        return pltpu.make_async_remote_copy(
            src_ref=src, dst_ref=dst, send_sem=send, recv_sem=recv,
            device_id={"tp": device}, device_id_type=pl.DeviceIdType.MESH,
        )

    def page_copy(rank, device, start=0, size=PAGE):
        return remote(
            pages.at[device * capacity + rank, pl.ds(start, size)],
            arrived_hbm.at[me * capacity + rank, pl.ds(start, size)],
            page_send, page_recv, device,
        )

    def row_copy(kind, owner, device):
        block = rows_all.at[owner]
        return remote(block, block, row_send, row_recv.at[kind], device)

    def many_rows(count):
        blocks = rows_all.at[pl.ds(0, count)]
        return remote(blocks, blocks, row_send, row_recv.at[1], partner)

    def att_copy(device):
        block = att_all.at[here]
        return remote(block, block, att_send, att_recv, device)

    def many_att(count):
        blocks = att_all.at[pl.ds(0, count)]
        return remote(blocks, blocks, att_send, att_recv, partner)

    def part_copy(src, dst, device):
        return remote(part_out.at[src], part_in.at[dst], part_send, part_recv, device)

    def many_parts(count):
        return remote(
            part_out.at[pl.ds(0, count)], part_in.at[pl.ds(0, count)], part_send, part_recv, partner
        )

    def swap_copy():
        return remote(swap_out, swap_in, swap_send, swap_recv, partner)

    turns = half * capacity

    def turn_of(turn):
        rank, place = turn // half, lax.rem(turn, half)
        if capacity == 1:
            return rank, place
        head = turn < 2 * half
        rank = jnp.where(head, lax.rem(turn // quarter, 2), rank)
        return rank, jnp.where(head, turn // half * quarter + lax.rem(turn, quarter), place)

    def send_far(start, stop, *part):
        @pl.loop(start, stop)
        def _(turn):
            rank, place = turn_of(turn)
            page_copy(rank, far(place), *part).start()

    def send_near(start, stop):
        @pl.loop(start, stop)
        def _(turn):
            rank, place = turn_of(turn)

            @pl.when(place > 0)
            def _():
                page_copy(rank, near(place)).start()

    def send_pages(start, stop):
        @pl.loop(start, stop)
        def _(turn):
            send_far(turn, turn + 1)
            send_near(turn, turn + 1)

    def share(numerator):
        return turns * numerator // 32

    def pack_totals(values):
        strip = PAGE // len(values)
        packed = jnp.zeros((2 * group_count, PAGE), jnp.float32)
        for j, total in enumerate(values):
            top = total.astype(jnp.bfloat16).astype(jnp.float32)
            packed = jnp.where(lane == j * strip, top, packed)
            packed = jnp.where(lane == j * strip + strip // 2, total - top, packed)
        return packed.astype(jnp.bfloat16)

    def unpack_total(packed, j, count=U_DEV):
        return jnp.sum(jnp.where(lane // (PAGE // count) == j, packed, 0.0), axis=-1, keepdims=True)

    lane = lax.broadcasted_iota(jnp.int32, (2 * group_count, PAGE), 1)

    small = [
        pltpu.make_async_copy(ids_hbm, ids, small_sem.at[0]),
        pltpu.make_async_copy(units_hbm, units_v, small_sem.at[1]),
        pltpu.make_async_copy(units_hbm, units_s, small_sem.at[2]),
        pltpu.make_async_copy(lengths_hbm, lengths, small_sem.at[3]),
    ]
    load_pages = [
        pltpu.make_async_copy(
            pages_hbm.at[:, pl.ds(start, part.shape[1])], part, small_sem.at[sem]
        )
        for start, part, sem in ((0, unsorted_head, 4), (FIRST, unsorted_tail, 6))
    ]
    load_hidden = pltpu.make_async_copy(hidden_hbm, hidden_in, small_sem.at[5])
    loads = [
        pltpu.make_async_copy(qkv_hbm.at[pl.ds(c * HD, HD)], qkv_w.at[c], load_sem.at[c])
        for c in range(heads)
    ]
    loads += [
        pltpu.make_async_copy(
            out_hbm.at[pl.ds(c * HD, HD)], out_w.at[c], load_sem.at[heads + c]
        )
        for c in range(tiles)
    ]
    for load in small + load_pages:
        load.start()

    barrier = pltpu.get_barrier_semaphore()

    def greet(semaphore, device):
        pl.semaphore_signal(
            semaphore, inc=1, device_id={"tp": device}, device_id_type=pl.DeviceIdType.MESH
        )

    @pl.when(side == 0)
    def _():
        @pl.loop(half, devices)
        def _(device):
            greet(barrier, device)

    @pl.when(me // quarter == 2)
    def _():
        @pl.loop(0, half)
        def _(device):
            greet(barrier, device)

    def numbers(shape, axis):
        return lax.broadcasted_iota(jnp.int32, shape, axis)

    def whole(values, size):
        return lax.shift_right_logical(values, jnp.full_like(values, size.bit_length() - 1))

    def index_row(values, size):
        return jnp.clip(values, 0, size - 1)

    def down(hit, values):
        return jnp.sum(jnp.where(hit, values, 0), axis=0, keepdims=True)

    def across(hit, values):
        return jnp.sum(jnp.where(hit, values, 0), axis=1, keepdims=True)

    square = (pages_dev, pages_dev)
    k_sub, k_lane = numbers(square, 0), numbers(square, 1)
    small[0].wait()
    first = me * pages_dev
    wide = (pages_dev, ids.shape[1])
    own_ids = ids[pl.ds(first // ids.shape[1], 1), :]
    mine = numbers(wide, 1) == numbers(wide, 0) + lax.rem(first, ids.shape[1])
    id_col = across(mine, own_ids)
    small[1].wait()
    unit_row = units_v[...]
    by_unit = (pages_dev, units)
    slot_col = across(whole(id_col, per_unit) == unit_row, numbers(by_unit, 1))
    target_col = whole(slot_col, U_DEV)
    target_row = down(k_sub == k_lane, target_col)
    rank_col = across((target_col == target_row) & (k_lane < k_sub), jnp.ones(square, jnp.int32))
    sent = target_col * capacity + rank_col == k_lane
    order_v[...] = index_row(down(sent, k_sub), pages_dev)
    to_order = pltpu.make_async_copy(order_v, order, table_sem.at[1])
    to_order.start()
    id_row = down(sent, id_col)
    tables_v[of_target : of_target + 1, :] = down(sent, slot_col - target_col * U_DEV)
    sent_unit = whole(id_row, per_unit)
    sent_request = whole(sent_unit, KVH)
    small[3].wait()
    sent_length = jnp.zeros_like(id_row)
    for r in range(requests):
        sent_length = jnp.where(sent_request == r, lengths[0, r], sent_length)
    tables_v[of_query : of_query + 1, :] = index_row(
        (sent_unit - sent_request * KVH) * requests + sent_request, units
    )
    tables_v[of_left : of_left + 1, :] = sent_length - (id_row - sent_unit * per_unit) * PAGE
    u_square = (units, units)
    u_sub, u_lane = numbers(u_square, 0), numbers(u_square, 1)
    unit_col = across(u_sub == u_lane, unit_row)
    u_device = whole(u_sub, U_DEV)
    u_side = whole(u_device, half)
    u_place = (u_device - u_side * half) * (2 * U_DEV) + u_side * U_DEV + (u_sub - u_device * U_DEV)
    tables_v[of_slot : of_slot + 1, :] = index_row(down(unit_col == u_lane, u_place), units)
    to_table = pltpu.make_async_copy(tables_v, table, table_sem.at[0])
    to_table.start()

    def sort_page(at, head=True, tail=True, source=None):
        source = order[0, at] if source is None else source
        if head:
            pages[at, pl.ds(0, FIRST)] = unsorted_head[source]
        if tail:
            pages[at, pl.ds(FIRST, PAGE - FIRST)] = unsorted_tail[source]

    def sort_far(start, stop, *part):
        @pl.loop(start, stop)
        def _(turn):
            rank, place = turn_of(turn)
            sort_page(far(place) * capacity + rank, *part)

    def sort_near(start, stop):
        @pl.loop(start, stop)
        def _(turn):
            rank, place = turn_of(turn)
            sort_page(near(place) * capacity + rank)

    early = min(share(PLAN[0]), min(capacity, 2) * quarter)
    load_pages[0].wait()
    order_row = index_row(down(sent, k_sub), pages_dev)
    for turn in range(early):
        rank, place = turn_of(turn)
        at = far(place) * capacity + rank
        sort_page(at, True, False, jnp.sum(jnp.where(k_lane[0:1] == at, order_row, 0)))
    pl.semaphore_wait(barrier, jnp.where(side == 0, quarter, half))
    send_far(0, early, 0, FIRST)
    load_pages[1].wait()
    to_order.wait()
    sort_far(0, early, False, True)
    send_far(0, early, FIRST, PAGE - FIRST)
    for load in [load_hidden] + loads[:heads]:
        load.start()

    @pl.when(side == 1)
    def _():
        @pl.loop(0, half)
        def _(device):
            greet(settled, device)

    sort_near(0, early)
    sort_far(early, turns)
    sort_near(early, turns)
    to_table.wait()

    small[2].wait()
    row_at = lax.broadcasted_iota(jnp.int32, (rows, HD), 0)
    lane_at = lax.broadcasted_iota(jnp.int32, (rows, HD), 1)
    positions = jnp.zeros((rows, HD), jnp.float32)
    for r in range(requests):
        positions = jnp.where(row_at // 2 == r, lengths[0, r].astype(jnp.float32), positions)
    positions = positions + (row_at % 2).astype(jnp.float32)
    power = (lane_at % (HD // 2)).astype(jnp.float32) * (2.0 / HD)
    angles = positions * jnp.exp(power * -math.log(rope_base))
    cos_ref[...] = jnp.cos(angles)
    sin_ref[...] = jnp.where(lane_at < HD // 2, -jnp.sin(angles), jnp.sin(angles))
    load_hidden.wait()
    for r in range(requests):
        hidden_wide[2 * r : 2 * r + 2, :] = hidden_in[r].astype(jnp.float32)
    hidden_ref[...] = hidden_wide[...].astype(jnp.bfloat16)

    @pl.when(side == 0)
    def _():
        pl.semaphore_wait(settled, half)
        greet(settled, partner)

    for c in range(heads):
        loads[c].wait()
        part = lax.dot_general(
            hidden_ref[...], qkv_w[c], NT, preferred_element_type=jnp.float32
        ).astype(jnp.bfloat16).astype(jnp.float32)
        turned = part * cos_ref[...] + pltpu.roll(part, HD // 2, 1) * sin_ref[...]
        is_value = lax.rem(me * heads + c, head_rows) == head_rows - 1
        rows_all[me, c] = jnp.where(is_value, part, turned).astype(jnp.bfloat16)

    row_copy(0, me, partner).start()

    @pl.when(side == 1)
    def _():
        pl.semaphore_wait(settled, 1)

    @pl.loop(1, half)
    def _(offset):
        row_copy(1, me, near(offset)).start()

    late = share(PLAN[1]) - early

    @pl.loop(0, late)
    def _(turn):
        send_far(early + turn, early + turn + 1)
        send_near(turn * early // late, (turn + 1) * early // late)

    send_near(early, share(PLAN[1]))
    for load in loads[heads:]:
        load.start()
    own_pages = pltpu.make_async_copy(
        pages.at[pl.ds(me * capacity, capacity)],
        arrived_hbm.at[pl.ds(me * capacity, capacity)],
        page_recv,
    )
    own_pages.start()

    row_copy(0, partner, partner).wait_recv()

    @pl.loop(1, half)
    def _(offset):
        row_copy(1, partner, near(offset)).start()

    send_pages(share(PLAN[1]), share(PLAN[2]))

    many_rows(devices - 2).wait_recv()

    for h in range(KVH):
        for g in range(group_count):
            at = h * head_rows + g
            spread[pl.ds(h * span + g, rows, stride=group_count), :] = rows_all[
                at // heads, at % heads
            ].astype(jnp.float32)
        at = h * head_rows + group_count
        new_keys[h] = rows_all[at // heads, at % heads]
        new_values[h] = rows_all[(at + 1) // heads, (at + 1) % heads]
        for r in range(requests):
            start = h * span + r * 2 * group_count
            queries[h * requests + r] = spread[start : start + 2 * group_count, :].astype(
                jnp.bfloat16
            )

    @pl.loop(0, devices)
    def _(target):
        spent = share(PLAN[3]) - share(PLAN[2])
        send_pages(
            share(PLAN[2]) + target * spent // devices,
            share(PLAN[2]) + (target + 1) * spent // devices,
        )
        zero = jnp.zeros((2 * group_count, PAGE), jnp.float32)
        sums, totals = [zero] * U_DEV, [zero[:, :1]] * U_DEV
        places = [target * capacity + rank for rank in range(capacity)]
        scores = [
            lax.dot_general(
                queries[table[of_query, at]], pages[at, :, :HD], NT, preferred_element_type=jnp.float32
            ) * score_scale
            for at in places
        ]
        weights = [
            jnp.where(lane < table[of_left, at], jnp.exp(score), 0.0)
            for at, score in zip(places, scores)
        ]
        weighted = [
            jnp.dot(weight.astype(jnp.bfloat16), pages[at, :, HD:], preferred_element_type=jnp.float32)
            for at, weight in zip(places, weights)
        ]
        for at, weight, added in zip(places, weights, weighted):
            slot, total = table[of_target, at], jnp.sum(weight, axis=-1, keepdims=True)
            for j in range(U_DEV):
                sums[j] = sums[j] + jnp.where(slot == j, added, 0.0)
                totals[j] = totals[j] + jnp.where(slot == j, total, 0.0)
        place, which = lax.rem(target, half), target // half
        for j in range(U_DEV):
            part_out[place, which, j] = sums[j].astype(jnp.bfloat16)
        part_out[place, which, U_DEV] = pack_totals(totals)

    @pl.loop(1, half)
    def _(offset):
        part_copy(lax.rem(here + offset, half), here, near(offset)).start()

    own_sums, own_totals = [], []
    row = lax.broadcasted_iota(jnp.int32, (2 * group_count, rows), 0)
    col = lax.broadcasted_iota(jnp.int32, (2 * group_count, rows), 1)
    line = lax.broadcasted_iota(jnp.int32, (rows, HD), 0)
    for j in range(2 * U_DEV):
        unit = units_s[0, (j // U_DEV * half + here) * U_DEV + j % U_DEV]
        request, head = unit // KVH, unit % KVH
        scores = lax.dot_general(
            queries[head * requests + request], new_keys[head], NT, preferred_element_type=jnp.float32
        ) * score_scale
        seen = (col // 2 == request) & (col % 2 <= row // group_count)
        weights = jnp.where(seen, jnp.exp(scores), 0.0)
        own_totals.append(jnp.sum(weights, axis=-1, keepdims=True))
        own_sums.append(
            jnp.dot(weights.astype(jnp.bfloat16), new_values[head], preferred_element_type=jnp.float32)
        )
    for j in range(U_DEV):
        unit = units_s[0, me * U_DEV + j]
        request, head = unit // KVH, unit % KVH
        for step in range(2):
            mine = line == request * 2 + step
            for part, kind in ((0, new_keys[head]), (1, new_values[head])):
                fresh_ref[j, step : step + 1, part * HD : (part + 1) * HD] = jnp.sum(
                    jnp.where(mine, kind.astype(jnp.float32), 0.0), axis=0, keepdims=True
                )

    slot_at = numbers((pages_dev, 1), 0)
    wanted = jnp.zeros((pages_dev, 1), jnp.int32)
    for j in range(U_DEV):
        first_page = units_s[0, me * U_DEV + j] * per_unit - j * per_unit
        wanted = jnp.where(whole(slot_at, per_unit) == j, slot_at + first_page, wanted)
    found = jnp.zeros(wide, jnp.int32)
    for b in range(ids.shape[0]):
        found = found + jnp.where(
            wanted == ids[b : b + 1, :], numbers(wide, 1) + b * wide[1], 0
        )
    source_col = jnp.sum(found, axis=1, keepdims=True)
    source_row = down(k_sub == k_lane, source_col)
    holder_col, holder_row = whole(source_col, pages_dev), whole(source_row, pages_dev)
    rank_col = across(
        (holder_col == holder_row) & (source_row < source_col), jnp.ones(square, jnp.int32)
    )
    arrives_col = jnp.clip(holder_col * capacity + rank_col, 0, pages_dev - 1)
    lane_row = numbers((1, pages_dev), 1)
    slot_row = whole(lane_row, per_unit)
    own_lengths = jnp.zeros((1, pages_dev), jnp.int32)
    for j in range(U_DEV):
        own_lengths = jnp.where(
            slot_row == j, lengths[0, units_s[0, me * U_DEV + j] // KVH], own_lengths
        )
    turned = whole(own_lengths, PAGE) + lane_row - slot_row * per_unit
    turned = turned - whole(turned, per_unit) * per_unit
    place_row = slot_row * per_unit + turned
    place_ref[0:1, :] = place_row
    place_ref[1:2, :] = down(k_sub == place_row, arrives_col)
    place_ref[2:3, :] = own_lengths - turned * PAGE

    many_parts(half - 1).wait_recv()

    def half_sum(which):
        def add(offset, carry):
            block = part_in.at[lax.rem(here + offset, half), which]
            return tuple(c + block[j].astype(jnp.float32) for j, c in enumerate(carry))

        first = tuple(
            part_out[here, which, j].astype(jnp.float32) for j in range(U_DEV + 1)
        )
        return lax.fori_loop(1, half, add, first)

    halves = [half_sum(0), half_sum(1)]
    kept = [block for halved in halves for block in halved[:U_DEV]]
    kept_totals = [unpack_total(halved[U_DEV], j) for halved in halves for j in range(U_DEV)]
    for j in range(2 * U_DEV):
        swap_out[j] = kept[j].astype(jnp.bfloat16)
    swap_out[2 * U_DEV] = pack_totals(kept_totals)
    swap_copy().start()
    send_pages(share(PLAN[3]), share(PLAN[4]))
    swap_copy().wait_recv()
    packed = swap_in[2 * U_DEV].astype(jnp.float32)
    for j in range(2 * U_DEV):
        total = own_totals[j] + kept_totals[j] + unpack_total(packed, j, 2 * U_DEV)
        weighted = own_sums[j] + kept[j] + swap_in[j].astype(jnp.float32)
        att_all[here, j] = (weighted / total).astype(jnp.bfloat16)

    @pl.loop(1, half)
    def _(offset):
        att_copy(near(offset)).start()

    send_pages(share(PLAN[4]), turns)
    many_att(half - 1).wait_recv()

    for r in range(requests):
        for h in range(KVH):
            slot = table[of_slot, r * KVH + h]
            spread[h * span + r * 2 * group_count : h * span + (r + 1) * 2 * group_count, :] = (
                att_all[slot // (2 * U_DEV), slot % (2 * U_DEV)].astype(jnp.float32)
            )
    for h in range(KVH):
        for g in range(group_count):
            at = (h * group_count + g) * HD
            flat[:, at : at + HD] = spread[
                pl.ds(h * span + g, rows, stride=group_count), :
            ].astype(jnp.bfloat16)
    for c in range(tiles):
        loads[heads + c].wait()
        mixed_ref[:, c * HD : (c + 1) * HD] = lax.dot_general(
            flat[...], out_w[c], NT, preferred_element_type=jnp.float32
        ).astype(jnp.bfloat16)

    results = [
        pltpu.make_async_copy(src, dst, result_sem.at[i])
        for i, (src, dst) in enumerate(
            ((mixed_ref, mixed_hbm), (fresh_ref, fresh_hbm), (place_ref, place_hbm))
        )
    ]
    for result in results:
        result.start()
    for result in results:
        result.wait()
    remote(arrived_hbm, arrived_hbm, page_send, page_recv, partner).wait_recv()
    sent_pages = pages.at[pl.ds(0, (devices - 1) * capacity)]
    remote(sent_pages, sent_pages, page_send, page_recv, partner).wait_send()
    many_rows(devices - 1).wait_send()
    many_parts(half - 1).wait_send()
    swap_copy().wait_send()
    many_att(half - 1).wait_send()


def fused_body(hidden_states, qkv_weight, out_weight, cache_pages, context_lengths, new_units, old_pages):
    devices = lax.axis_size("tp")
    requests = hidden_states.shape[0]
    rows = requests * 2
    pages_dev = cache_pages.shape[0]
    capacity = pages_dev // devices
    heads = qkv_weight.shape[0] // HD
    tiles = out_weight.shape[0] // HD
    group_count = HEADS // KVH
    units = new_units.shape[0]
    hbm = pl.BlockSpec(memory_space=pl.ANY)
    vmem = pl.BlockSpec(memory_space=pltpu.VMEM)
    smem = pl.BlockSpec(memory_space=pltpu.SMEM)
    dma = pltpu.SemaphoreType.DMA
    lengths = context_lengths.reshape(1, requests)
    unit_table = new_units.reshape(1, units)
    page_table = old_pages.reshape(-1, PAGE)
    tile = (2 * group_count, HD)
    f32, bf16, i32 = jnp.float32, jnp.bfloat16, jnp.int32
    arrived, mixed, fresh, place = pl.pallas_call(
        lambda *refs: layer_kernel(devices, capacity, *refs),
        out_shape=(
            jax.ShapeDtypeStruct(cache_pages.shape, bf16),
            jax.ShapeDtypeStruct((rows, out_weight.shape[0]), bf16),
            jax.ShapeDtypeStruct((U_DEV, 2, 2 * HD), f32),
            jax.ShapeDtypeStruct((3, pages_dev), i32),
        ),
        in_specs=[pl.BlockSpec(memory_space=pltpu.HBM)] * 7,
        out_specs=(hbm, hbm, hbm, hbm),
        scratch_shapes=[
            pltpu.SMEM(lengths.shape, i32),
            pltpu.SMEM(unit_table.shape, i32),
            pltpu.VMEM(unit_table.shape, i32),
            pltpu.VMEM(page_table.shape, i32),
            pltpu.VMEM((1, pages_dev), i32),
            pltpu.SMEM((1, pages_dev), i32),
            pltpu.VMEM((8, pages_dev), i32),
            pltpu.SMEM((8, pages_dev), i32),
            pltpu.VMEM(hidden_states.shape, bf16),
            pltpu.VMEM((rows, D), f32),
            pltpu.VMEM((rows, D), bf16),
            pltpu.VMEM((rows, HD), f32),
            pltpu.VMEM((rows, HD), f32),
            pltpu.VMEM((heads, HD, D), bf16),
            pltpu.VMEM((tiles, HD, HEADS * HD), bf16),
            pltpu.VMEM((pages_dev, FIRST, 2 * HD), bf16),
            pltpu.VMEM((pages_dev, PAGE - FIRST, 2 * HD), bf16),
            pltpu.VMEM(cache_pages.shape, bf16),
            pltpu.VMEM((devices, heads, rows, HD), bf16),
            pltpu.VMEM((units * 2 * group_count, HD), f32),
            pltpu.VMEM((units,) + tile, bf16),
            pltpu.VMEM((KVH, rows, HD), bf16),
            pltpu.VMEM((KVH, rows, HD), bf16),
            pltpu.VMEM((devices // 2, 2, U_DEV + 1) + tile, bf16),
            pltpu.VMEM((devices // 2, 2, U_DEV + 1) + tile, bf16),
            pltpu.VMEM((2 * U_DEV + 1,) + tile, bf16),
            pltpu.VMEM((2 * U_DEV + 1,) + tile, bf16),
            pltpu.VMEM((devices // 2, 2 * U_DEV) + tile, bf16),
            pltpu.VMEM((rows, HEADS * HD), bf16),
            dma((heads + tiles,)),
            dma(()), dma(()),
            dma(()), dma((2,)),
            dma(()), dma(()), dma(()), dma(()),
            dma(()), dma(()),
            dma((7,)), dma((2,)), pltpu.SemaphoreType.REGULAR,
            pltpu.VMEM((rows, out_weight.shape[0]), bf16),
            pltpu.VMEM((U_DEV, 2, 2 * HD), f32),
            pltpu.VMEM((3, pages_dev), i32),
            dma((3,)),
        ],
        compiler_params=pltpu.CompilerParams(
            collective_id=0, has_side_effects=True, vmem_limit_bytes=44 << 20
        ),
        name="layer",
    )(*[pltpu.with_memory_space_constraint(x, pltpu.HBM) for x in (lengths, unit_table, page_table, hidden_states, qkv_weight, out_weight, cache_pages)])
    mixed_shape = (requests, 2, out_weight.shape[0])
    placed, mixed = pl.pallas_call(
        place_kernel,
        out_shape=(
            jax.ShapeDtypeStruct(cache_pages.shape, bf16),
            jax.ShapeDtypeStruct(mixed_shape, bf16),
        ),
        in_specs=[vmem, vmem, vmem, vmem],
        out_specs=(hbm, hbm),
        scratch_shapes=[
            pltpu.VMEM((U_DEV, 2) + cache_pages.shape[1:], bf16),
            pltpu.VMEM(mixed_shape, bf16),
            dma(()), dma(()),
        ],
        compiler_params=pltpu.CompilerParams(vmem_limit_bytes=8 << 20),
        name="place_pages",
    )(place, arrived, fresh, mixed)
    return (mixed, placed)


def body(hidden_states, qkv_weight, out_weight, cache_pages, context_lengths, new_units, old_pages):
    devices = lax.axis_size("tp")
    whole_heads = qkv_weight.shape[0] % HD == 0 and out_weight.shape[0] % HD == 0
    pages_dev = cache_pages.shape[0]
    whole_shares = pages_dev % devices == 0 and devices % 4 == 0 and hidden_states.shape[0] == KVH
    whole_shares = whole_shares and new_units.shape[0] == pages_dev and PAGE % pages_dev == 0
    chosen = fused_body if whole_heads and whole_shares else plain_body
    return chosen(
        hidden_states, qkv_weight, out_weight, cache_pages, context_lengths, new_units, old_pages
    )


def solution(mesh):
    in_specs = (
        P("group", None, None),
        P("tp", None),
        P("tp", None),
        P(("group", "tp"), None, None),
        P("group"),
        P("group"),
        P("group"),
    )
    out_specs = (P("group", None, "tp"), P(("group", "tp"), None, None))
    return jax.shard_map(body, mesh=mesh, in_specs=in_specs, out_specs=out_specs, check_vma=False)
```

```python
import math

import jax
import jax.numpy as jnp
from jax import lax
from jax.experimental import pallas as pl
from jax.experimental.pallas import tpu as pltpu
from jax.sharding import PartitionSpec as P

D = 8192
HEADS = 64
KVH = 8
HD = 128
U_DEV = 4
MAXCTX = 2048
PAGE = 128


rope_base = 10000.0


def rotate_positions(values, positions):
    half_dim = values.shape[-1] // 2
    frequency = rope_base ** (-(jnp.arange(half_dim, dtype=jnp.float32) * 2.0 / values.shape[-1]))
    angles = positions.astype(jnp.float32)[..., None] * frequency
    cosine = jnp.concatenate([jnp.cos(angles), jnp.cos(angles)], axis=-1)
    sine_table = jnp.concatenate([jnp.sin(angles), jnp.sin(angles)], axis=-1)
    turned = jnp.concatenate([-values[..., half_dim:], values[..., :half_dim]], axis=-1)
    return values * cosine + turned * sine_table


def prepare(unit_qkv, base_lengths):
    group_count = HEADS // KVH
    count_units = unit_qkv.shape[0]
    positions = base_lengths[:, None] + jnp.arange(2, dtype=jnp.int32)[None, :]
    widened = unit_qkv.astype(jnp.float32)
    queries = widened[..., : group_count * HD].reshape(count_units, 2, group_count, HD)
    queries = rotate_positions(queries, positions[:, :, None]).astype(jnp.bfloat16)
    new_keys = rotate_positions(
        widened[..., group_count * HD : (group_count + 1) * HD], positions
    ).astype(jnp.bfloat16)
    new_values = unit_qkv[..., (group_count + 1) * HD :]
    return (queries, new_keys, new_values)


def context_terms(context, queries, valid_count):
    score_scale = 1.0 / math.sqrt(HD)
    cached_keys = context[..., :HD]
    cached_values = context[..., HD:]
    scores = (
        jnp.einsum("psgd,ptd->psgt", queries, cached_keys, preferred_element_type=jnp.float32)
        * score_scale
    )
    visible = jnp.arange(context.shape[1], dtype=jnp.int32)[None, :] < valid_count[:, None]
    weights = jnp.where(visible[:, None, None, :], jnp.exp(scores), 0.0)
    totals = jnp.sum(weights, axis=-1)
    weighted = jnp.einsum(
        "psgt,ptd->psgd",
        weights.astype(jnp.bfloat16),
        cached_values,
        preferred_element_type=jnp.float32,
    )
    return (weighted, totals)


def own_terms(queries, new_keys, new_values):
    score_scale = 1.0 / math.sqrt(HD)
    scores = (
        jnp.einsum("usgd,ujd->usgj", queries, new_keys, preferred_element_type=jnp.float32)
        * score_scale
    )
    recent = jnp.arange(2, dtype=jnp.int32)[None, :] <= jnp.arange(2, dtype=jnp.int32)[:, None]
    weights = jnp.where(recent[None, :, None, :], jnp.exp(scores), 0.0)
    totals = jnp.sum(weights, axis=-1)
    weighted = jnp.einsum(
        "usgj,ujd->usgd",
        weights.astype(jnp.bfloat16),
        new_values,
        preferred_element_type=jnp.float32,
    )
    return (weighted, totals)


def plain_body(hidden_states, qkv_weight, out_weight, cache_pages, context_lengths, new_units, old_pages):
    devices = lax.axis_size("tp")
    device = lax.axis_index("tp")
    requests = hidden_states.shape[0]
    rows_dev = qkv_weight.shape[0]
    pages_dev, page_rows, page_width = cache_pages.shape
    group_count = HEADS // KVH
    unit_rows = (group_count + 2) * HD
    per_unit = MAXCTX // PAGE
    unit_slots = U_DEV
    capacity = max(1, pages_dev // devices)
    total_units = new_units.shape[0]
    total_pages = old_pages.shape[0]
    flat_rows = hidden_states.reshape(requests * 2, D)
    partial_qkv = lax.dot_general(
        flat_rows, qkv_weight, (((1,), (1,)), ((), ())), preferred_element_type=jnp.float32
    )
    partial_qkv = partial_qkv.astype(jnp.bfloat16).reshape(requests, 2, rows_dev)
    slot_index = (
        jnp.zeros((total_units,), jnp.int32)
        .at[new_units]
        .set(jnp.arange(total_units, dtype=jnp.int32))
    )
    own_units = lax.dynamic_slice_in_dim(new_units, device * unit_slots, unit_slots)
    own_requests = own_units // KVH
    own_heads = own_units % KVH
    own_lengths = context_lengths[own_requests]
    local_ids = lax.dynamic_slice_in_dim(old_pages, device * pages_dev, pages_dev)
    local_units = local_ids // per_unit
    local_index = local_ids % per_unit
    target_dev = (slot_index[local_units] * per_unit + local_index) // pages_dev
    local_order = jnp.arange(pages_dev, dtype=jnp.int32)
    send_rank = jnp.sum(
        (
            (target_dev[:, None] == target_dev[None, :])
            & (local_order[None, :] < local_order[:, None])
        ).astype(jnp.int32),
        axis=1,
    )
    outgoing = (
        jnp.zeros((devices, capacity, page_rows, page_width), jnp.bfloat16)
        .at[target_dev, send_rank]
        .set(cache_pages)
    )
    arrived = lax.all_to_all(outgoing, "tp", split_axis=0, concat_axis=0, tiled=True)
    stored_position = (
        jnp.zeros((total_pages,), jnp.int32)
        .at[old_pages]
        .set(jnp.arange(total_pages, dtype=jnp.int32))
    )
    wanted = (
        own_units[:, None] * per_unit + jnp.arange(per_unit, dtype=jnp.int32)[None, :]
    ).reshape(pages_dev)
    source_pos = stored_position[wanted]
    source_dev = source_pos // pages_dev
    source_slot = source_pos % pages_dev
    arrival_rank = jnp.sum(
        (
            (source_dev[:, None] == source_dev[None, :])
            & (source_slot[None, :] < source_slot[:, None])
        ).astype(jnp.int32),
        axis=1,
    )
    relaid = arrived[source_dev, arrival_rank]
    contexts = relaid.reshape(unit_slots, MAXCTX, page_width)
    sources_per_head = unit_rows // rows_dev
    request_table = (new_units // KVH).reshape(devices, unit_slots)
    outgoing_rows = partial_qkv[request_table]
    incoming = lax.all_to_all(outgoing_rows, "tp", split_axis=0, concat_axis=0, tiled=True)
    grouped = jnp.moveaxis(incoming.reshape(KVH, sources_per_head, unit_slots, 2, rows_dev), 2, 0)
    chosen = jnp.take_along_axis(grouped, own_heads[:, None, None, None, None], axis=1)[:, 0]
    own_rows = chosen.transpose(0, 2, 1, 3).reshape(unit_slots, 2, unit_rows)
    queries, new_keys, new_values = prepare(own_rows, own_lengths)
    cache_sums, cache_totals = context_terms(contexts, queries, own_lengths)
    own_sums, own_totals = own_terms(queries, new_keys, new_values)
    attended = ((cache_sums + own_sums) / (cache_totals + own_totals)[..., None]).astype(
        jnp.bfloat16
    )
    attended = attended.reshape(unit_slots, 2, group_count * HD)
    all_heads = lax.all_gather(attended, "tp", axis=0, tiled=True)
    logical = (
        all_heads[slot_index]
        .reshape(requests, KVH, 2, group_count * HD)
        .transpose(0, 2, 1, 3)
        .reshape(requests * 2, HEADS * HD)
    )
    mixed_rows = lax.dot_general(
        logical, out_weight, (((1,), (1,)), ((), ())), preferred_element_type=jnp.float32
    )
    mixed_rows = mixed_rows.astype(jnp.bfloat16).reshape(requests, 2, out_weight.shape[0])
    fresh_rows = jnp.concatenate([new_keys, new_values], axis=-1)
    positions = jnp.arange(MAXCTX, dtype=jnp.int32)[None, :]
    contexts = jnp.where(
        (positions == own_lengths[:, None])[..., None], fresh_rows[:, 0:1], contexts
    )
    contexts = jnp.where(
        (positions == own_lengths[:, None] + 1)[..., None], fresh_rows[:, 1:2], contexts
    )
    return (mixed_rows, contexts.reshape(pages_dev, page_rows, page_width))


def place_kernel(
    table_ref, arrived_ref, fresh_ref, mixed_ref, out_ref, rows_ref, patched, rows, sem, rows_sem
):
    per_unit = MAXCTX // PAGE
    steps = fresh_ref.shape[1]

    def outward(at, src):
        return pltpu.make_async_copy(src, out_ref.at[at], sem)

    for slot in range(U_DEV):
        for page in range(steps, per_unit):
            k = slot * per_unit + page
            outward(table_ref[0, k], arrived_ref.at[table_ref[1, k]]).start()

    for slot in range(U_DEV):
        for page in range(steps):
            k = slot * per_unit + page
            at = table_ref[0, k]
            block = patched.at[slot, page]
            content = arrived_ref[table_ref[1, k]].astype(jnp.float32)
            line = lax.broadcasted_iota(jnp.int32, content.shape, 0)
            row = jnp.broadcast_to(table_ref[2:3, k : k + 1], content.shape)
            for step in range(steps):
                new = jnp.broadcast_to(fresh_ref[slot, step : step + 1, :], content.shape)
                content = jnp.where(line == row + step, new, content)
            block[...] = content.astype(jnp.bfloat16)
            outward(at, block).start()

    mixed = mixed_ref[...].astype(jnp.float32)
    for r in range(rows.shape[0]):
        rows[r] = mixed[2 * r : 2 * r + 2].astype(jnp.bfloat16)
    rows_out = pltpu.make_async_copy(rows, rows_ref, rows_sem)
    rows_out.start()
    pltpu.make_async_copy(arrived_ref, out_ref, sem).wait()
    rows_out.wait()


NT = (((1,), (1,)), ((), ()))
PLAN = (8,14,18,22,28)
FIRST = 16


def layer_kernel(
    devices, capacity,
    lengths_hbm, units_hbm, ids_hbm, hidden_hbm, qkv_hbm, out_hbm, pages_hbm,
    arrived_hbm, mixed_hbm, fresh_hbm, place_hbm,
    lengths, units_s, units_v, ids, order_v, order, tables_v, table, hidden_in, hidden_wide, hidden_ref, cos_ref, sin_ref,
    qkv_w, out_w, unsorted_head, unsorted_tail, pages, rows_all, spread, queries, new_keys, new_values, part_out, part_in, swap_out, swap_in, att_all, flat,
    load_sem, page_send, page_recv, row_send, row_recv, part_send, part_recv, swap_send, swap_recv, att_send, att_recv,
    small_sem, table_sem, settled, mixed_ref, fresh_ref, place_ref,
):
    me = lax.axis_index("tp")
    pages_dev = pages.shape[0]
    rows = hidden_ref.shape[0]
    requests = rows // 2
    units = requests * KVH
    per_unit = MAXCTX // PAGE
    heads = qkv_w.shape[0]
    tiles = out_w.shape[0]
    group_count = HEADS // KVH
    head_rows = group_count + 2
    score_scale = 1.0 / math.sqrt(HD)
    span = requests * 2 * group_count
    of_query, of_left, of_target, of_slot = range(4)

    half, quarter = devices // 2, devices // 4
    here, side = lax.rem(me, half), me // half
    partner = lax.rem(me + half, devices)

    def near(offset):
        return side * half + lax.rem(here + offset, half)

    def far(turn):
        return (1 - side) * half + (turn // quarter) * quarter + lax.rem(turn + me + 1, quarter)

    def remote(src, dst, send, recv, device):
        return pltpu.make_async_remote_copy(
            src_ref=src, dst_ref=dst, send_sem=send, recv_sem=recv,
            device_id={"tp": device}, device_id_type=pl.DeviceIdType.MESH,
        )

    def page_copy(rank, device, start=0, size=PAGE):
        return remote(
            pages.at[device * capacity + rank, pl.ds(start, size)],
            arrived_hbm.at[me * capacity + rank, pl.ds(start, size)],
            page_send, page_recv, device,
        )

    def row_copy(kind, owner, device):
        block = rows_all.at[owner]
        return remote(block, block, row_send, row_recv.at[kind], device)

    def many_rows(count):
        blocks = rows_all.at[pl.ds(0, count)]
        return remote(blocks, blocks, row_send, row_recv.at[1], partner)

    def att_copy(device):
        block = att_all.at[here]
        return remote(block, block, att_send, att_recv, device)

    def many_att(count):
        blocks = att_all.at[pl.ds(0, count)]
        return remote(blocks, blocks, att_send, att_recv, partner)

    def part_copy(src, dst, device):
        return remote(part_out.at[src], part_in.at[dst], part_send, part_recv, device)

    def many_parts(count):
        return remote(
            part_out.at[pl.ds(0, count)], part_in.at[pl.ds(0, count)], part_send, part_recv, partner
        )

    def swap_copy():
        return remote(swap_out, swap_in, swap_send, swap_recv, partner)

    turns = half * capacity

    def turn_of(turn):
        rank, place = turn // half, lax.rem(turn, half)
        if capacity == 1:
            return rank, place
        head = turn < 2 * half
        rank = jnp.where(head, lax.rem(turn // quarter, 2), rank)
        return rank, jnp.where(head, turn // half * quarter + lax.rem(turn, quarter), place)

    def send_far(start, stop, *part):
        @pl.loop(start, stop)
        def _(turn):
            rank, place = turn_of(turn)
            page_copy(rank, far(place), *part).start()

    def send_near(start, stop):
        @pl.loop(start, stop)
        def _(turn):
            rank, place = turn_of(turn)

            @pl.when(place > 0)
            def _():
                page_copy(rank, near(place)).start()

    def send_pages(start, stop):
        @pl.loop(start, stop)
        def _(turn):
            send_far(turn, turn + 1)
            send_near(turn, turn + 1)

    def share(numerator):
        return turns * numerator // 32

    def pack_totals(values):
        strip = PAGE // len(values)
        packed = jnp.zeros((2 * group_count, PAGE), jnp.float32)
        for j, total in enumerate(values):
            top = total.astype(jnp.bfloat16).astype(jnp.float32)
            packed = jnp.where(lane == j * strip, top, packed)
            packed = jnp.where(lane == j * strip + strip // 2, total - top, packed)
        return packed.astype(jnp.bfloat16)

    def unpack_total(packed, j, count=U_DEV):
        return jnp.sum(jnp.where(lane // (PAGE // count) == j, packed, 0.0), axis=-1, keepdims=True)

    lane = lax.broadcasted_iota(jnp.int32, (2 * group_count, PAGE), 1)

    small = [
        pltpu.make_async_copy(ids_hbm, ids, small_sem.at[0]),
        pltpu.make_async_copy(units_hbm, units_v, small_sem.at[1]),
        pltpu.make_async_copy(units_hbm, units_s, small_sem.at[2]),
        pltpu.make_async_copy(lengths_hbm, lengths, small_sem.at[3]),
    ]
    load_pages = [
        pltpu.make_async_copy(
            pages_hbm.at[:, pl.ds(start, part.shape[1])], part, small_sem.at[sem]
        )
        for start, part, sem in ((0, unsorted_head, 4), (FIRST, unsorted_tail, 6))
    ]
    load_hidden = pltpu.make_async_copy(hidden_hbm, hidden_in, small_sem.at[5])
    loads = [
        pltpu.make_async_copy(qkv_hbm.at[pl.ds(c * HD, HD)], qkv_w.at[c], load_sem.at[c])
        for c in range(heads)
    ]
    loads += [
        pltpu.make_async_copy(
            out_hbm.at[pl.ds(c * HD, HD)], out_w.at[c], load_sem.at[c]
        )
        for c in range(tiles)
    ]
    for load in small + load_pages:
        load.start()

    barrier = pltpu.get_barrier_semaphore()

    def greet(semaphore, device):
        pl.semaphore_signal(
            semaphore, inc=1, device_id={"tp": device}, device_id_type=pl.DeviceIdType.MESH
        )

    @pl.when(side == 0)
    def _():
        @pl.loop(half, devices)
        def _(device):
            greet(barrier, device)

    @pl.when(me // quarter == 2)
    def _():
        @pl.loop(0, half)
        def _(device):
            greet(barrier, half - 1 - device)

    def numbers(shape, axis):
        return lax.broadcasted_iota(jnp.int32, shape, axis)

    def whole(values, size):
        return lax.shift_right_logical(values, jnp.full_like(values, size.bit_length() - 1))

    def index_row(values, size):
        return jnp.clip(values, 0, size - 1)

    def down(hit, values):
        return jnp.sum(jnp.where(hit, values, 0), axis=0, keepdims=True)

    def across(hit, values):
        return jnp.sum(jnp.where(hit, values, 0), axis=1, keepdims=True)

    square = (pages_dev, pages_dev)
    k_sub, k_lane = numbers(square, 0), numbers(square, 1)
    small[0].wait()
    first = me * pages_dev
    wide = (pages_dev, ids.shape[1])
    own_ids = ids[pl.ds(first // ids.shape[1], 1), :]
    mine = numbers(wide, 1) == numbers(wide, 0) + lax.rem(first, ids.shape[1])
    id_col = across(mine, own_ids)
    small[1].wait()
    unit_row = units_v[...]
    by_unit = (pages_dev, units)
    slot_col = across(whole(id_col, per_unit) == unit_row, numbers(by_unit, 1))
    target_col = whole(slot_col, U_DEV)
    target_row = down(k_sub == k_lane, target_col)
    rank_col = across((target_col == target_row) & (k_lane < k_sub), jnp.ones(square, jnp.int32))
    sent = target_col * capacity + rank_col == k_lane
    order_v[...] = index_row(down(sent, k_sub), pages_dev)
    to_order = pltpu.make_async_copy(order_v, order, table_sem.at[1])
    to_order.start()
    def sort_page(at, head=True, tail=True, source=None):
        source = order[0, at] if source is None else source
        if head:
            pages[at, pl.ds(0, FIRST)] = unsorted_head[source]
        if tail:
            pages[at, pl.ds(FIRST, PAGE - FIRST)] = unsorted_tail[source]

    def sort_far(start, stop, *part):
        @pl.loop(start, stop)
        def _(turn):
            rank, place = turn_of(turn)
            sort_page(far(place) * capacity + rank, *part)

    def sort_near(start, stop):
        @pl.loop(start, stop)
        def _(turn):
            rank, place = turn_of(turn)
            sort_page(near(place) * capacity + rank)

    early = min(share(PLAN[0]), min(capacity, 2) * quarter)
    load_pages[0].wait()
    order_row = index_row(down(sent, k_sub), pages_dev)
    for turn in range(early):
        rank, place = turn_of(turn)
        at = far(place) * capacity + rank
        sort_page(at, True, False, jnp.sum(jnp.where(k_lane[0:1] == at, order_row, 0)))
    pl.semaphore_wait(barrier, jnp.where(side == 0, quarter, half))
    send_far(0, early, 0, FIRST)
    load_pages[1].wait()
    to_order.wait()
    sort_far(0, early, False, True)
    send_far(0, early, FIRST, PAGE - FIRST)
    id_row = down(sent, id_col)
    tables_v[of_target : of_target + 1, :] = down(sent, slot_col - target_col * U_DEV)
    sent_unit = whole(id_row, per_unit)
    sent_request = whole(sent_unit, KVH)
    small[3].wait()
    sent_length = jnp.zeros_like(id_row)
    for r in range(requests):
        sent_length = jnp.where(sent_request == r, lengths[0, r], sent_length)
    tables_v[of_query : of_query + 1, :] = index_row(
        (sent_unit - sent_request * KVH) * requests + sent_request, units
    )
    tables_v[of_left : of_left + 1, :] = sent_length - (id_row - sent_unit * per_unit) * PAGE
    u_square = (units, units)
    u_sub, u_lane = numbers(u_square, 0), numbers(u_square, 1)
    unit_col = across(u_sub == u_lane, unit_row)
    u_device = whole(u_sub, U_DEV)
    u_side = whole(u_device, half)
    u_place = (u_device - u_side * half) * (2 * U_DEV) + u_side * U_DEV + (u_sub - u_device * U_DEV)
    tables_v[of_slot : of_slot + 1, :] = index_row(down(unit_col == u_lane, u_place), units)
    to_table = pltpu.make_async_copy(tables_v, table, table_sem.at[0])
    to_table.start()

    for load in [load_hidden] + loads[:heads]:
        load.start()

    @pl.when(side == 1)
    def _():
        @pl.loop(0, half)
        def _(device):
            greet(settled, device)

    sort_near(0, early)
    sort_far(early, turns)
    sort_near(early, turns)
    to_table.wait()

    small[2].wait()
    row_at = lax.broadcasted_iota(jnp.int32, (rows, HD), 0)
    lane_at = lax.broadcasted_iota(jnp.int32, (rows, HD), 1)
    positions = jnp.zeros((rows, HD), jnp.float32)
    for r in range(requests):
        positions = jnp.where(row_at // 2 == r, lengths[0, r].astype(jnp.float32), positions)
    positions = positions + (row_at % 2).astype(jnp.float32)
    power = (lane_at % (HD // 2)).astype(jnp.float32) * (2.0 / HD)
    angles = positions * jnp.exp(power * -math.log(rope_base))
    cos_ref[...] = jnp.cos(angles)
    sin_ref[...] = jnp.where(lane_at < HD // 2, -jnp.sin(angles), jnp.sin(angles))
    load_hidden.wait()
    for r in range(requests):
        hidden_wide[2 * r : 2 * r + 2, :] = hidden_in[r].astype(jnp.float32)
    hidden_ref[...] = hidden_wide[...].astype(jnp.bfloat16)

    @pl.when(side == 0)
    def _():
        pl.semaphore_wait(settled, half)
        greet(settled, partner)

    for c in range(heads):
        loads[c].wait()
        part = lax.dot_general(
            hidden_ref[...], qkv_w[c], NT, preferred_element_type=jnp.float32
        ).astype(jnp.bfloat16).astype(jnp.float32)
        turned = part * cos_ref[...] + pltpu.roll(part, HD // 2, 1) * sin_ref[...]
        is_value = lax.rem(me * heads + c, head_rows) == head_rows - 1
        rows_all[me, c] = jnp.where(is_value, part, turned).astype(jnp.bfloat16)

    row_copy(0, me, partner).start()

    @pl.when(side == 1)
    def _():
        pl.semaphore_wait(settled, 1)

    @pl.loop(1, half)
    def _(offset):
        row_copy(1, me, near(offset)).start()

    late = share(PLAN[1]) - early

    @pl.loop(0, late)
    def _(turn):
        send_far(early + turn, early + turn + 1)
        send_near(turn * early // late, (turn + 1) * early // late)

    send_near(early, share(PLAN[1]))
    for load in loads[heads:]:
        load.start()
    own_pages = pltpu.make_async_copy(
        pages.at[pl.ds(me * capacity, capacity)],
        arrived_hbm.at[pl.ds(me * capacity, capacity)],
        page_recv,
    )
    own_pages.start()

    row_copy(0, partner, partner).wait_recv()

    @pl.loop(1, half)
    def _(offset):
        row_copy(1, partner, near(offset)).start()

    send_pages(share(PLAN[1]), share(PLAN[2]))

    many_rows(devices - 2).wait_recv()

    for h in range(KVH):
        for g in range(group_count):
            at = h * head_rows + g
            spread[pl.ds(h * span + g, rows, stride=group_count), :] = rows_all[
                at // heads, at % heads
            ].astype(jnp.float32)
        at = h * head_rows + group_count
        new_keys[h] = rows_all[at // heads, at % heads]
        new_values[h] = rows_all[(at + 1) // heads, (at + 1) % heads]
        for r in range(requests):
            start = h * span + r * 2 * group_count
            queries[h * requests + r] = spread[start : start + 2 * group_count, :].astype(
                jnp.bfloat16
            )

    @pl.loop(0, devices)
    def _(target):
        spent = share(PLAN[3]) - share(PLAN[2])
        send_pages(
            share(PLAN[2]) + target * spent // devices,
            share(PLAN[2]) + (target + 1) * spent // devices,
        )
        zero = jnp.zeros((2 * group_count, PAGE), jnp.float32)
        sums, totals = [zero] * U_DEV, [zero[:, :1]] * U_DEV
        places = [target * capacity + rank for rank in range(capacity)]
        scores = [
            lax.dot_general(
                queries[table[of_query, at]], pages[at, :, :HD], NT, preferred_element_type=jnp.float32
            ) * score_scale
            for at in places
        ]
        weights = [
            jnp.where(lane < table[of_left, at], jnp.exp(score), 0.0)
            for at, score in zip(places, scores)
        ]
        weighted = [
            jnp.dot(weight.astype(jnp.bfloat16), pages[at, :, HD:], preferred_element_type=jnp.float32)
            for at, weight in zip(places, weights)
        ]
        for at, weight, added in zip(places, weights, weighted):
            slot, total = table[of_target, at], jnp.sum(weight, axis=-1, keepdims=True)
            for j in range(U_DEV):
                sums[j] = sums[j] + jnp.where(slot == j, added, 0.0)
                totals[j] = totals[j] + jnp.where(slot == j, total, 0.0)
        place, which = lax.rem(target, half), target // half
        for j in range(U_DEV):
            part_out[place, which, j] = sums[j].astype(jnp.bfloat16)
        part_out[place, which, U_DEV] = pack_totals(totals)

    @pl.loop(1, half)
    def _(offset):
        part_copy(lax.rem(here + offset, half), here, near(offset)).start()

    own_sums, own_totals = [], []
    row = lax.broadcasted_iota(jnp.int32, (2 * group_count, rows), 0)
    col = lax.broadcasted_iota(jnp.int32, (2 * group_count, rows), 1)
    line = lax.broadcasted_iota(jnp.int32, (rows, HD), 0)
    for j in range(2 * U_DEV):
        unit = units_s[0, (j // U_DEV * half + here) * U_DEV + j % U_DEV]
        request, head = unit // KVH, unit % KVH
        scores = lax.dot_general(
            queries[head * requests + request], new_keys[head], NT, preferred_element_type=jnp.float32
        ) * score_scale
        seen = (col // 2 == request) & (col % 2 <= row // group_count)
        weights = jnp.where(seen, jnp.exp(scores), 0.0)
        own_totals.append(jnp.sum(weights, axis=-1, keepdims=True))
        own_sums.append(
            jnp.dot(weights.astype(jnp.bfloat16), new_values[head], preferred_element_type=jnp.float32)
        )
    for j in range(U_DEV):
        unit = units_s[0, me * U_DEV + j]
        request, head = unit // KVH, unit % KVH
        for step in range(2):
            mine = line == request * 2 + step
            for part, kind in ((0, new_keys[head]), (1, new_values[head])):
                fresh_ref[j, step : step + 1, part * HD : (part + 1) * HD] = jnp.sum(
                    jnp.where(mine, kind.astype(jnp.float32), 0.0), axis=0, keepdims=True
                )

    slot_at = numbers((pages_dev, 1), 0)
    wanted = jnp.zeros((pages_dev, 1), jnp.int32)
    for j in range(U_DEV):
        first_page = units_s[0, me * U_DEV + j] * per_unit - j * per_unit
        wanted = jnp.where(whole(slot_at, per_unit) == j, slot_at + first_page, wanted)
    found = jnp.zeros(wide, jnp.int32)
    for b in range(ids.shape[0]):
        found = found + jnp.where(
            wanted == ids[b : b + 1, :], numbers(wide, 1) + b * wide[1], 0
        )
    source_col = jnp.sum(found, axis=1, keepdims=True)
    source_row = down(k_sub == k_lane, source_col)
    holder_col, holder_row = whole(source_col, pages_dev), whole(source_row, pages_dev)
    rank_col = across(
        (holder_col == holder_row) & (source_row < source_col), jnp.ones(square, jnp.int32)
    )
    arrives_col = jnp.clip(holder_col * capacity + rank_col, 0, pages_dev - 1)
    lane_row = numbers((1, pages_dev), 1)
    slot_row = whole(lane_row, per_unit)
    own_lengths = jnp.zeros((1, pages_dev), jnp.int32)
    for j in range(U_DEV):
        own_lengths = jnp.where(
            slot_row == j, lengths[0, units_s[0, me * U_DEV + j] // KVH], own_lengths
        )
    turned = whole(own_lengths, PAGE) + lane_row - slot_row * per_unit
    turned = turned - whole(turned, per_unit) * per_unit
    place_row = slot_row * per_unit + turned
    place_ref[0:1, :] = place_row
    place_ref[1:2, :] = down(k_sub == place_row, arrives_col)
    place_ref[2:3, :] = own_lengths - turned * PAGE

    many_parts(half - 1).wait_recv()

    def half_sum(which):
        def add(offset, carry):
            block = part_in.at[lax.rem(here + offset, half), which]
            return tuple(c + block[j].astype(jnp.float32) for j, c in enumerate(carry))

        first = tuple(
            part_out[here, which, j].astype(jnp.float32) for j in range(U_DEV + 1)
        )
        return lax.fori_loop(1, half, add, first)

    halves = [half_sum(0), half_sum(1)]
    kept = [block for halved in halves for block in halved[:U_DEV]]
    kept_totals = [unpack_total(halved[U_DEV], j) for halved in halves for j in range(U_DEV)]
    for j in range(2 * U_DEV):
        swap_out[j] = kept[j].astype(jnp.bfloat16)
    swap_out[2 * U_DEV] = pack_totals(kept_totals)
    swap_copy().start()
    send_pages(share(PLAN[3]), share(PLAN[4]))
    swap_copy().wait_recv()
    packed = swap_in[2 * U_DEV].astype(jnp.float32)
    for j in range(2 * U_DEV):
        total = own_totals[j] + kept_totals[j] + unpack_total(packed, j, 2 * U_DEV)
        weighted = own_sums[j] + kept[j] + swap_in[j].astype(jnp.float32)
        att_all[here, j] = (weighted / total).astype(jnp.bfloat16)

    @pl.loop(1, half)
    def _(offset):
        att_copy(near(offset)).start()

    send_pages(share(PLAN[4]), turns)
    many_att(half - 1).wait_recv()

    for r in range(requests):
        for h in range(KVH):
            slot = table[of_slot, r * KVH + h]
            spread[h * span + r * 2 * group_count : h * span + (r + 1) * 2 * group_count, :] = (
                att_all[slot // (2 * U_DEV), slot % (2 * U_DEV)].astype(jnp.float32)
            )
    for h in range(KVH):
        for g in range(group_count):
            at = (h * group_count + g) * HD
            flat[:, at : at + HD] = spread[
                pl.ds(h * span + g, rows, stride=group_count), :
            ].astype(jnp.bfloat16)
    for c in range(tiles):
        loads[heads + c].wait()
        mixed_ref[:, c * HD : (c + 1) * HD] = lax.dot_general(
            flat[...], out_w[c], NT, preferred_element_type=jnp.float32
        ).astype(jnp.bfloat16)

    results = [
        pltpu.make_async_copy(src, dst, small_sem.at[i])
        for i, (src, dst) in enumerate(
            ((mixed_ref, mixed_hbm), (fresh_ref, fresh_hbm), (place_ref, place_hbm))
        )
    ]
    for result in results:
        result.start()
    for result in results:
        result.wait()
    remote(arrived_hbm, arrived_hbm, page_send, page_recv, partner).wait_recv()
    sent_pages = pages.at[pl.ds(0, (devices - 1) * capacity)]
    remote(sent_pages, sent_pages, page_send, page_recv, partner).wait_send()
    many_rows(devices - 1).wait_send()
    many_parts(half - 1).wait_send()
    swap_copy().wait_send()
    many_att(half - 1).wait_send()


def fused_body(hidden_states, qkv_weight, out_weight, cache_pages, context_lengths, new_units, old_pages):
    devices = lax.axis_size("tp")
    requests = hidden_states.shape[0]
    rows = requests * 2
    pages_dev = cache_pages.shape[0]
    capacity = pages_dev // devices
    heads = qkv_weight.shape[0] // HD
    tiles = out_weight.shape[0] // HD
    group_count = HEADS // KVH
    units = new_units.shape[0]
    hbm = pl.BlockSpec(memory_space=pl.ANY)
    vmem = pl.BlockSpec(memory_space=pltpu.VMEM)
    smem = pl.BlockSpec(memory_space=pltpu.SMEM)
    dma = pltpu.SemaphoreType.DMA
    lengths = context_lengths.reshape(1, requests)
    unit_table = new_units.reshape(1, units)
    page_table = old_pages.reshape(-1, PAGE)
    tile = (2 * group_count, HD)
    f32, bf16, i32 = jnp.float32, jnp.bfloat16, jnp.int32
    arrived, mixed, fresh, place = pl.pallas_call(
        lambda *refs: layer_kernel(devices, capacity, *refs),
        out_shape=(
            jax.ShapeDtypeStruct(cache_pages.shape, bf16),
            jax.ShapeDtypeStruct((rows, out_weight.shape[0]), bf16),
            jax.ShapeDtypeStruct((U_DEV, 2, 2 * HD), f32),
            jax.ShapeDtypeStruct((3, pages_dev), i32),
        ),
        in_specs=[pl.BlockSpec(memory_space=pltpu.HBM)] * 7,
        out_specs=(hbm, hbm, hbm, hbm),
        scratch_shapes=[
            pltpu.SMEM(lengths.shape, i32),
            pltpu.SMEM(unit_table.shape, i32),
            pltpu.VMEM(unit_table.shape, i32),
            pltpu.VMEM(page_table.shape, i32),
            pltpu.VMEM((1, pages_dev), i32),
            pltpu.SMEM((1, pages_dev), i32),
            pltpu.VMEM((8, pages_dev), i32),
            pltpu.SMEM((8, pages_dev), i32),
            pltpu.VMEM(hidden_states.shape, bf16),
            pltpu.VMEM((rows, D), f32),
            pltpu.VMEM((rows, D), bf16),
            pltpu.VMEM((rows, HD), f32),
            pltpu.VMEM((rows, HD), f32),
            pltpu.VMEM((heads, HD, D), bf16),
            pltpu.VMEM((tiles, HD, HEADS * HD), bf16),
            pltpu.VMEM((pages_dev, FIRST, 2 * HD), bf16),
            pltpu.VMEM((pages_dev, PAGE - FIRST, 2 * HD), bf16),
            pltpu.VMEM(cache_pages.shape, bf16),
            pltpu.VMEM((devices, heads, rows, HD), bf16),
            pltpu.VMEM((units * 2 * group_count, HD), f32),
            pltpu.VMEM((units,) + tile, bf16),
            pltpu.VMEM((KVH, rows, HD), bf16),
            pltpu.VMEM((KVH, rows, HD), bf16),
            pltpu.VMEM((devices // 2, 2, U_DEV + 1) + tile, bf16),
            pltpu.VMEM((devices // 2, 2, U_DEV + 1) + tile, bf16),
            pltpu.VMEM((2 * U_DEV + 1,) + tile, bf16),
            pltpu.VMEM((2 * U_DEV + 1,) + tile, bf16),
            pltpu.VMEM((devices // 2, 2 * U_DEV) + tile, bf16),
            pltpu.VMEM((rows, HEADS * HD), bf16),
            dma((max(heads, tiles),)),
            dma(()), dma(()),
            dma(()), dma((2,)),
            dma(()), dma(()), dma(()), dma(()),
            dma(()), dma(()),
            dma((7,)), dma((2,)), pltpu.SemaphoreType.REGULAR,
            pltpu.VMEM((rows, out_weight.shape[0]), bf16),
            pltpu.VMEM((U_DEV, 2, 2 * HD), f32),
            pltpu.VMEM((3, pages_dev), i32),
        ],
        compiler_params=pltpu.CompilerParams(
            collective_id=0, has_side_effects=True, vmem_limit_bytes=44 << 20
        ),
        name="layer",
    )(*[pltpu.with_memory_space_constraint(x, pltpu.HBM) for x in (lengths, unit_table, page_table, hidden_states, qkv_weight, out_weight, cache_pages)])
    mixed_shape = (requests, 2, out_weight.shape[0])
    placed, mixed = pl.pallas_call(
        place_kernel,
        out_shape=(
            jax.ShapeDtypeStruct(cache_pages.shape, bf16),
            jax.ShapeDtypeStruct(mixed_shape, bf16),
        ),
        in_specs=[vmem, vmem, vmem, vmem],
        out_specs=(hbm, hbm),
        scratch_shapes=[
            pltpu.VMEM((U_DEV, 2) + cache_pages.shape[1:], bf16),
            pltpu.VMEM(mixed_shape, bf16),
            dma(()), dma(()),
        ],
        compiler_params=pltpu.CompilerParams(vmem_limit_bytes=8 << 20),
        name="place_pages",
    )(place, arrived, fresh, mixed)
    return (mixed, placed)


def body(hidden_states, qkv_weight, out_weight, cache_pages, context_lengths, new_units, old_pages):
    devices = lax.axis_size("tp")
    whole_heads = qkv_weight.shape[0] % HD == 0 and out_weight.shape[0] % HD == 0
    pages_dev = cache_pages.shape[0]
    whole_shares = pages_dev % devices == 0 and devices % 4 == 0 and hidden_states.shape[0] == KVH
    whole_shares = whole_shares and new_units.shape[0] == pages_dev and PAGE % pages_dev == 0
    chosen = fused_body if whole_heads and whole_shares else plain_body
    return chosen(
        hidden_states, qkv_weight, out_weight, cache_pages, context_lengths, new_units, old_pages
    )


def solution(mesh):
    in_specs = (
        P("group", None, None),
        P("tp", None),
        P("tp", None),
        P(("group", "tp"), None, None),
        P("group"),
        P("group"),
        P("group"),
    )
    out_specs = (P("group", None, "tp"), P(("group", "tp"), None, None))
    return jax.shard_map(body, mesh=mesh, in_specs=in_specs, out_specs=out_specs, check_vma=False)
```

```python
import math

import jax
import jax.numpy as jnp
from jax import lax
from jax.experimental import pallas as pl
from jax.experimental.pallas import tpu as pltpu
from jax.sharding import PartitionSpec as P

D = 8192
HEADS = 64
KVH = 8
HD = 128
U_DEV = 4
MAXCTX = 2048
PAGE = 128


rope_base = 10000.0


def rotate_positions(values, positions):
    half_dim = values.shape[-1] // 2
    frequency = rope_base ** (-(jnp.arange(half_dim, dtype=jnp.float32) * 2.0 / values.shape[-1]))
    angles = positions.astype(jnp.float32)[..., None] * frequency
    cosine = jnp.concatenate([jnp.cos(angles), jnp.cos(angles)], axis=-1)
    sine_table = jnp.concatenate([jnp.sin(angles), jnp.sin(angles)], axis=-1)
    turned = jnp.concatenate([-values[..., half_dim:], values[..., :half_dim]], axis=-1)
    return values * cosine + turned * sine_table


def prepare(unit_qkv, base_lengths):
    group_count = HEADS // KVH
    count_units = unit_qkv.shape[0]
    positions = base_lengths[:, None] + jnp.arange(2, dtype=jnp.int32)[None, :]
    widened = unit_qkv.astype(jnp.float32)
    queries = widened[..., : group_count * HD].reshape(count_units, 2, group_count, HD)
    queries = rotate_positions(queries, positions[:, :, None]).astype(jnp.bfloat16)
    new_keys = rotate_positions(
        widened[..., group_count * HD : (group_count + 1) * HD], positions
    ).astype(jnp.bfloat16)
    new_values = unit_qkv[..., (group_count + 1) * HD :]
    return (queries, new_keys, new_values)


def context_terms(context, queries, valid_count):
    score_scale = 1.0 / math.sqrt(HD)
    cached_keys = context[..., :HD]
    cached_values = context[..., HD:]
    scores = (
        jnp.einsum("psgd,ptd->psgt", queries, cached_keys, preferred_element_type=jnp.float32)
        * score_scale
    )
    visible = jnp.arange(context.shape[1], dtype=jnp.int32)[None, :] < valid_count[:, None]
    weights = jnp.where(visible[:, None, None, :], jnp.exp(scores), 0.0)
    totals = jnp.sum(weights, axis=-1)
    weighted = jnp.einsum(
        "psgt,ptd->psgd",
        weights.astype(jnp.bfloat16),
        cached_values,
        preferred_element_type=jnp.float32,
    )
    return (weighted, totals)


def own_terms(queries, new_keys, new_values):
    score_scale = 1.0 / math.sqrt(HD)
    scores = (
        jnp.einsum("usgd,ujd->usgj", queries, new_keys, preferred_element_type=jnp.float32)
        * score_scale
    )
    recent = jnp.arange(2, dtype=jnp.int32)[None, :] <= jnp.arange(2, dtype=jnp.int32)[:, None]
    weights = jnp.where(recent[None, :, None, :], jnp.exp(scores), 0.0)
    totals = jnp.sum(weights, axis=-1)
    weighted = jnp.einsum(
        "usgj,ujd->usgd",
        weights.astype(jnp.bfloat16),
        new_values,
        preferred_element_type=jnp.float32,
    )
    return (weighted, totals)


def plain_body(hidden_states, qkv_weight, out_weight, cache_pages, context_lengths, new_units, old_pages):
    devices = lax.axis_size("tp")
    device = lax.axis_index("tp")
    requests = hidden_states.shape[0]
    rows_dev = qkv_weight.shape[0]
    pages_dev, page_rows, page_width = cache_pages.shape
    group_count = HEADS // KVH
    unit_rows = (group_count + 2) * HD
    per_unit = MAXCTX // PAGE
    unit_slots = U_DEV
    capacity = max(1, pages_dev // devices)
    total_units = new_units.shape[0]
    total_pages = old_pages.shape[0]
    flat_rows = hidden_states.reshape(requests * 2, D)
    partial_qkv = lax.dot_general(
        flat_rows, qkv_weight, (((1,), (1,)), ((), ())), preferred_element_type=jnp.float32
    )
    partial_qkv = partial_qkv.astype(jnp.bfloat16).reshape(requests, 2, rows_dev)
    slot_index = (
        jnp.zeros((total_units,), jnp.int32)
        .at[new_units]
        .set(jnp.arange(total_units, dtype=jnp.int32))
    )
    own_units = lax.dynamic_slice_in_dim(new_units, device * unit_slots, unit_slots)
    own_requests = own_units // KVH
    own_heads = own_units % KVH
    own_lengths = context_lengths[own_requests]
    local_ids = lax.dynamic_slice_in_dim(old_pages, device * pages_dev, pages_dev)
    local_units = local_ids // per_unit
    local_index = local_ids % per_unit
    target_dev = (slot_index[local_units] * per_unit + local_index) // pages_dev
    local_order = jnp.arange(pages_dev, dtype=jnp.int32)
    send_rank = jnp.sum(
        (
            (target_dev[:, None] == target_dev[None, :])
            & (local_order[None, :] < local_order[:, None])
        ).astype(jnp.int32),
        axis=1,
    )
    outgoing = (
        jnp.zeros((devices, capacity, page_rows, page_width), jnp.bfloat16)
        .at[target_dev, send_rank]
        .set(cache_pages)
    )
    arrived = lax.all_to_all(outgoing, "tp", split_axis=0, concat_axis=0, tiled=True)
    stored_position = (
        jnp.zeros((total_pages,), jnp.int32)
        .at[old_pages]
        .set(jnp.arange(total_pages, dtype=jnp.int32))
    )
    wanted = (
        own_units[:, None] * per_unit + jnp.arange(per_unit, dtype=jnp.int32)[None, :]
    ).reshape(pages_dev)
    source_pos = stored_position[wanted]
    source_dev = source_pos // pages_dev
    source_slot = source_pos % pages_dev
    arrival_rank = jnp.sum(
        (
            (source_dev[:, None] == source_dev[None, :])
            & (source_slot[None, :] < source_slot[:, None])
        ).astype(jnp.int32),
        axis=1,
    )
    relaid = arrived[source_dev, arrival_rank]
    contexts = relaid.reshape(unit_slots, MAXCTX, page_width)
    sources_per_head = unit_rows // rows_dev
    request_table = (new_units // KVH).reshape(devices, unit_slots)
    outgoing_rows = partial_qkv[request_table]
    incoming = lax.all_to_all(outgoing_rows, "tp", split_axis=0, concat_axis=0, tiled=True)
    grouped = jnp.moveaxis(incoming.reshape(KVH, sources_per_head, unit_slots, 2, rows_dev), 2, 0)
    chosen = jnp.take_along_axis(grouped, own_heads[:, None, None, None, None], axis=1)[:, 0]
    own_rows = chosen.transpose(0, 2, 1, 3).reshape(unit_slots, 2, unit_rows)
    queries, new_keys, new_values = prepare(own_rows, own_lengths)
    cache_sums, cache_totals = context_terms(contexts, queries, own_lengths)
    own_sums, own_totals = own_terms(queries, new_keys, new_values)
    attended = ((cache_sums + own_sums) / (cache_totals + own_totals)[..., None]).astype(
        jnp.bfloat16
    )
    attended = attended.reshape(unit_slots, 2, group_count * HD)
    all_heads = lax.all_gather(attended, "tp", axis=0, tiled=True)
    logical = (
        all_heads[slot_index]
        .reshape(requests, KVH, 2, group_count * HD)
        .transpose(0, 2, 1, 3)
        .reshape(requests * 2, HEADS * HD)
    )
    mixed_rows = lax.dot_general(
        logical, out_weight, (((1,), (1,)), ((), ())), preferred_element_type=jnp.float32
    )
    mixed_rows = mixed_rows.astype(jnp.bfloat16).reshape(requests, 2, out_weight.shape[0])
    fresh_rows = jnp.concatenate([new_keys, new_values], axis=-1)
    positions = jnp.arange(MAXCTX, dtype=jnp.int32)[None, :]
    contexts = jnp.where(
        (positions == own_lengths[:, None])[..., None], fresh_rows[:, 0:1], contexts
    )
    contexts = jnp.where(
        (positions == own_lengths[:, None] + 1)[..., None], fresh_rows[:, 1:2], contexts
    )
    return (mixed_rows, contexts.reshape(pages_dev, page_rows, page_width))


def place_kernel(
    table_ref, arrived_ref, fresh_ref, mixed_ref, out_ref, rows_ref, patched, rows, sem, rows_sem
):
    per_unit = MAXCTX // PAGE
    steps = fresh_ref.shape[1]

    def outward(at, src):
        return pltpu.make_async_copy(src, out_ref.at[at], sem)

    for slot in range(U_DEV):
        for page in range(steps, per_unit):
            k = slot * per_unit + page
            outward(table_ref[0, k], arrived_ref.at[table_ref[1, k]]).start()

    for slot in range(U_DEV):
        for page in range(steps):
            k = slot * per_unit + page
            at = table_ref[0, k]
            block = patched.at[slot, page]
            content = arrived_ref[table_ref[1, k]].astype(jnp.float32)
            line = lax.broadcasted_iota(jnp.int32, content.shape, 0)
            row = jnp.broadcast_to(table_ref[2:3, k : k + 1], content.shape)
            for step in range(steps):
                new = jnp.broadcast_to(fresh_ref[slot, step : step + 1, :], content.shape)
                content = jnp.where(line == row + step, new, content)
            block[...] = content.astype(jnp.bfloat16)
            outward(at, block).start()

    mixed = mixed_ref[...].astype(jnp.float32)
    for r in range(rows.shape[0]):
        rows[r] = mixed[2 * r : 2 * r + 2].astype(jnp.bfloat16)
    rows_out = pltpu.make_async_copy(rows, rows_ref, rows_sem)
    rows_out.start()
    pltpu.make_async_copy(arrived_ref, out_ref, sem).wait()
    rows_out.wait()


NT = (((1,), (1,)), ((), ()))
PLAN = (8,15,19,23,28)
FIRST = 16


def layer_kernel(
    devices, capacity,
    lengths_hbm, units_hbm, ids_hbm, hidden_hbm, qkv_hbm, out_hbm, pages_hbm,
    arrived_hbm, mixed_hbm, fresh_hbm, place_hbm,
    lengths, units_s, units_v, ids, order_v, order, tables_v, table, hidden_in, hidden_wide, hidden_ref, cos_ref, sin_ref,
    qkv_w, out_w, unsorted_head, unsorted_tail, pages, rows_all, spread, queries, new_keys, new_values, part_out, part_in, swap_out, swap_in, att_all, flat,
    load_sem, page_send, page_recv, row_send, row_recv, part_send, part_recv, swap_send, swap_recv, att_send, att_recv,
    small_sem, table_sem, settled, mixed_ref, fresh_ref, place_ref,
):
    me = lax.axis_index("tp")
    pages_dev = pages.shape[0]
    rows = hidden_ref.shape[0]
    requests = rows // 2
    units = requests * KVH
    per_unit = MAXCTX // PAGE
    heads = qkv_w.shape[0]
    tiles = out_w.shape[0]
    group_count = HEADS // KVH
    head_rows = group_count + 2
    score_scale = 1.0 / math.sqrt(HD)
    span = requests * 2 * group_count
    of_query, of_left, of_target, of_slot = range(4)

    half, quarter = devices // 2, devices // 4
    here, side = lax.rem(me, half), me // half
    partner = lax.rem(me + half, devices)

    def near(offset):
        return side * half + lax.rem(here + offset, half)

    def far(turn):
        return (1 - side) * half + (turn // quarter) * quarter + lax.rem(turn + me + 1, quarter)

    def remote(src, dst, send, recv, device):
        return pltpu.make_async_remote_copy(
            src_ref=src, dst_ref=dst, send_sem=send, recv_sem=recv,
            device_id={"tp": device}, device_id_type=pl.DeviceIdType.MESH,
        )

    def page_copy(rank, device, start=0, size=PAGE):
        return remote(
            pages.at[device * capacity + rank, pl.ds(start, size)],
            arrived_hbm.at[me * capacity + rank, pl.ds(start, size)],
            page_send, page_recv, device,
        )

    def row_copy(kind, owner, device):
        block = rows_all.at[owner]
        return remote(block, block, row_send, row_recv.at[kind], device)

    def many_rows(count):
        blocks = rows_all.at[pl.ds(0, count)]
        return remote(blocks, blocks, row_send, row_recv.at[1], partner)

    def att_copy(device):
        block = att_all.at[here]
        return remote(block, block, att_send, att_recv, device)

    def many_att(count):
        blocks = att_all.at[pl.ds(0, count)]
        return remote(blocks, blocks, att_send, att_recv, partner)

    def part_copy(src, dst, device):
        return remote(part_out.at[src], part_in.at[dst], part_send, part_recv, device)

    def many_parts(count):
        return remote(
            part_out.at[pl.ds(0, count)], part_in.at[pl.ds(0, count)], part_send, part_recv, partner
        )

    def swap_copy():
        return remote(swap_out, swap_in, swap_send, swap_recv, partner)

    turns = half * capacity

    def turn_of(turn):
        rank, place = turn // half, lax.rem(turn, half)
        if capacity == 1:
            return rank, place
        head = turn < 2 * half
        rank = jnp.where(head, lax.rem(turn // quarter, 2), rank)
        return rank, jnp.where(head, turn // half * quarter + lax.rem(turn, quarter), place)

    def send_far(start, stop, *part):
        @pl.loop(start, stop)
        def _(turn):
            rank, place = turn_of(turn)
            page_copy(rank, far(place), *part).start()

    def send_near(start, stop):
        @pl.loop(start, stop)
        def _(turn):
            rank, place = turn_of(turn)

            @pl.when(place > 0)
            def _():
                page_copy(rank, near(place)).start()

    def send_pages(start, stop):
        @pl.loop(start, stop)
        def _(turn):
            send_far(turn, turn + 1)
            send_near(turn, turn + 1)

    def share(numerator):
        return turns * numerator // 32

    def pack_totals(values):
        strip = PAGE // len(values)
        packed = jnp.zeros((2 * group_count, PAGE), jnp.float32)
        for j, total in enumerate(values):
            top = total.astype(jnp.bfloat16).astype(jnp.float32)
            packed = jnp.where(lane == j * strip, top, packed)
            packed = jnp.where(lane == j * strip + strip // 2, total - top, packed)
        return packed.astype(jnp.bfloat16)

    def unpack_total(packed, j, count=U_DEV):
        return jnp.sum(jnp.where(lane // (PAGE // count) == j, packed, 0.0), axis=-1, keepdims=True)

    lane = lax.broadcasted_iota(jnp.int32, (2 * group_count, PAGE), 1)

    small = [
        pltpu.make_async_copy(ids_hbm, ids, small_sem.at[0]),
        pltpu.make_async_copy(units_hbm, units_v, small_sem.at[1]),
        pltpu.make_async_copy(units_hbm, units_s, small_sem.at[2]),
        pltpu.make_async_copy(lengths_hbm, lengths, small_sem.at[3]),
    ]
    load_pages = [
        pltpu.make_async_copy(
            pages_hbm.at[:, pl.ds(start, part.shape[1])], part, small_sem.at[sem]
        )
        for start, part, sem in ((0, unsorted_head, 4), (FIRST, unsorted_tail, 6))
    ]
    load_hidden = pltpu.make_async_copy(hidden_hbm, hidden_in, small_sem.at[5])
    loads = [
        pltpu.make_async_copy(qkv_hbm.at[pl.ds(c * HD, HD)], qkv_w.at[c], load_sem.at[c])
        for c in range(heads)
    ]
    loads += [
        pltpu.make_async_copy(
            out_hbm.at[pl.ds(c * HD, HD)], out_w.at[c], load_sem.at[c]
        )
        for c in range(tiles)
    ]
    for load in small + load_pages:
        load.start()

    barrier = pltpu.get_barrier_semaphore()

    def greet(semaphore, device):
        pl.semaphore_signal(
            semaphore, inc=1, device_id={"tp": device}, device_id_type=pl.DeviceIdType.MESH
        )

    @pl.when(side == 0)
    def _():
        @pl.loop(half, devices)
        def _(device):
            greet(barrier, device)

    @pl.when(me // quarter == 2)
    def _():
        @pl.loop(0, half)
        def _(device):
            greet(barrier, half - 1 - device)

    def numbers(shape, axis):
        return lax.broadcasted_iota(jnp.int32, shape, axis)

    def whole(values, size):
        return lax.shift_right_logical(values, jnp.full_like(values, size.bit_length() - 1))

    def index_row(values, size):
        return jnp.clip(values, 0, size - 1)

    def down(hit, values):
        return jnp.sum(jnp.where(hit, values, 0), axis=0, keepdims=True)

    def across(hit, values):
        return jnp.sum(jnp.where(hit, values, 0), axis=1, keepdims=True)

    square = (pages_dev, pages_dev)
    k_sub, k_lane = numbers(square, 0), numbers(square, 1)
    small[0].wait()
    first = me * pages_dev
    wide = (pages_dev, ids.shape[1])
    own_ids = ids[pl.ds(first // ids.shape[1], 1), :]
    mine = numbers(wide, 1) == numbers(wide, 0) + lax.rem(first, ids.shape[1])
    id_col = across(mine, own_ids)
    small[1].wait()
    unit_row = units_v[...]
    by_unit = (pages_dev, units)
    slot_col = across(whole(id_col, per_unit) == unit_row, numbers(by_unit, 1))
    target_col = whole(slot_col, U_DEV)
    target_row = down(k_sub == k_lane, target_col)
    rank_col = across((target_col == target_row) & (k_lane < k_sub), jnp.ones(square, jnp.int32))
    sent = target_col * capacity + rank_col == k_lane
    order_v[...] = index_row(down(sent, k_sub), pages_dev)
    to_order = pltpu.make_async_copy(order_v, order, table_sem.at[1])
    to_order.start()
    def sort_page(at, head=True, tail=True, source=None):
        source = order[0, at] if source is None else source
        if head:
            pages[at, pl.ds(0, FIRST)] = unsorted_head[source]
        if tail:
            pages[at, pl.ds(FIRST, PAGE - FIRST)] = unsorted_tail[source]

    def sort_far(start, stop, *part):
        @pl.loop(start, stop)
        def _(turn):
            rank, place = turn_of(turn)
            sort_page(far(place) * capacity + rank, *part)

    def sort_near(start, stop):
        @pl.loop(start, stop)
        def _(turn):
            rank, place = turn_of(turn)
            sort_page(near(place) * capacity + rank)

    early = min(share(PLAN[0]), min(capacity, 2) * quarter)
    load_pages[0].wait()
    order_row = index_row(down(sent, k_sub), pages_dev)
    for turn in range(early):
        rank, place = turn_of(turn)
        at = far(place) * capacity + rank
        sort_page(at, True, False, jnp.sum(jnp.where(k_lane[0:1] == at, order_row, 0)))
    pl.semaphore_wait(barrier, jnp.where(side == 0, quarter, half))
    send_far(0, early, 0, FIRST)
    load_pages[1].wait()
    to_order.wait()
    sort_far(0, early, False, True)
    send_far(0, early, FIRST, PAGE - FIRST)
    id_row = down(sent, id_col)
    tables_v[of_target : of_target + 1, :] = down(sent, slot_col - target_col * U_DEV)
    sent_unit = whole(id_row, per_unit)
    sent_request = whole(sent_unit, KVH)
    small[3].wait()
    sent_length = jnp.zeros_like(id_row)
    for r in range(requests):
        sent_length = jnp.where(sent_request == r, lengths[0, r], sent_length)
    tables_v[of_query : of_query + 1, :] = index_row(
        (sent_unit - sent_request * KVH) * requests + sent_request, units
    )
    tables_v[of_left : of_left + 1, :] = sent_length - (id_row - sent_unit * per_unit) * PAGE
    u_square = (units, units)
    u_sub, u_lane = numbers(u_square, 0), numbers(u_square, 1)
    unit_col = across(u_sub == u_lane, unit_row)
    u_device = whole(u_sub, U_DEV)
    u_side = whole(u_device, half)
    u_place = (u_device - u_side * half) * (2 * U_DEV) + u_side * U_DEV + (u_sub - u_device * U_DEV)
    tables_v[of_slot : of_slot + 1, :] = index_row(down(unit_col == u_lane, u_place), units)
    to_table = pltpu.make_async_copy(tables_v, table, table_sem.at[0])
    to_table.start()

    for load in [load_hidden] + loads[:heads]:
        load.start()

    @pl.when(side == 1)
    def _():
        @pl.loop(0, half)
        def _(device):
            greet(settled, device)

    sort_near(0, early)
    sort_far(early, turns)
    sort_near(early, turns)
    to_table.wait()

    small[2].wait()
    row_at = lax.broadcasted_iota(jnp.int32, (rows, HD), 0)
    lane_at = lax.broadcasted_iota(jnp.int32, (rows, HD), 1)
    positions = jnp.zeros((rows, HD), jnp.float32)
    for r in range(requests):
        positions = jnp.where(row_at // 2 == r, lengths[0, r].astype(jnp.float32), positions)
    positions = positions + (row_at % 2).astype(jnp.float32)
    power = (lane_at % (HD // 2)).astype(jnp.float32) * (2.0 / HD)
    angles = positions * jnp.exp(power * -math.log(rope_base))
    cos_ref[...] = jnp.cos(angles)
    sin_ref[...] = jnp.where(lane_at < HD // 2, -jnp.sin(angles), jnp.sin(angles))
    load_hidden.wait()
    for r in range(requests):
        hidden_wide[2 * r : 2 * r + 2, :] = hidden_in[r].astype(jnp.float32)
    hidden_ref[...] = hidden_wide[...].astype(jnp.bfloat16)

    @pl.when(side == 0)
    def _():
        pl.semaphore_wait(settled, half)
        greet(settled, partner)

    for c in range(heads):
        loads[c].wait()
        part = lax.dot_general(
            hidden_ref[...], qkv_w[c], NT, preferred_element_type=jnp.float32
        ).astype(jnp.bfloat16).astype(jnp.float32)
        turned = part * cos_ref[...] + pltpu.roll(part, HD // 2, 1) * sin_ref[...]
        is_value = lax.rem(me * heads + c, head_rows) == head_rows - 1
        rows_all[me, c] = jnp.where(is_value, part, turned).astype(jnp.bfloat16)

    row_copy(0, me, partner).start()

    @pl.when(side == 1)
    def _():
        pl.semaphore_wait(settled, 1)

    @pl.loop(1, half)
    def _(offset):
        row_copy(1, me, near(offset)).start()

    late = share(PLAN[1]) - early

    @pl.loop(0, late)
    def _(turn):
        send_far(early + turn, early + turn + 1)
        send_near(turn * early // late, (turn + 1) * early // late)

    send_near(early, share(PLAN[1]))
    for load in loads[heads:]:
        load.start()
    own_pages = pltpu.make_async_copy(
        pages.at[pl.ds(me * capacity, capacity)],
        arrived_hbm.at[pl.ds(me * capacity, capacity)],
        page_recv,
    )
    own_pages.start()

    row_copy(0, partner, partner).wait_recv()

    @pl.loop(1, half)
    def _(offset):
        row_copy(1, partner, near(offset)).start()

    send_pages(share(PLAN[1]), share(PLAN[2]))

    many_rows(devices - 2).wait_recv()

    for h in range(KVH):
        for g in range(group_count):
            at = h * head_rows + g
            spread[pl.ds(h * span + g, rows, stride=group_count), :] = rows_all[
                at // heads, at % heads
            ].astype(jnp.float32)
        at = h * head_rows + group_count
        new_keys[h] = rows_all[at // heads, at % heads]
        new_values[h] = rows_all[(at + 1) // heads, (at + 1) % heads]
        for r in range(requests):
            start = h * span + r * 2 * group_count
            queries[h * requests + r] = spread[start : start + 2 * group_count, :].astype(
                jnp.bfloat16
            )

    @pl.loop(0, devices)
    def _(target):
        spent = share(PLAN[3]) - share(PLAN[2])
        send_pages(
            share(PLAN[2]) + target * spent // devices,
            share(PLAN[2]) + (target + 1) * spent // devices,
        )
        zero = jnp.zeros((2 * group_count, PAGE), jnp.float32)
        sums, totals = [zero] * U_DEV, [zero[:, :1]] * U_DEV
        places = [target * capacity + rank for rank in range(capacity)]
        scores = [
            lax.dot_general(
                queries[table[of_query, at]], pages[at, :, :HD], NT, preferred_element_type=jnp.float32
            ) * score_scale
            for at in places
        ]
        weights = [
            jnp.where(lane < table[of_left, at], jnp.exp(score), 0.0)
            for at, score in zip(places, scores)
        ]
        weighted = [
            jnp.dot(weight.astype(jnp.bfloat16), pages[at, :, HD:], preferred_element_type=jnp.float32)
            for at, weight in zip(places, weights)
        ]
        for at, weight, added in zip(places, weights, weighted):
            slot, total = table[of_target, at], jnp.sum(weight, axis=-1, keepdims=True)
            for j in range(U_DEV):
                sums[j] = sums[j] + jnp.where(slot == j, added, 0.0)
                totals[j] = totals[j] + jnp.where(slot == j, total, 0.0)
        place, which = lax.rem(target, half), target // half
        for j in range(U_DEV):
            part_out[place, which, j] = sums[j].astype(jnp.bfloat16)
        part_out[place, which, U_DEV] = pack_totals(totals)

    @pl.loop(1, half)
    def _(offset):
        part_copy(lax.rem(here + offset, half), here, near(offset)).start()

    own_sums, own_totals = [], []
    row = lax.broadcasted_iota(jnp.int32, (2 * group_count, rows), 0)
    col = lax.broadcasted_iota(jnp.int32, (2 * group_count, rows), 1)
    line = lax.broadcasted_iota(jnp.int32, (rows, HD), 0)
    for j in range(2 * U_DEV):
        unit = units_s[0, (j // U_DEV * half + here) * U_DEV + j % U_DEV]
        request, head = unit // KVH, unit % KVH
        scores = lax.dot_general(
            queries[head * requests + request], new_keys[head], NT, preferred_element_type=jnp.float32
        ) * score_scale
        seen = (col // 2 == request) & (col % 2 <= row // group_count)
        weights = jnp.where(seen, jnp.exp(scores), 0.0)
        own_totals.append(jnp.sum(weights, axis=-1, keepdims=True))
        own_sums.append(
            jnp.dot(weights.astype(jnp.bfloat16), new_values[head], preferred_element_type=jnp.float32)
        )
    for j in range(U_DEV):
        unit = units_s[0, me * U_DEV + j]
        request, head = unit // KVH, unit % KVH
        for step in range(2):
            mine = line == request * 2 + step
            for part, kind in ((0, new_keys[head]), (1, new_values[head])):
                fresh_ref[j, step : step + 1, part * HD : (part + 1) * HD] = jnp.sum(
                    jnp.where(mine, kind.astype(jnp.float32), 0.0), axis=0, keepdims=True
                )

    slot_at = numbers((pages_dev, 1), 0)
    wanted = jnp.zeros((pages_dev, 1), jnp.int32)
    for j in range(U_DEV):
        first_page = units_s[0, me * U_DEV + j] * per_unit - j * per_unit
        wanted = jnp.where(whole(slot_at, per_unit) == j, slot_at + first_page, wanted)
    found = jnp.zeros(wide, jnp.int32)
    for b in range(ids.shape[0]):
        found = found + jnp.where(
            wanted == ids[b : b + 1, :], numbers(wide, 1) + b * wide[1], 0
        )
    source_col = jnp.sum(found, axis=1, keepdims=True)
    source_row = down(k_sub == k_lane, source_col)
    holder_col, holder_row = whole(source_col, pages_dev), whole(source_row, pages_dev)
    rank_col = across(
        (holder_col == holder_row) & (source_row < source_col), jnp.ones(square, jnp.int32)
    )
    arrives_col = jnp.clip(holder_col * capacity + rank_col, 0, pages_dev - 1)
    lane_row = numbers((1, pages_dev), 1)
    slot_row = whole(lane_row, per_unit)
    own_lengths = jnp.zeros((1, pages_dev), jnp.int32)
    for j in range(U_DEV):
        own_lengths = jnp.where(
            slot_row == j, lengths[0, units_s[0, me * U_DEV + j] // KVH], own_lengths
        )
    turned = whole(own_lengths, PAGE) + lane_row - slot_row * per_unit
    turned = turned - whole(turned, per_unit) * per_unit
    place_row = slot_row * per_unit + turned
    place_ref[0:1, :] = place_row
    place_ref[1:2, :] = down(k_sub == place_row, arrives_col)
    place_ref[2:3, :] = own_lengths - turned * PAGE

    many_parts(half - 1).wait_recv()

    def half_sum(which):
        def add(offset, carry):
            block = part_in.at[lax.rem(here + offset, half), which]
            return tuple(c + block[j].astype(jnp.float32) for j, c in enumerate(carry))

        first = tuple(
            part_out[here, which, j].astype(jnp.float32) for j in range(U_DEV + 1)
        )
        return lax.fori_loop(1, half, add, first)

    halves = [half_sum(0), half_sum(1)]
    kept = [block for halved in halves for block in halved[:U_DEV]]
    kept_totals = [unpack_total(halved[U_DEV], j) for halved in halves for j in range(U_DEV)]
    for j in range(2 * U_DEV):
        swap_out[j] = kept[j].astype(jnp.bfloat16)
    swap_out[2 * U_DEV] = pack_totals(kept_totals)
    swap_copy().start()
    send_pages(share(PLAN[3]), share(PLAN[4]))
    swap_copy().wait_recv()
    packed = swap_in[2 * U_DEV].astype(jnp.float32)
    for j in range(2 * U_DEV):
        total = own_totals[j] + kept_totals[j] + unpack_total(packed, j, 2 * U_DEV)
        weighted = own_sums[j] + kept[j] + swap_in[j].astype(jnp.float32)
        att_all[here, j] = (weighted / total).astype(jnp.bfloat16)

    @pl.loop(1, half)
    def _(offset):
        att_copy(near(offset)).start()

    send_pages(share(PLAN[4]), turns)
    many_att(half - 1).wait_recv()

    for r in range(requests):
        for h in range(KVH):
            slot = table[of_slot, r * KVH + h]
            spread[h * span + r * 2 * group_count : h * span + (r + 1) * 2 * group_count, :] = (
                att_all[slot // (2 * U_DEV), slot % (2 * U_DEV)].astype(jnp.float32)
            )
    for h in range(KVH):
        for g in range(group_count):
            at = (h * group_count + g) * HD
            flat[:, at : at + HD] = spread[
                pl.ds(h * span + g, rows, stride=group_count), :
            ].astype(jnp.bfloat16)
    for c in range(tiles):
        loads[heads + c].wait()
        mixed_ref[:, c * HD : (c + 1) * HD] = lax.dot_general(
            flat[...], out_w[c], NT, preferred_element_type=jnp.float32
        ).astype(jnp.bfloat16)

    results = [
        pltpu.make_async_copy(src, dst, small_sem.at[i])
        for i, (src, dst) in enumerate(
            ((mixed_ref, mixed_hbm), (fresh_ref, fresh_hbm), (place_ref, place_hbm))
        )
    ]
    for result in results:
        result.start()
    for result in results:
        result.wait()
    remote(arrived_hbm, arrived_hbm, page_send, page_recv, partner).wait_recv()
    sent_pages = pages.at[pl.ds(0, (devices - 1) * capacity)]
    remote(sent_pages, sent_pages, page_send, page_recv, partner).wait_send()
    many_rows(devices - 1).wait_send()
    many_parts(half - 1).wait_send()
    swap_copy().wait_send()
    many_att(half - 1).wait_send()


def fused_body(hidden_states, qkv_weight, out_weight, cache_pages, context_lengths, new_units, old_pages):
    devices = lax.axis_size("tp")
    requests = hidden_states.shape[0]
    rows = requests * 2
    pages_dev = cache_pages.shape[0]
    capacity = pages_dev // devices
    heads = qkv_weight.shape[0] // HD
    tiles = out_weight.shape[0] // HD
    group_count = HEADS // KVH
    units = new_units.shape[0]
    hbm = pl.BlockSpec(memory_space=pl.ANY)
    vmem = pl.BlockSpec(memory_space=pltpu.VMEM)
    smem = pl.BlockSpec(memory_space=pltpu.SMEM)
    dma = pltpu.SemaphoreType.DMA
    lengths = context_lengths.reshape(1, requests)
    unit_table = new_units.reshape(1, units)
    page_table = old_pages.reshape(-1, PAGE)
    tile = (2 * group_count, HD)
    f32, bf16, i32 = jnp.float32, jnp.bfloat16, jnp.int32
    arrived, mixed, fresh, place = pl.pallas_call(
        lambda *refs: layer_kernel(devices, capacity, *refs),
        out_shape=(
            jax.ShapeDtypeStruct(cache_pages.shape, bf16),
            jax.ShapeDtypeStruct((rows, out_weight.shape[0]), bf16),
            jax.ShapeDtypeStruct((U_DEV, 2, 2 * HD), f32),
            jax.ShapeDtypeStruct((3, pages_dev), i32),
        ),
        in_specs=[pl.BlockSpec(memory_space=pltpu.HBM)] * 7,
        out_specs=(hbm, hbm, hbm, hbm),
        scratch_shapes=[
            pltpu.SMEM(lengths.shape, i32),
            pltpu.SMEM(unit_table.shape, i32),
            pltpu.VMEM(unit_table.shape, i32),
            pltpu.VMEM(page_table.shape, i32),
            pltpu.VMEM((1, pages_dev), i32),
            pltpu.SMEM((1, pages_dev), i32),
            pltpu.VMEM((8, pages_dev), i32),
            pltpu.SMEM((8, pages_dev), i32),
            pltpu.VMEM(hidden_states.shape, bf16),
            pltpu.VMEM((rows, D), f32),
            pltpu.VMEM((rows, D), bf16),
            pltpu.VMEM((rows, HD), f32),
            pltpu.VMEM((rows, HD), f32),
            pltpu.VMEM((heads, HD, D), bf16),
            pltpu.VMEM((tiles, HD, HEADS * HD), bf16),
            pltpu.VMEM((pages_dev, FIRST, 2 * HD), bf16),
            pltpu.VMEM((pages_dev, PAGE - FIRST, 2 * HD), bf16),
            pltpu.VMEM(cache_pages.shape, bf16),
            pltpu.VMEM((devices, heads, rows, HD), bf16),
            pltpu.VMEM((units * 2 * group_count, HD), f32),
            pltpu.VMEM((units,) + tile, bf16),
            pltpu.VMEM((KVH, rows, HD), bf16),
            pltpu.VMEM((KVH, rows, HD), bf16),
            pltpu.VMEM((devices // 2, 2, U_DEV + 1) + tile, bf16),
            pltpu.VMEM((devices // 2, 2, U_DEV + 1) + tile, bf16),
            pltpu.VMEM((2 * U_DEV + 1,) + tile, bf16),
            pltpu.VMEM((2 * U_DEV + 1,) + tile, bf16),
            pltpu.VMEM((devices // 2, 2 * U_DEV) + tile, bf16),
            pltpu.VMEM((rows, HEADS * HD), bf16),
            dma((max(heads, tiles),)),
            dma(()), dma(()),
            dma(()), dma((2,)),
            dma(()), dma(()), dma(()), dma(()),
            dma(()), dma(()),
            dma((7,)), dma((2,)), pltpu.SemaphoreType.REGULAR,
            pltpu.VMEM((rows, out_weight.shape[0]), bf16),
            pltpu.VMEM((U_DEV, 2, 2 * HD), f32),
            pltpu.VMEM((3, pages_dev), i32),
        ],
        compiler_params=pltpu.CompilerParams(
            collective_id=0, has_side_effects=True, vmem_limit_bytes=44 << 20
        ),
        name="layer",
    )(*[pltpu.with_memory_space_constraint(x, pltpu.HBM) for x in (lengths, unit_table, page_table, hidden_states, qkv_weight, out_weight, cache_pages)])
    mixed_shape = (requests, 2, out_weight.shape[0])
    placed, mixed = pl.pallas_call(
        place_kernel,
        out_shape=(
            jax.ShapeDtypeStruct(cache_pages.shape, bf16),
            jax.ShapeDtypeStruct(mixed_shape, bf16),
        ),
        in_specs=[vmem, vmem, vmem, vmem],
        out_specs=(hbm, hbm),
        scratch_shapes=[
            pltpu.VMEM((U_DEV, 2) + cache_pages.shape[1:], bf16),
            pltpu.VMEM(mixed_shape, bf16),
            dma(()), dma(()),
        ],
        compiler_params=pltpu.CompilerParams(vmem_limit_bytes=8 << 20),
        name="place_pages",
    )(place, arrived, fresh, mixed)
    return (mixed, placed)


def body(hidden_states, qkv_weight, out_weight, cache_pages, context_lengths, new_units, old_pages):
    devices = lax.axis_size("tp")
    whole_heads = qkv_weight.shape[0] % HD == 0 and out_weight.shape[0] % HD == 0
    pages_dev = cache_pages.shape[0]
    whole_shares = pages_dev % devices == 0 and devices % 4 == 0 and hidden_states.shape[0] == KVH
    whole_shares = whole_shares and new_units.shape[0] == pages_dev and PAGE % pages_dev == 0
    chosen = fused_body if whole_heads and whole_shares else plain_body
    return chosen(
        hidden_states, qkv_weight, out_weight, cache_pages, context_lengths, new_units, old_pages
    )


def solution(mesh):
    in_specs = (
        P("group", None, None),
        P("tp", None),
        P("tp", None),
        P(("group", "tp"), None, None),
        P("group"),
        P("group"),
        P("group"),
    )
    out_specs = (P("group", None, "tp"), P(("group", "tp"), None, None))
    return jax.shard_map(body, mesh=mesh, in_specs=in_specs, out_specs=out_specs, check_vma=False)
```

```python
import math

import jax
import jax.numpy as jnp
from jax import lax
from jax.experimental import pallas as pl
from jax.experimental.pallas import tpu as pltpu
from jax.sharding import PartitionSpec as P

D = 8192
HEADS = 64
KVH = 8
HD = 128
U_DEV = 4
MAXCTX = 2048
PAGE = 128


rope_base = 10000.0


def rotate_positions(values, positions):
    half_dim = values.shape[-1] // 2
    frequency = rope_base ** (-(jnp.arange(half_dim, dtype=jnp.float32) * 2.0 / values.shape[-1]))
    angles = positions.astype(jnp.float32)[..., None] * frequency
    cosine = jnp.concatenate([jnp.cos(angles), jnp.cos(angles)], axis=-1)
    sine_table = jnp.concatenate([jnp.sin(angles), jnp.sin(angles)], axis=-1)
    turned = jnp.concatenate([-values[..., half_dim:], values[..., :half_dim]], axis=-1)
    return values * cosine + turned * sine_table


def prepare(unit_qkv, base_lengths):
    group_count = HEADS // KVH
    count_units = unit_qkv.shape[0]
    positions = base_lengths[:, None] + jnp.arange(2, dtype=jnp.int32)[None, :]
    widened = unit_qkv.astype(jnp.float32)
    queries = widened[..., : group_count * HD].reshape(count_units, 2, group_count, HD)
    queries = rotate_positions(queries, positions[:, :, None]).astype(jnp.bfloat16)
    new_keys = rotate_positions(
        widened[..., group_count * HD : (group_count + 1) * HD], positions
    ).astype(jnp.bfloat16)
    new_values = unit_qkv[..., (group_count + 1) * HD :]
    return (queries, new_keys, new_values)


def context_terms(context, queries, valid_count):
    score_scale = 1.0 / math.sqrt(HD)
    cached_keys = context[..., :HD]
    cached_values = context[..., HD:]
    scores = (
        jnp.einsum("psgd,ptd->psgt", queries, cached_keys, preferred_element_type=jnp.float32)
        * score_scale
    )
    visible = jnp.arange(context.shape[1], dtype=jnp.int32)[None, :] < valid_count[:, None]
    weights = jnp.where(visible[:, None, None, :], jnp.exp(scores), 0.0)
    totals = jnp.sum(weights, axis=-1)
    weighted = jnp.einsum(
        "psgt,ptd->psgd",
        weights.astype(jnp.bfloat16),
        cached_values,
        preferred_element_type=jnp.float32,
    )
    return (weighted, totals)


def own_terms(queries, new_keys, new_values):
    score_scale = 1.0 / math.sqrt(HD)
    scores = (
        jnp.einsum("usgd,ujd->usgj", queries, new_keys, preferred_element_type=jnp.float32)
        * score_scale
    )
    recent = jnp.arange(2, dtype=jnp.int32)[None, :] <= jnp.arange(2, dtype=jnp.int32)[:, None]
    weights = jnp.where(recent[None, :, None, :], jnp.exp(scores), 0.0)
    totals = jnp.sum(weights, axis=-1)
    weighted = jnp.einsum(
        "usgj,ujd->usgd",
        weights.astype(jnp.bfloat16),
        new_values,
        preferred_element_type=jnp.float32,
    )
    return (weighted, totals)


def plain_body(hidden_states, qkv_weight, out_weight, cache_pages, context_lengths, new_units, old_pages):
    devices = lax.axis_size("tp")
    device = lax.axis_index("tp")
    requests = hidden_states.shape[0]
    rows_dev = qkv_weight.shape[0]
    pages_dev, page_rows, page_width = cache_pages.shape
    group_count = HEADS // KVH
    unit_rows = (group_count + 2) * HD
    per_unit = MAXCTX // PAGE
    unit_slots = U_DEV
    capacity = max(1, pages_dev // devices)
    total_units = new_units.shape[0]
    total_pages = old_pages.shape[0]
    flat_rows = hidden_states.reshape(requests * 2, D)
    partial_qkv = lax.dot_general(
        flat_rows, qkv_weight, (((1,), (1,)), ((), ())), preferred_element_type=jnp.float32
    )
    partial_qkv = partial_qkv.astype(jnp.bfloat16).reshape(requests, 2, rows_dev)
    slot_index = (
        jnp.zeros((total_units,), jnp.int32)
        .at[new_units]
        .set(jnp.arange(total_units, dtype=jnp.int32))
    )
    own_units = lax.dynamic_slice_in_dim(new_units, device * unit_slots, unit_slots)
    own_requests = own_units // KVH
    own_heads = own_units % KVH
    own_lengths = context_lengths[own_requests]
    local_ids = lax.dynamic_slice_in_dim(old_pages, device * pages_dev, pages_dev)
    local_units = local_ids // per_unit
    local_index = local_ids % per_unit
    target_dev = (slot_index[local_units] * per_unit + local_index) // pages_dev
    local_order = jnp.arange(pages_dev, dtype=jnp.int32)
    send_rank = jnp.sum(
        (
            (target_dev[:, None] == target_dev[None, :])
            & (local_order[None, :] < local_order[:, None])
        ).astype(jnp.int32),
        axis=1,
    )
    outgoing = (
        jnp.zeros((devices, capacity, page_rows, page_width), jnp.bfloat16)
        .at[target_dev, send_rank]
        .set(cache_pages)
    )
    arrived = lax.all_to_all(outgoing, "tp", split_axis=0, concat_axis=0, tiled=True)
    stored_position = (
        jnp.zeros((total_pages,), jnp.int32)
        .at[old_pages]
        .set(jnp.arange(total_pages, dtype=jnp.int32))
    )
    wanted = (
        own_units[:, None] * per_unit + jnp.arange(per_unit, dtype=jnp.int32)[None, :]
    ).reshape(pages_dev)
    source_pos = stored_position[wanted]
    source_dev = source_pos // pages_dev
    source_slot = source_pos % pages_dev
    arrival_rank = jnp.sum(
        (
            (source_dev[:, None] == source_dev[None, :])
            & (source_slot[None, :] < source_slot[:, None])
        ).astype(jnp.int32),
        axis=1,
    )
    relaid = arrived[source_dev, arrival_rank]
    contexts = relaid.reshape(unit_slots, MAXCTX, page_width)
    sources_per_head = unit_rows // rows_dev
    request_table = (new_units // KVH).reshape(devices, unit_slots)
    outgoing_rows = partial_qkv[request_table]
    incoming = lax.all_to_all(outgoing_rows, "tp", split_axis=0, concat_axis=0, tiled=True)
    grouped = jnp.moveaxis(incoming.reshape(KVH, sources_per_head, unit_slots, 2, rows_dev), 2, 0)
    chosen = jnp.take_along_axis(grouped, own_heads[:, None, None, None, None], axis=1)[:, 0]
    own_rows = chosen.transpose(0, 2, 1, 3).reshape(unit_slots, 2, unit_rows)
    queries, new_keys, new_values = prepare(own_rows, own_lengths)
    cache_sums, cache_totals = context_terms(contexts, queries, own_lengths)
    own_sums, own_totals = own_terms(queries, new_keys, new_values)
    attended = ((cache_sums + own_sums) / (cache_totals + own_totals)[..., None]).astype(
        jnp.bfloat16
    )
    attended = attended.reshape(unit_slots, 2, group_count * HD)
    all_heads = lax.all_gather(attended, "tp", axis=0, tiled=True)
    logical = (
        all_heads[slot_index]
        .reshape(requests, KVH, 2, group_count * HD)
        .transpose(0, 2, 1, 3)
        .reshape(requests * 2, HEADS * HD)
    )
    mixed_rows = lax.dot_general(
        logical, out_weight, (((1,), (1,)), ((), ())), preferred_element_type=jnp.float32
    )
    mixed_rows = mixed_rows.astype(jnp.bfloat16).reshape(requests, 2, out_weight.shape[0])
    fresh_rows = jnp.concatenate([new_keys, new_values], axis=-1)
    positions = jnp.arange(MAXCTX, dtype=jnp.int32)[None, :]
    contexts = jnp.where(
        (positions == own_lengths[:, None])[..., None], fresh_rows[:, 0:1], contexts
    )
    contexts = jnp.where(
        (positions == own_lengths[:, None] + 1)[..., None], fresh_rows[:, 1:2], contexts
    )
    return (mixed_rows, contexts.reshape(pages_dev, page_rows, page_width))


def place_kernel(
    table_ref, arrived_ref, fresh_ref, mixed_ref, out_ref, rows_ref, patched, rows, sem, rows_sem
):
    per_unit = MAXCTX // PAGE
    steps = fresh_ref.shape[1]

    def outward(at, src):
        return pltpu.make_async_copy(src, out_ref.at[at], sem)

    for slot in range(U_DEV):
        for page in range(steps, per_unit):
            k = slot * per_unit + page
            outward(table_ref[0, k], arrived_ref.at[table_ref[1, k]]).start()

    for slot in range(U_DEV):
        for page in range(steps):
            k = slot * per_unit + page
            at = table_ref[0, k]
            block = patched.at[slot, page]
            content = arrived_ref[table_ref[1, k]].astype(jnp.float32)
            line = lax.broadcasted_iota(jnp.int32, content.shape, 0)
            row = jnp.broadcast_to(table_ref[2:3, k : k + 1], content.shape)
            for step in range(steps):
                new = jnp.broadcast_to(fresh_ref[slot, step : step + 1, :], content.shape)
                content = jnp.where(line == row + step, new, content)
            block[...] = content.astype(jnp.bfloat16)
            outward(at, block).start()

    mixed = mixed_ref[...].astype(jnp.float32)
    for r in range(rows.shape[0]):
        rows[r] = mixed[2 * r : 2 * r + 2].astype(jnp.bfloat16)
    rows_out = pltpu.make_async_copy(rows, rows_ref, rows_sem)
    rows_out.start()
    pltpu.make_async_copy(arrived_ref, out_ref, sem).wait()
    rows_out.wait()


NT = (((1,), (1,)), ((), ()))
PLAN = (8,16,20,24,29)
FIRST = 16


def layer_kernel(
    devices, capacity,
    lengths_hbm, units_hbm, ids_hbm, hidden_hbm, qkv_hbm, out_hbm, pages_hbm,
    arrived_hbm, mixed_hbm, fresh_hbm, place_hbm,
    lengths, units_s, units_v, ids, order_v, order, tables_v, table, hidden_in, hidden_wide, hidden_ref, cos_ref, sin_ref,
    qkv_w, out_w, unsorted_head, unsorted_tail, pages, rows_all, spread, queries, new_keys, new_values, part_out, part_in, swap_out, swap_in, att_all, flat,
    load_sem, page_send, page_recv, row_send, row_recv, part_send, part_recv, swap_send, swap_recv, att_send, att_recv,
    small_sem, table_sem, settled, mixed_ref, fresh_ref, place_ref,
):
    me = lax.axis_index("tp")
    pages_dev = pages.shape[0]
    rows = hidden_ref.shape[0]
    requests = rows // 2
    units = requests * KVH
    per_unit = MAXCTX // PAGE
    heads = qkv_w.shape[0]
    tiles = out_w.shape[0]
    group_count = HEADS // KVH
    head_rows = group_count + 2
    score_scale = 1.0 / math.sqrt(HD)
    span = requests * 2 * group_count
    of_query, of_left, of_target, of_slot = range(4)

    half, quarter = devices // 2, devices // 4
    here, side = lax.rem(me, half), me // half
    partner = lax.rem(me + half, devices)

    def near(offset):
        return side * half + lax.rem(here + offset, half)

    def far(turn):
        return (1 - side) * half + (turn // quarter) * quarter + lax.rem(turn + me + 1, quarter)

    def remote(src, dst, send, recv, device):
        return pltpu.make_async_remote_copy(
            src_ref=src, dst_ref=dst, send_sem=send, recv_sem=recv,
            device_id={"tp": device}, device_id_type=pl.DeviceIdType.MESH,
        )

    def page_copy(rank, device, start=0, size=PAGE):
        return remote(
            pages.at[device * capacity + rank, pl.ds(start, size)],
            arrived_hbm.at[me * capacity + rank, pl.ds(start, size)],
            page_send, page_recv, device,
        )

    def row_copy(kind, owner, device):
        block = rows_all.at[owner]
        return remote(block, block, row_send, row_recv.at[kind], device)

    def many_rows(count):
        blocks = rows_all.at[pl.ds(0, count)]
        return remote(blocks, blocks, row_send, row_recv.at[1], partner)

    def att_copy(device):
        block = att_all.at[here]
        return remote(block, block, att_send, att_recv, device)

    def many_att(count):
        blocks = att_all.at[pl.ds(0, count)]
        return remote(blocks, blocks, att_send, att_recv, partner)

    def part_copy(src, dst, device):
        return remote(part_out.at[src], part_in.at[dst], part_send, part_recv, device)

    def many_parts(count):
        return remote(
            part_out.at[pl.ds(0, count)], part_in.at[pl.ds(0, count)], part_send, part_recv, partner
        )

    def swap_copy():
        return remote(swap_out, swap_in, swap_send, swap_recv, partner)

    turns = half * capacity

    def turn_of(turn):
        rank, place = turn // half, lax.rem(turn, half)
        if capacity == 1:
            return rank, place
        head = turn < 2 * half
        rank = jnp.where(head, lax.rem(turn // quarter, 2), rank)
        return rank, jnp.where(head, turn // half * quarter + lax.rem(turn, quarter), place)

    def send_far(start, stop, *part):
        @pl.loop(start, stop)
        def _(turn):
            rank, place = turn_of(turn)
            page_copy(rank, far(place), *part).start()

    def send_near(start, stop):
        @pl.loop(start, stop)
        def _(turn):
            rank, place = turn_of(turn)

            @pl.when(place > 0)
            def _():
                page_copy(rank, near(place)).start()

    def send_pages(start, stop):
        @pl.loop(start, stop)
        def _(turn):
            send_far(turn, turn + 1)
            send_near(turn, turn + 1)

    def share(numerator):
        return turns * numerator // 32

    def pack_totals(values):
        strip = PAGE // len(values)
        packed = jnp.zeros((2 * group_count, PAGE), jnp.float32)
        for j, total in enumerate(values):
            top = total.astype(jnp.bfloat16).astype(jnp.float32)
            packed = jnp.where(lane == j * strip, top, packed)
            packed = jnp.where(lane == j * strip + strip // 2, total - top, packed)
        return packed.astype(jnp.bfloat16)

    def unpack_total(packed, j, count=U_DEV):
        return jnp.sum(jnp.where(lane // (PAGE // count) == j, packed, 0.0), axis=-1, keepdims=True)

    lane = lax.broadcasted_iota(jnp.int32, (2 * group_count, PAGE), 1)

    small = [
        pltpu.make_async_copy(ids_hbm, ids, small_sem.at[0]),
        pltpu.make_async_copy(units_hbm, units_v, small_sem.at[1]),
        pltpu.make_async_copy(units_hbm, units_s, small_sem.at[2]),
        pltpu.make_async_copy(lengths_hbm, lengths, small_sem.at[3]),
    ]
    load_pages = [
        pltpu.make_async_copy(
            pages_hbm.at[:, pl.ds(start, part.shape[1])], part, small_sem.at[sem]
        )
        for start, part, sem in ((0, unsorted_head, 4), (FIRST, unsorted_tail, 6))
    ]
    load_hidden = pltpu.make_async_copy(hidden_hbm, hidden_in, small_sem.at[5])
    loads = [
        pltpu.make_async_copy(qkv_hbm.at[pl.ds(c * HD, HD)], qkv_w.at[c], load_sem.at[c])
        for c in range(heads)
    ]
    loads += [
        pltpu.make_async_copy(
            out_hbm.at[pl.ds(c * HD, HD)], out_w.at[c], load_sem.at[c]
        )
        for c in range(tiles)
    ]
    for load in small + load_pages:
        load.start()

    barrier = pltpu.get_barrier_semaphore()

    def greet(semaphore, device):
        pl.semaphore_signal(
            semaphore, inc=1, device_id={"tp": device}, device_id_type=pl.DeviceIdType.MESH
        )

    @pl.when(side == 0)
    def _():
        @pl.loop(half, devices)
        def _(device):
            greet(barrier, device)

    @pl.when(me // quarter == 2)
    def _():
        @pl.loop(0, half)
        def _(device):
            greet(barrier, half - 1 - device)

    def numbers(shape, axis):
        return lax.broadcasted_iota(jnp.int32, shape, axis)

    def whole(values, size):
        return lax.shift_right_logical(values, jnp.full_like(values, size.bit_length() - 1))

    def index_row(values, size):
        return jnp.clip(values, 0, size - 1)

    def down(hit, values):
        return jnp.sum(jnp.where(hit, values, 0), axis=0, keepdims=True)

    def across(hit, values):
        return jnp.sum(jnp.where(hit, values, 0), axis=1, keepdims=True)

    square = (pages_dev, pages_dev)
    k_sub, k_lane = numbers(square, 0), numbers(square, 1)
    small[0].wait()
    first = me * pages_dev
    wide = (pages_dev, ids.shape[1])
    own_ids = ids[pl.ds(first // ids.shape[1], 1), :]
    mine = numbers(wide, 1) == numbers(wide, 0) + lax.rem(first, ids.shape[1])
    id_col = across(mine, own_ids)
    small[1].wait()
    unit_row = units_v[...]
    by_unit = (pages_dev, units)
    slot_col = across(whole(id_col, per_unit) == unit_row, numbers(by_unit, 1))
    target_col = whole(slot_col, U_DEV)
    target_row = down(k_sub == k_lane, target_col)
    rank_col = across((target_col == target_row) & (k_lane < k_sub), jnp.ones(square, jnp.int32))
    sent = target_col * capacity + rank_col == k_lane
    order_v[...] = index_row(down(sent, k_sub), pages_dev)
    to_order = pltpu.make_async_copy(order_v, order, table_sem.at[1])
    to_order.start()
    def sort_page(at, head=True, tail=True, source=None):
        source = order[0, at] if source is None else source
        if head:
            pages[at, pl.ds(0, FIRST)] = unsorted_head[source]
        if tail:
            pages[at, pl.ds(FIRST, PAGE - FIRST)] = unsorted_tail[source]

    def sort_far(start, stop, *part):
        @pl.loop(start, stop)
        def _(turn):
            rank, place = turn_of(turn)
            sort_page(far(place) * capacity + rank, *part)

    def sort_near(start, stop):
        @pl.loop(start, stop)
        def _(turn):
            rank, place = turn_of(turn)
            sort_page(near(place) * capacity + rank)

    early = min(share(PLAN[0]), min(capacity, 2) * quarter)
    load_pages[0].wait()
    order_row = index_row(down(sent, k_sub), pages_dev)
    for turn in range(early):
        rank, place = turn_of(turn)
        at = far(place) * capacity + rank
        sort_page(at, True, False, jnp.sum(jnp.where(k_lane[0:1] == at, order_row, 0)))
    pl.semaphore_wait(barrier, jnp.where(side == 0, quarter, half))
    send_far(0, early, 0, FIRST)
    load_pages[1].wait()
    to_order.wait()
    sort_far(0, early, False, True)
    send_far(0, early, FIRST, PAGE - FIRST)
    id_row = down(sent, id_col)
    tables_v[of_target : of_target + 1, :] = down(sent, slot_col - target_col * U_DEV)
    sent_unit = whole(id_row, per_unit)
    sent_request = whole(sent_unit, KVH)
    small[3].wait()
    sent_length = jnp.zeros_like(id_row)
    for r in range(requests):
        sent_length = jnp.where(sent_request == r, lengths[0, r], sent_length)
    tables_v[of_query : of_query + 1, :] = index_row(
        (sent_unit - sent_request * KVH) * requests + sent_request, units
    )
    tables_v[of_left : of_left + 1, :] = sent_length - (id_row - sent_unit * per_unit) * PAGE
    u_square = (units, units)
    u_sub, u_lane = numbers(u_square, 0), numbers(u_square, 1)
    unit_col = across(u_sub == u_lane, unit_row)
    u_device = whole(u_sub, U_DEV)
    u_side = whole(u_device, half)
    u_place = (u_device - u_side * half) * (2 * U_DEV) + u_side * U_DEV + (u_sub - u_device * U_DEV)
    tables_v[of_slot : of_slot + 1, :] = index_row(down(unit_col == u_lane, u_place), units)
    to_table = pltpu.make_async_copy(tables_v, table, table_sem.at[0])
    to_table.start()

    for load in [load_hidden] + loads[:heads]:
        load.start()

    @pl.when(side == 1)
    def _():
        @pl.loop(0, half)
        def _(device):
            greet(settled, device)

    sort_near(0, early)
    sort_far(early, turns)
    sort_near(early, turns)
    to_table.wait()

    small[2].wait()
    row_at = lax.broadcasted_iota(jnp.int32, (rows, HD), 0)
    lane_at = lax.broadcasted_iota(jnp.int32, (rows, HD), 1)
    positions = jnp.zeros((rows, HD), jnp.float32)
    for r in range(requests):
        positions = jnp.where(row_at // 2 == r, lengths[0, r].astype(jnp.float32), positions)
    positions = positions + (row_at % 2).astype(jnp.float32)
    power = (lane_at % (HD // 2)).astype(jnp.float32) * (2.0 / HD)
    angles = positions * jnp.exp(power * -math.log(rope_base))
    cos_ref[...] = jnp.cos(angles)
    sin_ref[...] = jnp.where(lane_at < HD // 2, -jnp.sin(angles), jnp.sin(angles))
    load_hidden.wait()
    for r in range(requests):
        hidden_wide[2 * r : 2 * r + 2, :] = hidden_in[r].astype(jnp.float32)
    hidden_ref[...] = hidden_wide[...].astype(jnp.bfloat16)

    @pl.when(side == 0)
    def _():
        pl.semaphore_wait(settled, half)
        greet(settled, partner)

    for c in range(heads):
        loads[c].wait()
        part = lax.dot_general(
            hidden_ref[...], qkv_w[c], NT, preferred_element_type=jnp.float32
        ).astype(jnp.bfloat16).astype(jnp.float32)
        turned = part * cos_ref[...] + pltpu.roll(part, HD // 2, 1) * sin_ref[...]
        is_value = lax.rem(me * heads + c, head_rows) == head_rows - 1
        rows_all[me, c] = jnp.where(is_value, part, turned).astype(jnp.bfloat16)

    row_copy(0, me, partner).start()

    @pl.when(side == 1)
    def _():
        pl.semaphore_wait(settled, 1)

    @pl.loop(1, half)
    def _(offset):
        row_copy(1, me, near(offset)).start()

    late = share(PLAN[1]) - early

    @pl.loop(0, late)
    def _(turn):
        send_far(early + turn, early + turn + 1)
        send_near(turn * early // late, (turn + 1) * early // late)

    send_near(early, share(PLAN[1]))
    for load in loads[heads:]:
        load.start()
    own_pages = pltpu.make_async_copy(
        pages.at[pl.ds(me * capacity, capacity)],
        arrived_hbm.at[pl.ds(me * capacity, capacity)],
        page_recv,
    )
    own_pages.start()

    row_copy(0, partner, partner).wait_recv()

    @pl.loop(1, half)
    def _(offset):
        row_copy(1, partner, near(offset)).start()

    send_pages(share(PLAN[1]), share(PLAN[2]))

    many_rows(devices - 2).wait_recv()

    for h in range(KVH):
        for g in range(group_count):
            at = h * head_rows + g
            spread[pl.ds(h * span + g, rows, stride=group_count), :] = rows_all[
                at // heads, at % heads
            ].astype(jnp.float32)
        at = h * head_rows + group_count
        new_keys[h] = rows_all[at // heads, at % heads]
        new_values[h] = rows_all[(at + 1) // heads, (at + 1) % heads]
        for r in range(requests):
            start = h * span + r * 2 * group_count
            queries[h * requests + r] = spread[start : start + 2 * group_count, :].astype(
                jnp.bfloat16
            )

    @pl.loop(0, devices)
    def _(target):
        spent = share(PLAN[3]) - share(PLAN[2])
        send_pages(
            share(PLAN[2]) + target * spent // devices,
            share(PLAN[2]) + (target + 1) * spent // devices,
        )
        zero = jnp.zeros((2 * group_count, PAGE), jnp.float32)
        sums, totals = [zero] * U_DEV, [zero[:, :1]] * U_DEV
        places = [target * capacity + rank for rank in range(capacity)]
        scores = [
            lax.dot_general(
                queries[table[of_query, at]], pages[at, :, :HD], NT, preferred_element_type=jnp.float32
            ) * score_scale
            for at in places
        ]
        weights = [
            jnp.where(lane < table[of_left, at], jnp.exp(score), 0.0)
            for at, score in zip(places, scores)
        ]
        weighted = [
            jnp.dot(weight.astype(jnp.bfloat16), pages[at, :, HD:], preferred_element_type=jnp.float32)
            for at, weight in zip(places, weights)
        ]
        for at, weight, added in zip(places, weights, weighted):
            slot, total = table[of_target, at], jnp.sum(weight, axis=-1, keepdims=True)
            for j in range(U_DEV):
                sums[j] = sums[j] + jnp.where(slot == j, added, 0.0)
                totals[j] = totals[j] + jnp.where(slot == j, total, 0.0)
        place, which = lax.rem(target, half), target // half
        for j in range(U_DEV):
            part_out[place, which, j] = sums[j].astype(jnp.bfloat16)
        part_out[place, which, U_DEV] = pack_totals(totals)

    @pl.loop(1, half)
    def _(offset):
        part_copy(lax.rem(here + offset, half), here, near(offset)).start()

    own_sums, own_totals = [], []
    row = lax.broadcasted_iota(jnp.int32, (2 * group_count, rows), 0)
    col = lax.broadcasted_iota(jnp.int32, (2 * group_count, rows), 1)
    line = lax.broadcasted_iota(jnp.int32, (rows, HD), 0)
    for j in range(2 * U_DEV):
        unit = units_s[0, (j // U_DEV * half + here) * U_DEV + j % U_DEV]
        request, head = unit // KVH, unit % KVH
        scores = lax.dot_general(
            queries[head * requests + request], new_keys[head], NT, preferred_element_type=jnp.float32
        ) * score_scale
        seen = (col // 2 == request) & (col % 2 <= row // group_count)
        weights = jnp.where(seen, jnp.exp(scores), 0.0)
        own_totals.append(jnp.sum(weights, axis=-1, keepdims=True))
        own_sums.append(
            jnp.dot(weights.astype(jnp.bfloat16), new_values[head], preferred_element_type=jnp.float32)
        )
    for j in range(U_DEV):
        unit = units_s[0, me * U_DEV + j]
        request, head = unit // KVH, unit % KVH
        for step in range(2):
            mine = line == request * 2 + step
            for part, kind in ((0, new_keys[head]), (1, new_values[head])):
                fresh_ref[j, step : step + 1, part * HD : (part + 1) * HD] = jnp.sum(
                    jnp.where(mine, kind.astype(jnp.float32), 0.0), axis=0, keepdims=True
                )

    slot_at = numbers((pages_dev, 1), 0)
    wanted = jnp.zeros((pages_dev, 1), jnp.int32)
    for j in range(U_DEV):
        first_page = units_s[0, me * U_DEV + j] * per_unit - j * per_unit
        wanted = jnp.where(whole(slot_at, per_unit) == j, slot_at + first_page, wanted)
    found = jnp.zeros(wide, jnp.int32)
    for b in range(ids.shape[0]):
        found = found + jnp.where(
            wanted == ids[b : b + 1, :], numbers(wide, 1) + b * wide[1], 0
        )
    source_col = jnp.sum(found, axis=1, keepdims=True)
    source_row = down(k_sub == k_lane, source_col)
    holder_col, holder_row = whole(source_col, pages_dev), whole(source_row, pages_dev)
    rank_col = across(
        (holder_col == holder_row) & (source_row < source_col), jnp.ones(square, jnp.int32)
    )
    arrives_col = jnp.clip(holder_col * capacity + rank_col, 0, pages_dev - 1)
    lane_row = numbers((1, pages_dev), 1)
    slot_row = whole(lane_row, per_unit)
    own_lengths = jnp.zeros((1, pages_dev), jnp.int32)
    for j in range(U_DEV):
        own_lengths = jnp.where(
            slot_row == j, lengths[0, units_s[0, me * U_DEV + j] // KVH], own_lengths
        )
    turned = whole(own_lengths, PAGE) + lane_row - slot_row * per_unit
    turned = turned - whole(turned, per_unit) * per_unit
    place_row = slot_row * per_unit + turned
    place_ref[0:1, :] = place_row
    place_ref[1:2, :] = down(k_sub == place_row, arrives_col)
    place_ref[2:3, :] = own_lengths - turned * PAGE

    many_parts(half - 1).wait_recv()

    def half_sum(which):
        def add(offset, carry):
            block = part_in.at[lax.rem(here + offset, half), which]
            return tuple(c + block[j].astype(jnp.float32) for j, c in enumerate(carry))

        first = tuple(
            part_out[here, which, j].astype(jnp.float32) for j in range(U_DEV + 1)
        )
        return lax.fori_loop(1, half, add, first)

    halves = [half_sum(0), half_sum(1)]
    kept = [block for halved in halves for block in halved[:U_DEV]]
    kept_totals = [unpack_total(halved[U_DEV], j) for halved in halves for j in range(U_DEV)]
    for j in range(2 * U_DEV):
        swap_out[j] = kept[j].astype(jnp.bfloat16)
    swap_out[2 * U_DEV] = pack_totals(kept_totals)
    swap_copy().start()
    send_pages(share(PLAN[3]), share(PLAN[4]))
    swap_copy().wait_recv()
    packed = swap_in[2 * U_DEV].astype(jnp.float32)
    for j in range(2 * U_DEV):
        total = own_totals[j] + kept_totals[j] + unpack_total(packed, j, 2 * U_DEV)
        weighted = own_sums[j] + kept[j] + swap_in[j].astype(jnp.float32)
        att_all[here, j] = (weighted / total).astype(jnp.bfloat16)

    @pl.loop(1, half)
    def _(offset):
        att_copy(near(offset)).start()

    send_pages(share(PLAN[4]), turns)
    many_att(half - 1).wait_recv()

    for r in range(requests):
        for h in range(KVH):
            slot = table[of_slot, r * KVH + h]
            spread[h * span + r * 2 * group_count : h * span + (r + 1) * 2 * group_count, :] = (
                att_all[slot // (2 * U_DEV), slot % (2 * U_DEV)].astype(jnp.float32)
            )
    for h in range(KVH):
        for g in range(group_count):
            at = (h * group_count + g) * HD
            flat[:, at : at + HD] = spread[
                pl.ds(h * span + g, rows, stride=group_count), :
            ].astype(jnp.bfloat16)
    for c in range(tiles):
        loads[heads + c].wait()
        mixed_ref[:, c * HD : (c + 1) * HD] = lax.dot_general(
            flat[...], out_w[c], NT, preferred_element_type=jnp.float32
        ).astype(jnp.bfloat16)

    results = [
        pltpu.make_async_copy(src, dst, small_sem.at[i])
        for i, (src, dst) in enumerate(
            ((mixed_ref, mixed_hbm), (fresh_ref, fresh_hbm), (place_ref, place_hbm))
        )
    ]
    for result in results:
        result.start()
    for result in results:
        result.wait()
    remote(arrived_hbm, arrived_hbm, page_send, page_recv, partner).wait_recv()
    sent_pages = pages.at[pl.ds(0, (devices - 1) * capacity)]
    remote(sent_pages, sent_pages, page_send, page_recv, partner).wait_send()
    many_rows(devices - 1).wait_send()
    many_parts(half - 1).wait_send()
    swap_copy().wait_send()
    many_att(half - 1).wait_send()


def fused_body(hidden_states, qkv_weight, out_weight, cache_pages, context_lengths, new_units, old_pages):
    devices = lax.axis_size("tp")
    requests = hidden_states.shape[0]
    rows = requests * 2
    pages_dev = cache_pages.shape[0]
    capacity = pages_dev // devices
    heads = qkv_weight.shape[0] // HD
    tiles = out_weight.shape[0] // HD
    group_count = HEADS // KVH
    units = new_units.shape[0]
    hbm = pl.BlockSpec(memory_space=pl.ANY)
    vmem = pl.BlockSpec(memory_space=pltpu.VMEM)
    smem = pl.BlockSpec(memory_space=pltpu.SMEM)
    dma = pltpu.SemaphoreType.DMA
    lengths = context_lengths.reshape(1, requests)
    unit_table = new_units.reshape(1, units)
    page_table = old_pages.reshape(-1, PAGE)
    tile = (2 * group_count, HD)
    f32, bf16, i32 = jnp.float32, jnp.bfloat16, jnp.int32
    arrived, mixed, fresh, place = pl.pallas_call(
        lambda *refs: layer_kernel(devices, capacity, *refs),
        out_shape=(
            jax.ShapeDtypeStruct(cache_pages.shape, bf16),
            jax.ShapeDtypeStruct((rows, out_weight.shape[0]), bf16),
            jax.ShapeDtypeStruct((U_DEV, 2, 2 * HD), f32),
            jax.ShapeDtypeStruct((3, pages_dev), i32),
        ),
        in_specs=[pl.BlockSpec(memory_space=pltpu.HBM)] * 7,
        out_specs=(hbm, hbm, hbm, hbm),
        scratch_shapes=[
            pltpu.SMEM(lengths.shape, i32),
            pltpu.SMEM(unit_table.shape, i32),
            pltpu.VMEM(unit_table.shape, i32),
            pltpu.VMEM(page_table.shape, i32),
            pltpu.VMEM((1, pages_dev), i32),
            pltpu.SMEM((1, pages_dev), i32),
            pltpu.VMEM((8, pages_dev), i32),
            pltpu.SMEM((8, pages_dev), i32),
            pltpu.VMEM(hidden_states.shape, bf16),
            pltpu.VMEM((rows, D), f32),
            pltpu.VMEM((rows, D), bf16),
            pltpu.VMEM((rows, HD), f32),
            pltpu.VMEM((rows, HD), f32),
            pltpu.VMEM((heads, HD, D), bf16),
            pltpu.VMEM((tiles, HD, HEADS * HD), bf16),
            pltpu.VMEM((pages_dev, FIRST, 2 * HD), bf16),
            pltpu.VMEM((pages_dev, PAGE - FIRST, 2 * HD), bf16),
            pltpu.VMEM(cache_pages.shape, bf16),
            pltpu.VMEM((devices, heads, rows, HD), bf16),
            pltpu.VMEM((units * 2 * group_count, HD), f32),
            pltpu.VMEM((units,) + tile, bf16),
            pltpu.VMEM((KVH, rows, HD), bf16),
            pltpu.VMEM((KVH, rows, HD), bf16),
            pltpu.VMEM((devices // 2, 2, U_DEV + 1) + tile, bf16),
            pltpu.VMEM((devices // 2, 2, U_DEV + 1) + tile, bf16),
            pltpu.VMEM((2 * U_DEV + 1,) + tile, bf16),
            pltpu.VMEM((2 * U_DEV + 1,) + tile, bf16),
            pltpu.VMEM((devices // 2, 2 * U_DEV) + tile, bf16),
            pltpu.VMEM((rows, HEADS * HD), bf16),
            dma((max(heads, tiles),)),
            dma(()), dma(()),
            dma(()), dma((2,)),
            dma(()), dma(()), dma(()), dma(()),
            dma(()), dma(()),
            dma((7,)), dma((2,)), pltpu.SemaphoreType.REGULAR,
            pltpu.VMEM((rows, out_weight.shape[0]), bf16),
            pltpu.VMEM((U_DEV, 2, 2 * HD), f32),
            pltpu.VMEM((3, pages_dev), i32),
        ],
        compiler_params=pltpu.CompilerParams(
            collective_id=0, has_side_effects=True, vmem_limit_bytes=44 << 20
        ),
        name="layer",
    )(*[pltpu.with_memory_space_constraint(x, pltpu.HBM) for x in (lengths, unit_table, page_table, hidden_states, qkv_weight, out_weight, cache_pages)])
    mixed_shape = (requests, 2, out_weight.shape[0])
    placed, mixed = pl.pallas_call(
        place_kernel,
        out_shape=(
            jax.ShapeDtypeStruct(cache_pages.shape, bf16),
            jax.ShapeDtypeStruct(mixed_shape, bf16),
        ),
        in_specs=[vmem, vmem, vmem, vmem],
        out_specs=(hbm, hbm),
        scratch_shapes=[
            pltpu.VMEM((U_DEV, 2) + cache_pages.shape[1:], bf16),
            pltpu.VMEM(mixed_shape, bf16),
            dma(()), dma(()),
        ],
        compiler_params=pltpu.CompilerParams(vmem_limit_bytes=8 << 20),
        name="place_pages",
    )(place, arrived, fresh, mixed)
    return (mixed, placed)


def body(hidden_states, qkv_weight, out_weight, cache_pages, context_lengths, new_units, old_pages):
    devices = lax.axis_size("tp")
    whole_heads = qkv_weight.shape[0] % HD == 0 and out_weight.shape[0] % HD == 0
    pages_dev = cache_pages.shape[0]
    whole_shares = pages_dev % devices == 0 and devices % 4 == 0 and hidden_states.shape[0] == KVH
    whole_shares = whole_shares and new_units.shape[0] == pages_dev and PAGE % pages_dev == 0
    chosen = fused_body if whole_heads and whole_shares else plain_body
    return chosen(
        hidden_states, qkv_weight, out_weight, cache_pages, context_lengths, new_units, old_pages
    )


def solution(mesh):
    in_specs = (
        P("group", None, None),
        P("tp", None),
        P("tp", None),
        P(("group", "tp"), None, None),
        P("group"),
        P("group"),
        P("group"),
    )
    out_specs = (P("group", None, "tp"), P(("group", "tp"), None, None))
    return jax.shard_map(body, mesh=mesh, in_specs=in_specs, out_specs=out_specs, check_vma=False)
```
